32 devices in a mesh: gx: 8 (over z, x), gy: 4 (over y, core).
Axes of the slice: x: 2, y: 2, z: 4, core: 2. Of those that a mesh axis runs over, the one named last changes fastest.
Arguments:
- coarse_pop: float32 [9, 8192, 512], P(None, 'gx', 'gy'), may hold values from 0.001 to 1, as said below
- fine_pop: float32 [512, 9, 4096], P(('gx', 'gy')), may hold values from 0.001 to 1, as said below
- fine_block: int32 [512], P(('gx', 'gy')), may hold values from 0 to 4095, as said below
Outputs:
- coarse_out: float32 [9, 8192, 512], P(None, 'gx', 'gy')
- fine_out: float32 [512, 9, 4096], P(('gx', 'gy'))
The draws below stay inside these ranges and needn't reach their ends.
Inputs may be any that keep to these rules, and one draw needn't show every extreme that they name: `coarse_pop`: populations of a state near equilibrium, positive. `fine_pop`: populations of a state near equilibrium, positive. `fine_block`: the slots of the device at (gx, gy) name distinct blocks whose rows lie in the gy-th band of 4 rows; no block is named twice; of one device's slots, at most 2 name blocks whose columns lie in the band of 32 columns of any one gx index, and this bound is reached for every device.
All inputs are finite; a program needn't handle non-finite values.
Results may differ from the reference program's by a relative error of at most 0.0003.
Values sent between devices are 32-bit elements; how exact they have to be, the bound alone decides.
No kernel may reach another device: no remote copies, remote signals or barrier semaphores. Data moves between devices by JAX's collectives and lax.ppermute only.
A program may use at most 192 MiB of HBM per device.

```python
import jax
import jax.numpy as jnp
from jax import lax

FINE_EDGE = 64
COARSE_EDGE = 32
BX = 32
BY = 4
SLOTS = 16
CAP = 2
NBX = 256
NBY = 16
NXC = 8192
NYC = 512
FINE_TOTAL = 512
N_GX = 8
N_GY = 4


along_x = [0, 1, 0, -1, 0, 1, -1, -1, 1]


along_y = [0, 0, 1, 0, -1, 1, 1, -1, -1]


lattice_weights = [4.0 / 9, 1.0 / 9, 1.0 / 9, 1.0 / 9, 1.0 / 9, 1.0 / 36, 1.0 / 36, 1.0 / 36, 1.0 / 36]


def near_balance(key, cells, axis_pos):
    key_one, key_two, key_three, key_four = jax.random.split(key, 4)
    density = 1.0 + jnp.clip(0.08 * jax.random.normal(key_one, cells, jnp.float32), -0.2, 0.2)
    speed_x = jnp.clip(0.06 * jax.random.normal(key_two, cells, jnp.float32), -0.15, 0.15)
    speed_y = jnp.clip(0.06 * jax.random.normal(key_three, cells, jnp.float32), -0.15, 0.15)
    noise = jnp.clip(0.1 * jax.random.normal(key_four, (9,) + cells, jnp.float32), -0.25, 0.25)
    squared = speed_x * speed_x + speed_y * speed_y
    result = []
    for direction in range(9):
        projected = float(along_x[direction]) * speed_x + float(along_y[direction]) * speed_y
        balance = float(lattice_weights[direction]) * density * (1.0 + 3.0 * projected + 4.5 * projected * projected - 1.5 * squared)
        result.append(balance * (1.0 + noise[direction]))
    return jnp.stack(result, axis=axis_pos)


def draw_coarse_pop(key, part):
    return near_balance(jax.random.fold_in(key, 11), (NXC, NYC), 0)


def draw_fine_pop(key, part):
    return near_balance(jax.random.fold_in(key, 13), (FINE_TOTAL, FINE_EDGE * FINE_EDGE), 1)


def draw_fine_block(key, part):
    key_one, key_two, key_three = jax.random.split(jax.random.fold_in(key, 17), 3)
    local_count = BX * BY
    offsets = jax.random.randint(key_one, (N_GY,), 0, N_GX)
    local_perm = jax.vmap(lambda subkey: jax.random.permutation(subkey, local_count))(jax.random.split(key_two, N_GX * N_GY)).reshape(N_GX, N_GY, local_count)
    slot_perm = jax.vmap(lambda subkey: jax.random.permutation(subkey, SLOTS))(jax.random.split(key_three, N_GX * N_GY)).reshape(N_GX, N_GY, SLOTS)
    holder = jnp.arange(N_GX, dtype=jnp.int32)[:, None, None]
    band = jnp.broadcast_to(jnp.arange(N_GY, dtype=jnp.int32)[None, :, None], (N_GX, N_GY, SLOTS))
    request = slot_perm.astype(jnp.int32)
    group = request // CAP
    source = (holder + group + offsets[band]) % N_GX
    chosen = local_perm[source, band, request].astype(jnp.int32)
    column = source * BX + chosen // BY
    row_id = band * BY + chosen % BY
    return (column * (BY * N_GY) + row_id).reshape(-1).astype(jnp.int32)


def setup_inputs(seed: int = 0) -> dict:
    key_of = jax.random.split(jax.random.key(seed), 4)
    coarse_pop = draw_coarse_pop(jax.random.fold_in(key_of[3], 71), 0)
    fine_pop = draw_fine_pop(jax.random.fold_in(key_of[3], 71), 0)
    fine_block = draw_fine_block(jax.random.fold_in(key_of[3], 71), 0)
    return dict(coarse_pop=coarse_pop, fine_pop=fine_pop, fine_block=fine_block)


along_x = [0, 1, 0, -1, 0, 1, -1, -1, 1]
along_y = [0, 0, 1, 0, -1, 1, 1, -1, -1]
opposite = [0, 3, 4, 1, 2, 7, 8, 5, 6]
lattice_weights = [4.0 / 9, 1.0 / 9, 1.0 / 9, 1.0 / 9, 1.0 / 9, 1.0 / 36, 1.0 / 36, 1.0 / 36, 1.0 / 36]
moment_list = [
    [1.0, 1, 1, 1, 1, 1, 1, 1, 1],
    [-4, -1, -1, -1, -1, 2, 2, 2, 2],
    [4, -2, -2, -2, -2, 1, 1, 1, 1],
    [0, 1, 0, -1, 0, 1, -1, -1, 1],
    [0, -2, 0, 2, 0, 1, -1, -1, 1],
    [0, 0, 1, 0, -1, 1, 1, -1, -1],
    [0, 0, -2, 0, 2, 1, 1, -1, -1],
    [0, 1, -1, 1, -1, 0, 0, 0, 0],
    [0, 0, 0, 0, 0, 1, -1, 1, -1]]
fine_relax = 0.8
coarse_relax = 0.65
explode_factor = 0.8 / 1.3
coalesce_factor = 1.3 / 0.8


def mrt_table(relax_time):
    rates = [0.0, 1.4, 1.4, 0.0, 1.2, 0.0, 1.2, 1.0 / relax_time, 1.0 / relax_time]
    norms = [sum(float(value) * float(value) for value in moment_list[k]) for k in range(9)]
    table = []
    for first in range(9):
        line = []
        for second in range(9):
            total = 0.0
            for k in range(9):
                total = total + float(moment_list[k][first]) / norms[k] * rates[k] * float(moment_list[k][second])
            line.append(total)
        table.append(line)
    return table


def macroscopic(popul):
    step_x = jnp.asarray(along_x, jnp.float32)[:, None]
    step_y = jnp.asarray(along_y, jnp.float32)[:, None]
    density = jnp.sum(popul, axis=-2)
    speed_x = jnp.sum(popul * step_x, axis=-2) / density
    speed_y = jnp.sum(popul * step_y, axis=-2) / density
    return density, speed_x, speed_y


def equilibrium(density, speed_x, speed_y):
    step_x = jnp.asarray(along_x, jnp.float32)[:, None]
    step_y = jnp.asarray(along_y, jnp.float32)[:, None]
    weights = jnp.asarray(lattice_weights, jnp.float32)[:, None]
    projected = step_x * speed_x[..., None, :] + step_y * speed_y[..., None, :]
    squared = (speed_x * speed_x + speed_y * speed_y)[..., None, :]
    return weights * density[..., None, :] * (1.0 + 3.0 * projected + 4.5 * projected * projected - 1.5 * squared)


def collide(popul, relax_time):
    balance = equilibrium(*macroscopic(popul))
    matrix = jnp.asarray(mrt_table(relax_time), jnp.float32)
    return popul - jnp.einsum("ij,...jn->...in", matrix, popul - balance, precision=lax.Precision.HIGHEST)


def rescale(popul, factor):
    balance = equilibrium(*macroscopic(popul))
    return balance + factor * (popul - balance)


def stream_coarse(collided, base_y, total_y):
    width_x = collided.shape[1] - 2
    width_y = collided.shape[2] - 2
    coord_y = jnp.arange(width_y, dtype=jnp.int32) + base_y - 1
    result = []
    for direction in range(9):
        shift_x = int(along_x[direction])
        shift_y = int(along_y[direction])
        source = collided[direction, 1 - shift_x:1 - shift_x + width_x, 1 - shift_y:1 - shift_y + width_y]
        bounced = collided[opposite[direction], 1:1 + width_x, 1:1 + width_y]
        beyond = ((coord_y - shift_y) < 0) | ((coord_y - shift_y) >= total_y)
        result.append(jnp.where(beyond[None, :], bounced, source))
    return jnp.stack(result)


def cycle_of(square):
    return jnp.stack([square[..., 0, :], square[..., -1, :], square[..., :, 0], square[..., :, -1]], axis=-2)


def widen(border):
    return jnp.concatenate([border[..., :1], jnp.repeat(border[..., 1:-1], 2, axis=-1), border[..., -1:]], axis=-1)


def fine_substep(interior, cycle_pre, low_wall, high_wall):
    slot_count = interior.shape[0]
    edge_len = interior.shape[-1]
    cycle_len = cycle_pre.shape[-1]
    ghost_pre = rescale(cycle_pre.reshape(slot_count, 9, 4 * cycle_len), explode_factor)
    ghosts = collide(ghost_pre, fine_relax).reshape(slot_count, 9, 4, cycle_len)
    inner = collide(interior.reshape(slot_count, 9, edge_len * edge_len), fine_relax).reshape(slot_count, 9, edge_len, edge_len)
    upper_row = widen(ghosts[:, :, 0])
    lower_row = widen(ghosts[:, :, 1])
    left_col = widen(ghosts[:, :, 2])
    right_col = widen(ghosts[:, :, 3])
    middle = jnp.concatenate([left_col[:, :, 1:-1, None], inner, right_col[:, :, 1:-1, None]], axis=3)
    padded = jnp.concatenate([upper_row[:, :, None, :], middle, lower_row[:, :, None, :]], axis=2)
    coord_y = jnp.arange(edge_len, dtype=jnp.int32)
    result = []
    for direction in range(9):
        shift_x = int(along_x[direction])
        shift_y = int(along_y[direction])
        source = padded[:, direction, 1 - shift_x:1 - shift_x + edge_len, 1 - shift_y:1 - shift_y + edge_len]
        bounced = inner[:, opposite[direction]]
        beyond = (low_wall[:, None] & ((coord_y - shift_y) < 0)[None, :]) | (high_wall[:, None] & ((coord_y - shift_y) >= edge_len)[None, :])
        result.append(jnp.where(beyond[:, None, :], bounced, source))
    return jnp.stack(result, axis=1)


def coalesce(interior):
    slot_count = interior.shape[0]
    half = interior.shape[-1] // 2
    grouped = interior.reshape(slot_count, 9, half, 2, half, 2)
    average = jnp.sum(grouped, axis=(3, 5)) * 0.25
    return rescale(average.reshape(slot_count, 9, half * half), coalesce_factor)


def fine_advance(interior, cycles, low_wall, high_wall):
    old_cycle = cycles[:, 0]
    new_cycle = cycles[:, 1]
    first = fine_substep(interior, old_cycle, low_wall, high_wall)
    second = fine_substep(first, 0.5 * (old_cycle + new_cycle), low_wall, high_wall)
    return second, coalesce(second)


def cut_square(field, start_x, start_y):
    cycle_len = COARSE_EDGE + 2
    zero = jnp.zeros((), jnp.int32)
    return lax.dynamic_slice(field, (zero, start_x.astype(jnp.int32), start_y.astype(jnp.int32)), (9, cycle_len, cycle_len))


def reference(coarse_pop, fine_pop, fine_block):
    padded_two = jnp.pad(coarse_pop, ((0, 0), (2, 2), (2, 2)), mode="wrap")
    collided = collide(padded_two.reshape(9, -1), coarse_relax).reshape(padded_two.shape)
    new_one = stream_coarse(collided, 0, NYC)
    old_one = padded_two[:, 1:-1, 1:-1]
    coarse_next = new_one[:, 1:-1, 1:-1]

    def one_group(inputs):
        states, idents = inputs
        column = idents // NBY
        row_id = idents % NBY
        old_cut = jax.vmap(lambda start_x, start_y: cut_square(old_one, start_x, start_y))(column * COARSE_EDGE, row_id * COARSE_EDGE)
        new_cut = jax.vmap(lambda start_x, start_y: cut_square(new_one, start_x, start_y))(column * COARSE_EDGE, row_id * COARSE_EDGE)
        cycles = cycle_of(jnp.stack([old_cut, new_cut], axis=1))
        interior = states.reshape(states.shape[0], 9, FINE_EDGE, FINE_EDGE)
        return fine_advance(interior, cycles, row_id == 0, row_id == NBY - 1)

    fine_next, merged = lax.map(one_group, (fine_pop.reshape(-1, SLOTS, 9, FINE_EDGE * FINE_EDGE), fine_block.reshape(-1, SLOTS)))
    blocks = coarse_next.reshape(9, NBX, COARSE_EDGE, NBY, COARSE_EDGE).transpose(1, 3, 0, 2, 4).reshape(NBX * NBY, 9 * COARSE_EDGE * COARSE_EDGE)
    blocks = blocks.at[fine_block].set(merged.reshape(FINE_TOTAL, 9 * COARSE_EDGE * COARSE_EDGE))
    coarse_out = blocks.reshape(NBX, NBY, 9, COARSE_EDGE, COARSE_EDGE).transpose(2, 0, 3, 1, 4).reshape(9, NXC, NYC)
    return coarse_out, fine_next.reshape(FINE_TOTAL, 9, FINE_EDGE * FINE_EDGE)
```

```python
import functools

import jax
import jax.numpy as jnp
from jax import lax
from jax.experimental import pallas as pl
from jax.experimental.pallas import tpu as pltpu
from jax.sharding import PartitionSpec as P

FINE_EDGE = 64
COARSE_EDGE = 32
CAP = 2
LANES = 128
WINDOW = 42

along_x = [0, 1, 0, -1, 0, 1, -1, -1, 1]
along_y = [0, 0, 1, 0, -1, 1, 1, -1, -1]
opposite = [0, 3, 4, 1, 2, 7, 8, 5, 6]
UP = (1, 5, 8)
DOWN = (3, 6, 7)
LEFT = (2, 5, 6)
RIGHT = (4, 8, 7)
ORDER = (0, 1, -1)

F32 = jnp.float32


def rates_of(relax_time, factor=1.0):
    return tuple((1.0 - factor) + factor * rate for rate in (1.4, 1.4, 1.2, 1.0 / relax_time))


COARSE = rates_of(0.65)
FINE = rates_of(0.8)
GHOST = rates_of(0.8, 0.8 / 1.3)
COALESCE = (1.0 - 1.3 / 0.8,) * 4


def relax(p, rates, which=tuple(range(9))):
    s_e, s_p, s_q, s_n = rates
    p0, p1, p2, p3, p4, p5, p6, p7, p8 = p
    s1, d1 = p1 + p3, p1 - p3
    s2, d2 = p2 + p4, p2 - p4
    s5, d5 = p5 + p7, p5 - p7
    s6, d6 = p6 + p8, p6 - p8
    axial, diagonal = s1 + s2, s5 + s6
    rho = p0 + axial + diagonal
    dq, sq = d5 - d6, d5 + d6
    jx, jy = d1 + dq, d2 + sq
    inv = 1.0 / rho
    xx, yy = jx * jx, jy * jy
    square = 3.0 * ((xx + yy) * inv)
    e = (axial - 2.0 * p0) + 4.0 * diagonal - square
    eps = 3.0 * (p0 - axial) + square
    a = (s_e / 36.0) * e
    b = (s_p / 36.0) * eps
    c = (s_q / 12.0) * (2.0 * dq - d1)
    d = (s_q / 12.0) * (2.0 * sq - d2)
    f = (s_n / 4.0) * ((s1 - s2) - (xx - yy) * inv)
    g = (s_n / 4.0) * ((s5 - s6) - (jx * jy) * inv)
    out = {}
    t = a + 2.0 * b
    w = 2.0 * a + b
    if 0 in which:
        out[0] = p0 + 4.0 * (a - b)
    if 1 in which:
        out[1] = p1 + ((t - f) + 2.0 * c)
    if 3 in which:
        out[3] = p3 + ((t - f) - 2.0 * c)
    if 2 in which:
        out[2] = p2 + ((t + f) + 2.0 * d)
    if 4 in which:
        out[4] = p4 + ((t + f) - 2.0 * d)
    if 5 in which:
        out[5] = p5 - ((w + g) + (c + d))
    if 7 in which:
        out[7] = p7 - ((w + g) - (c + d))
    if 6 in which:
        out[6] = p6 - ((w - g) - (c - d))
    if 8 in which:
        out[8] = p8 - ((w - g) + (c - d))
    return out


def lane_of(shape):
    return lax.broadcasted_iota(jnp.int32, shape, 1)


def row_of(shape):
    return lax.broadcasted_iota(jnp.int32, shape, 0)


def take_lanes(value, index):
    return jnp.take_along_axis(value, index, axis=1, mode="promise_in_bounds")


def table_kernel(columns, blocks_x, blocks_y, count_x, block_ref, id_ref, slot_ref, seen_ref):
    places = count_x * CAP
    for place in range(places):
        id_ref[place] = -1
        slot_ref[place] = -1
        slot_ref[places + place] = 0
    for owner in range(count_x):
        seen_ref[owner] = 0
    for slot in range(block_ref.shape[0]):
        block = block_ref[slot]
        column = lax.div(block, columns)
        row = block - column * columns
        owner = lax.div(column, blocks_x)
        rank = seen_ref[owner]
        seen_ref[owner] = rank + 1
        place = owner * CAP + rank
        id_ref[place] = (column - owner * blocks_x) * blocks_y + lax.rem(row, blocks_y)
        slot_ref[place] = slot
        slot_ref[places + place] = jnp.where(row == 0, 1, 0) + jnp.where(row == columns - 1, 2, 0)


def pack_kernel(coarse, low, high, sets, to_high, to_low, buf, ext, z, sems):
    width = coarse.shape[1]
    wide = width + LANES
    copies = [pltpu.make_async_copy(coarse.at[d], buf.at[d], sems.at[d]) for d in range(9)]
    for copy in copies:
        copy.start()
    ext[...] = jnp.full(ext.shape, 0.1, F32)
    ext[0, :, 0:2, :] = high[...]
    ext[1, :, 6:8, :] = low[...]
    z[:, width:, :] = jnp.full((2, LANES, LANES), 0.1, F32)
    rows = 64

    def columns_of(shape):
        lane = lane_of(shape)
        key = lax.rem(lane, 24)
        col = 32 * (key & 3) + (key >> 3) + jnp.where((key & 4) == 0, -2, 31)
        return lane, col & (LANES - 1)

    def place(group, part, start, count, value):
        lane, col = columns_of((count, LANES))
        got = take_lanes(value, col)
        if part:
            inside = (lane >= 24 * part) & (lane < 24 * part + 24)
            got = jnp.where(inside, got, z[group, pl.ds(start, count), :])
        z[group, pl.ds(start, count), :] = got

    for d in range(9):
        group, part = divmod(d, 5)
        place(group, part, width, 8, ext[0, d])
        place(group, part, wide - 8, 8, ext[1, d])
        copies[d].wait()

        def chunk(k, carry, group=group, part=part, d=d):
            start = pl.multiple_of(k * rows, rows)
            place(group, part, start, rows, buf[d, pl.ds(start, rows), :])
            return carry

        lax.fori_loop(0, width // rows, chunk, 0)
    to_high[...] = jnp.full(to_high.shape, 0.1, F32)
    to_low[...] = jnp.full(to_low.shape, 0.1, F32)
    for group in range(2):
        for t in range(wide // LANES):
            lanes = pl.ds(t * LANES, LANES)
            turned = z[group, t * LANES : (t + 1) * LANES, :].T
            for part in range(5 - group):
                d = 5 * group + part
                for s in range(3):
                    sets[s, d, :, lanes] = turned[24 * part + 8 * s : 24 * part + 8 * s + 8]
                base = 24 * part
                to_high[2 * d : 2 * d + 1, lanes] = turned[base : base + 1]
                to_high[2 * d + 1 : 2 * d + 2, lanes] = turned[base + 8 : base + 9]
                to_low[2 * d : 2 * d + 1, lanes] = turned[base + 15 : base + 16]
                to_low[2 * d + 1 : 2 * d + 2, lanes] = turned[base + 23 : base + 24]


def ghost_kernel(
    count_y,
    ids,
    coarse,
    low,
    high,
    sets,
    from_low,
    from_high,
    message,
    inject,
    first,
    last,
    turn,
    mt,
    old_t,
    post_t,
    new_t,
    g_t,
    pack_t,
    raw_r,
    post_r,
    new_r,
    g_r,
    pack_r,
    sems,
):
    blocks_x = coarse.shape[1]
    width = blocks_x * COARSE_EDGE
    wide = width + LANES
    tiles = wide // LANES
    width_y = LANES
    blocks_y = width_y // COARSE_EDGE
    total_y = width_y * count_y
    base_y = lax.axis_index("gy") * width_y
    copy_first = pltpu.make_async_copy(coarse.at[:, :, pl.ds(0, 8), :], first, sems.at[0])
    copy_last = pltpu.make_async_copy(
        coarse.at[:, :, pl.ds(COARSE_EDGE - 8, 8), :], last, sems.at[1]
    )
    copy_first.start()
    copy_last.start()

    turn[...] = jnp.full(turn.shape, 0.1, F32)
    for d in range(9):
        turn[4 * d : 4 * d + 2, :] = from_high[2 * d : 2 * d + 2, :]
        at = (4 * d - 2) % LANES
        turn[at : at + 2, :] = from_low[2 * d : 2 * d + 2, :]
    for t in range(tiles):
        mt[t * LANES : (t + 1) * LANES, :] = turn[:, t * LANES : (t + 1) * LANES].T
    tile = (8, LANES)
    row8 = row_of(tile)

    def collide_t(t, carry):
        lanes = pl.ds(pl.multiple_of(t * LANES, LANES), LANES)
        for s in range(3):
            p = []
            for d in range(9):
                value = sets[s, d, :, lanes]
                if s < 2:
                    value = jnp.where(row8 == 0, from_low[2 * d + s : 2 * d + s + 1, lanes], value)
                if s > 0:
                    value = jnp.where(
                        row8 == 7, from_high[2 * d + s - 1 : 2 * d + s, lanes], value
                    )
                if s == 1:
                    old_t[d, :, lanes] = value
                p.append(value)
            out = relax(p, COARSE)
            for d in range(9):
                post_t[s, d, :, lanes] = out[d]
        return carry

    lax.fori_loop(0, tiles, collide_t, 0)
    turn[...] = jnp.zeros(turn.shape, F32)
    row_t = row_of((8, wide))
    coord_t = base_y + 32 * (row_t & 3) + jnp.where(row_t < 4, -1, 32)
    for d in range(9):
        source = post_t[{1: 0, 0: 1, -1: 2}[along_y[d]], d]
        if along_x[d]:
            source = pltpu.roll(source, along_x[d] % wide, 1)
        back = coord_t - along_y[d]
        beyond = (back < 0) | (back >= total_y)
        new_t[d] = jnp.where(beyond, post_t[1, opposite[d]], source)
    for j in range(3):
        for side, (d, row) in enumerate(((LEFT[j], 0), (RIGHT[j], 7))):
            source = post_t[1, d]
            if along_x[d]:
                source = pltpu.roll(source, along_x[d] % wide, 1)
            turn[3 * side + j : 3 * side + j + 1, :] = source[row : row + 1, :]
    for t in range(width // LANES):
        inject[t * LANES : (t + 1) * LANES, :] = turn[:, t * LANES : (t + 1) * LANES].T

    def ghosts_t(t, carry):
        lanes = pl.ds(pl.multiple_of(t * LANES, LANES), LANES)
        old = [old_t[d, :, lanes] for d in range(9)]
        mean = [0.5 * (old[d] + new_t[d, :, lanes]) for d in range(9)]
        for sub, p in enumerate((old, mean)):
            out = relax(p, GHOST, LEFT + RIGHT)
            for j in range(3):
                g_t[sub, j, :, lanes] = jnp.where(row8 < 4, out[LEFT[j]], out[RIGHT[j]])
        return carry

    lax.fori_loop(0, tiles, ghosts_t, 0)
    lane8 = lane_of(tile)
    for sub in range(2):
        moved = [pltpu.roll(g_t[sub, j], 1, 1) for j in range(3)]
        for bx in range(blocks_x):
            t, off = divmod(COARSE_EDGE * bx, LANES)
            got = []
            for j in range(3):
                shift = (WINDOW * j - off) % LANES
                value = moved[j][:, t * LANES : (t + 1) * LANES]
                value = pltpu.roll(value, shift, 1) if shift else value
                if off == LANES - COARSE_EDGE:
                    after = moved[j][:, (t + 1) * LANES : (t + 2) * LANES]
                    after = pltpu.roll(after, shift, 1)
                    value = jnp.where(lane8 < WINDOW * j + COARSE_EDGE, value, after)
                got.append(value)
            pack_t[sub, bx] = jnp.where(
                lane8 < WINDOW, got[0], jnp.where(lane8 < 2 * WINDOW, got[1], got[2])
            )

    plane = (blocks_x, LANES)
    rows_b = row_of(plane)

    def lower(value, row):
        return jnp.where(rows_b == 0, row, pltpu.roll(value, 1, 0))

    def upper(value, row):
        return jnp.where(rows_b == blocks_x - 1, row, pltpu.roll(value, blocks_x - 1, 0))

    def every(ref, start, step):
        return ref[pl.ds(start, blocks_x, stride=step), :]

    side_rows = [every(mt, c, COARSE_EDGE) for c in (0, 1, COARSE_EDGE - 2, COARSE_EDGE - 1)]
    m0, m1, m30, m31 = side_rows
    extra = (
        lower(m30, mt[wide - 2 : wide - 1, :]),
        lower(m31, mt[wide - 1 : wide, :]),
        m0,
        m31,
        upper(m0, mt[width : width + 1, :]),
        upper(m1, mt[width + 1 : width + 2, :]),
    )
    copy_first.wait()
    copy_last.wait()
    first2 = first.reshape(9 * blocks_x * 8, LANES)
    last2 = last.reshape(9 * blocks_x * 8, LANES)
    for d in range(9):
        at = d * blocks_x * 8
        a0, a1 = every(first2, at, 8), every(first2, at + 1, 8)
        b30, b31 = every(last2, at + 6, 8), every(last2, at + 7, 8)
        main = (
            lower(b30, low[d, 0:1, :]),
            lower(b31, low[d, 1:2, :]),
            a0,
            b31,
            upper(a0, high[d, 0:1, :]),
            upper(a1, high[d, 1:2, :]),
        )
        for s in range(6):
            raw_r[s, d, :, 0:LANES] = main[s]
            value = extra[s]
            raw_r[s, d, :, LANES:] = pltpu.roll(value, (-4 * d) % LANES, 1) if d else value

    def collide_r(k, carry):
        rows = pl.ds(pl.multiple_of(k * 8, 8), 8)
        for s in range(6):
            for half in range(2):
                lanes = pl.ds(half * LANES, LANES)
                out = relax([raw_r[s, d, rows, lanes] for d in range(9)], COARSE)
                for d in range(9):
                    post_r[s, d, rows, lanes] = out[d]
        return carry

    lax.fori_loop(0, blocks_x // 8, collide_r, 0)
    double = (8, 2 * LANES)
    lane_r = lane_of(double)
    coord_r = base_y + jnp.where(lane_r < LANES + 2, lane_r, lane_r - 2 * LANES)

    def ghosts_r(k, carry):
        rows = pl.ds(pl.multiple_of(k * 8, 8), 8)
        for side in range(2):
            for d in range(9):
                source = post_r[3 * side + {1: 0, 0: 1, -1: 2}[along_x[d]], d, rows, :]
                if along_y[d]:
                    source = pltpu.roll(source, along_y[d] % (2 * LANES), 1)
                back = coord_r - along_y[d]
                beyond = (back < 0) | (back >= total_y)
                new_r[d] = jnp.where(beyond, post_r[3 * side + 1, opposite[d], rows, :], source)
            which = (UP, DOWN)[side]
            for half in range(2):
                lanes = pl.ds(half * LANES, LANES)
                old = [raw_r[3 * side + 1, d, rows, lanes] for d in range(9)]
                mean = [0.5 * (old[d] + new_r[d, :, lanes]) for d in range(9)]
                for sub, p in enumerate((old, mean)):
                    out = relax(p, GHOST, which)
                    for j in range(3):
                        g_r[j, sub, :, lanes] = out[which[j]]
            for sub in range(2):
                moved = [pltpu.roll(g_r[j, sub], 1, 1) for j in range(3)]
                for by in range(blocks_y):
                    got = []
                    for j in range(3):
                        off = COARSE_EDGE * by
                        shift = (WINDOW * j - off) % LANES
                        value = moved[j][:, 0:LANES]
                        value = pltpu.roll(value, shift, 1) if shift else value
                        if off == LANES - COARSE_EDGE:
                            after = pltpu.roll(moved[j][:, LANES:], shift, 1)
                            value = jnp.where(lane8 < WINDOW * j + COARSE_EDGE, value, after)
                        got.append(value)
                    pack_r[side, sub, by, rows, :] = jnp.where(
                        lane8 < WINDOW, got[0], jnp.where(lane8 < 2 * WINDOW, got[1], got[2])
                    )
        return carry

    lax.fori_loop(0, blocks_x // 8, ghosts_r, 0)

    def pick(q, carry):
        block = jnp.maximum(ids[q], 0)
        bx = lax.div(block, blocks_y)
        by = block - bx * blocks_y
        for sub in range(2):
            for side in range(2):
                row = 4 * sub + side
                message[q, row : row + 1, :] = pack_r[side, sub, by, pl.ds(bx, 1), :]
                row = 4 * sub + 2 + side
                message[q, row : row + 1, :] = pack_t[sub, bx, pl.ds(4 * side + by, 1), :]
        return carry

    lax.fori_loop(0, message.shape[0], pick, 0)


def start_kernel(slot, fine, post, sem):
    places = post.shape[1]
    copies = []
    for q in range(places):
        source = fine.at[:, pl.ds(jnp.maximum(slot[q], 0), 1), :]
        copy = pltpu.make_async_copy(source, post.at[:, pl.ds(q, 1), :], sem.at[q])
        copy.start()
        copies.append(copy)
    for copy in copies:
        copy.wait()

    def body(k, carry):
        lanes = pl.ds(pl.multiple_of(k * LANES, LANES), LANES)
        for h in range(places // 8):
            rows = pl.ds(8 * h, 8)
            out = relax([post[d, rows, lanes] for d in range(9)], FINE)
            for d in range(9):
                post[d, rows, lanes] = out[d]
        return carry

    lax.fori_loop(0, post.shape[2] // LANES, body, 0, unroll=2)


def fine_kernel(slot, post, ghosts, result, back, post_two, mean, line):
    places = post.shape[1]
    tiles = post.shape[2] // LANES
    tile = (8, LANES)
    lane, row = lane_of(tile), row_of(tile)
    low_half = lane < 64
    at_low = (lane & 63) == 0
    at_high = (lane & 63) == 63
    odd = (lane & 1) == 1
    ghosts2 = ghosts.reshape(places * 8, LANES)
    over = [WINDOW * j + 1 + (((lane & 63) - c) >> 1) for j, c in enumerate(ORDER)]
    cell = 2 * (lane & 63) + (lane >> 6)
    along = [(WINDOW * j + 1 + ((cell - c) >> 1)) & (LANES - 1) for j, c in enumerate(ORDER)]
    squeeze = 64 * ((lane >> 5) & 1) + 2 * (lane & 31) + (lane >> 6)

    def half(h, carry):
        rows = pl.ds(pl.multiple_of(8 * h, 8), 8)
        wall = jnp.zeros(tile, jnp.int32)
        for r in range(8):
            wall = jnp.where(row == r, slot[places + 8 * h + r], wall)
        wall_low = at_low & ((wall & 1) != 0)
        wall_high = at_high & ((wall & 2) != 0)

        def substep(sub, source, emit):
            border = [
                ghosts2[pl.ds(h * 64 + 4 * sub + side, 8, stride=8), :] for side in range(4)
            ]
            up = [take_lanes(border[0], over[j]) for j in range(3)]
            down = [take_lanes(border[1], over[j]) for j in range(3)]
            left = [take_lanes(border[2], along[j]) for j in range(3)]
            right = [take_lanes(border[3], along[j]) for j in range(3)]

            def load(d, k):
                return source[d, rows, k * LANES : (k + 1) * LANES]

            def crossed(d, k):
                if k < 0:
                    return up[UP.index(d)]
                if k == tiles:
                    return down[DOWN.index(d)]
                return pltpu.roll(load(d, k), (64 + along_y[d]) % LANES, 1)

            before = {d: crossed(d, -1) for d in UP}
            now = {d: crossed(d, 0) for d in DOWN}
            for k in range(tiles):
                out = []
                for d in range(9):
                    if along_x[d] > 0:
                        turned = crossed(d, k)
                        value = jnp.where(low_half, before[d], turned)
                        before[d] = turned
                    elif along_x[d] < 0:
                        turned = crossed(d, k + 1)
                        value = jnp.where(low_half, now[d], turned)
                        now[d] = turned
                    else:
                        value = load(d, k)
                        if along_y[d]:
                            value = pltpu.roll(value, along_y[d] % LANES, 1)
                    if along_y[d] > 0:
                        ghost = left[LEFT.index(d)]
                        ghost = pltpu.roll(ghost, (-k) % LANES, 1) if k else ghost
                        value = jnp.where(at_low, ghost, value)
                        value = jnp.where(wall_low, load(opposite[d], k), value)
                    elif along_y[d] < 0:
                        ghost = pltpu.roll(right[RIGHT.index(d)], 63 - k, 1)
                        value = jnp.where(at_high, ghost, value)
                        value = jnp.where(wall_high, load(opposite[d], k), value)
                    out.append(value)
                emit(k, out)

        def emit_first(k, p):
            out = relax(p, FINE)
            for d in range(9):
                post_two[d, :, k * LANES : (k + 1) * LANES] = out[d]

        def emit_second(k, p):
            j, i = divmod(k, 8)
            total = []
            for d in range(9):
                result[d, rows, k * LANES : (k + 1) * LANES] = p[d]
                pair = p[d] + pltpu.roll(p[d], 64, 1)
                value = pair + pltpu.roll(pair, LANES - 1 if j < 2 else 1, 1)
                if j:
                    kept = mean[d, i]
                    side = low_half if j & 1 == 0 else ~low_half
                    value = jnp.where(side & odd if j > 1 else side, value, kept)
                if j < 3:
                    mean[d, i] = value
                total.append(value)
            if j == 3:
                out = relax([0.25 * value for value in total], COALESCE)
                for d in range(9):
                    line[d, i * 8 : i * 8 + 8, :] = take_lanes(out[d], squeeze)

        post_rows = post
        substep(0, post_rows, emit_first)
        substep(1, _Rows(post_two), emit_second)
        for d in range(9):
            flat = line.at[d]
            for q in range(8):
                back[8 * h + q, d * 8 : d * 8 + 8, :] = flat[pl.ds(q, 8, stride=8), :]
        return carry

    lax.fori_loop(0, places // 8, half, 0)


class _Rows:
    def __init__(self, ref):
        self.ref = ref

    def __getitem__(self, key):
        d, _, lanes = key
        return self.ref[d, :, lanes]


def store_kernel(slot, result, fine, sem):
    places = result.shape[1]

    def copy(q):
        target = fine.at[:, pl.ds(jnp.maximum(slot[q], 0), 1), :]
        return pltpu.make_async_copy(result.at[:, pl.ds(q, 1), :], target, sem.at[q])

    for q in range(places):

        @pl.when(slot[q] >= 0)
        def _(q=q):
            copy(q).start()

    for q in range(places):

        @pl.when(slot[q] >= 0)
        def _(q=q):
            copy(q).wait()


def coarse_kernel(count_y, coarse, low, high, inject, after, new, post, sems):
    width = coarse.shape[1]
    tile = (8, LANES)
    lane = lane_of(tile)
    copies = [
        pltpu.make_async_copy(coarse.at[d], post.at[d, pl.ds(8, width), :], sems.at[d])
        for d in range(9)
    ]
    for copy in copies:
        copy.start()
    out = relax([low[d, 1:2, :] for d in range(9)], COARSE)
    for d in range(9):
        post[d, 7:8, :] = out[d]
    out = relax([high[d, 0:1, :] for d in range(9)], COARSE)
    for d in range(9):
        post[d, width + 8 : width + 9, :] = out[d]
    for copy in copies:
        copy.wait()

    def collide(k, carry):
        rows = pl.ds(pl.multiple_of(8 + 8 * k, 8), 8)
        out = relax([post[d, rows, :] for d in range(9)], COARSE)
        for d in range(9):
            post[d, rows, :] = out[d]
        return carry

    lax.fori_loop(0, width // 8, collide, 0, unroll=4)
    index_y = lax.axis_index("gy")
    wall_low = (lane == 0) & (index_y == 0)
    wall_high = (lane == LANES - 1) & (index_y == count_y - 1)

    def stream(k, carry):
        start = pl.multiple_of(8 * k, 8)
        edge = inject[pl.ds(start, 8), :]
        for d in range(9):
            value = post[d, pl.ds(start + (8 - along_x[d]), 8), :]
            if along_y[d]:
                value = pltpu.roll(value, along_y[d] % LANES, 1)
                same = post[opposite[d], pl.ds(start + 8, 8), :]
                if along_y[d] > 0:
                    j = LEFT.index(d)
                    value = jnp.where(lane == 0, pltpu.roll(edge, (-j) % LANES, 1), value)
                    value = jnp.where(wall_low, same, value)
                else:
                    j = RIGHT.index(d)
                    moved = pltpu.roll(edge, LANES - 4 - j, 1)
                    value = jnp.where(lane == LANES - 1, moved, value)
                    value = jnp.where(wall_high, same, value)
            new[d, pl.ds(start, 8), :] = value
        return carry

    lax.fori_loop(0, width // 8, stream, 0, unroll=4)


def patch_kernel(blocks_y, ids, new, back, out, buf, sems):
    width = new.shape[1]
    load = pltpu.make_async_copy(new, buf, sems.at[0])
    load.start()
    lane = lane_of((8, LANES))
    load.wait()

    def patch(q, carry):
        block = ids[q]

        @pl.when(block >= 0)
        def _():
            bx = lax.div(block, blocks_y)
            by = block - bx * blocks_y
            inside = (lane >> 5) == by
            for d in range(9):
                value = back[q, d * 8 : d * 8 + 8, :]
                for j in range(4):
                    rows = pl.ds(pl.multiple_of(COARSE_EDGE * bx + 8 * j, 8), 8)
                    moved = pltpu.roll(value, lax.rem(by + 4 - j, 4) * 32, 1)
                    buf[d, rows, :] = jnp.where(inside, moved, buf[d, rows, :])

        return carry

    lax.fori_loop(0, ids.shape[0], patch, 0)
    store = pltpu.make_async_copy(buf, out, sems.at[1])
    store.start()
    store.wait()


def local(coarse_pop, fine_pop, fine_block):
    width_x, width_y = coarse_pop.shape[1:]
    blocks_x = width_x // COARSE_EDGE
    blocks_y = width_y // COARSE_EDGE
    count_x = lax.axis_size("gx")
    count_y = lax.axis_size("gy")
    columns = blocks_y * count_y
    places = count_x * CAP
    slots = fine_block.shape[0]
    cells = FINE_EDGE * FINE_EDGE
    wide = width_x + LANES
    smem = pl.BlockSpec(memory_space=pltpu.SMEM)
    vmem = pl.BlockSpec(memory_space=pltpu.VMEM)
    hbm = pl.BlockSpec(memory_space=pl.ANY)
    sds = jax.ShapeDtypeStruct
    forward = [(i, (i + 1) % count_x) for i in range(count_x)]
    backward = [(target, source) for source, target in forward]
    low = lax.ppermute(coarse_pop[:, width_x - 2 :, :], "gx", forward)
    high = lax.ppermute(coarse_pop[:, :2, :], "gx", backward)
    ids, slot = pl.pallas_call(
        functools.partial(table_kernel, columns, blocks_x, blocks_y, count_x),
        out_shape=(sds((places,), jnp.int32), sds((2 * places,), jnp.int32)),
        in_specs=[smem],
        out_specs=(smem, smem),
        scratch_shapes=[pltpu.SMEM((count_x,), jnp.int32)],
        name="table",
    )(fine_block)
    wanted = lax.all_to_all(ids, "gx", split_axis=0, concat_axis=0, tiled=True)
    sets, to_high, to_low = pl.pallas_call(
        pack_kernel,
        out_shape=(sds((3, 9, 8, wide), F32), sds((24, wide), F32), sds((24, wide), F32)),
        in_specs=[hbm, vmem, vmem],
        out_specs=(vmem, vmem, vmem),
        scratch_shapes=[
            pltpu.VMEM((9, width_x, LANES), F32),
            pltpu.VMEM((2, 9, 8, LANES), F32),
            pltpu.VMEM((2, wide, LANES), F32),
            pltpu.SemaphoreType.DMA((9,)),
        ],
        name="pack",
    )(coarse_pop, low, high)
    forward_y = [(i, (i + 1) % count_y) for i in range(count_y)]
    backward_y = [(target, source) for source, target in forward_y]
    from_low = lax.ppermute(to_high, "gy", forward_y)
    from_high = lax.ppermute(to_low, "gy", backward_y)
    fine_turned = jnp.transpose(fine_pop, (1, 0, 2))
    post = pl.pallas_call(
        start_kernel,
        out_shape=sds((9, places, cells), F32),
        in_specs=[smem, hbm],
        out_specs=vmem,
        scratch_shapes=[pltpu.SemaphoreType.DMA((places,))],
        name="start",
    )(slot, fine_turned)
    message, inject = pl.pallas_call(
        functools.partial(ghost_kernel, count_y),
        out_shape=(sds((places, 8, LANES), F32), sds((width_x, LANES), F32)),
        in_specs=[smem, hbm, vmem, vmem, vmem, vmem, vmem],
        out_specs=(vmem, vmem),
        scratch_shapes=[
            pltpu.VMEM((9, blocks_x, 8, LANES), F32),
            pltpu.VMEM((9, blocks_x, 8, LANES), F32),
            pltpu.VMEM((LANES, wide), F32),
            pltpu.VMEM((wide, LANES), F32),
            pltpu.VMEM((9, 8, wide), F32),
            pltpu.VMEM((3, 9, 8, wide), F32),
            pltpu.VMEM((9, 8, wide), F32),
            pltpu.VMEM((2, 3, 8, wide), F32),
            pltpu.VMEM((2, blocks_x, 8, LANES), F32),
            pltpu.VMEM((6, 9, blocks_x, 2 * LANES), F32),
            pltpu.VMEM((6, 9, blocks_x, 2 * LANES), F32),
            pltpu.VMEM((9, 8, 2 * LANES), F32),
            pltpu.VMEM((3, 2, 8, 2 * LANES), F32),
            pltpu.VMEM((2, 2, blocks_y, blocks_x, LANES), F32),
            pltpu.SemaphoreType.DMA((2,)),
        ],
        name="ghost",
    )(
        wanted,
        coarse_pop.reshape(9, blocks_x, COARSE_EDGE, width_y),
        low,
        high,
        sets,
        from_low,
        from_high,
    )
    ghosts = lax.all_to_all(message, "gx", split_axis=0, concat_axis=0, tiled=True)
    result, back = pl.pallas_call(
        fine_kernel,
        out_shape=(sds((9, places, cells), F32), sds((places, 72, LANES), F32)),
        in_specs=[smem, vmem, vmem],
        out_specs=(vmem, vmem),
        scratch_shapes=[
            pltpu.VMEM((9, 8, cells), F32),
            pltpu.VMEM((9, 8, 8, LANES), F32),
            pltpu.VMEM((9, 64, LANES), F32),
        ],
        name="fine",
    )(slot, post, ghosts)
    returned = lax.all_to_all(back, "gx", split_axis=0, concat_axis=0, tiled=True)
    fine_out = pl.pallas_call(
        store_kernel,
        out_shape=sds((9, slots, cells), F32),
        in_specs=[smem, vmem],
        out_specs=hbm,
        scratch_shapes=[pltpu.SemaphoreType.DMA((places,))],
        name="store",
    )(slot, result)
    new = pl.pallas_call(
        functools.partial(coarse_kernel, count_y),
        out_shape=sds((9, width_x, width_y), F32),
        in_specs=[hbm, vmem, vmem, vmem, hbm],
        out_specs=vmem,
        scratch_shapes=[
            pltpu.VMEM((9, width_x + 16, LANES), F32),
            pltpu.SemaphoreType.DMA((9,)),
        ],
        name="coarse",
    )(coarse_pop, low, high, inject, back)
    coarse_out = pl.pallas_call(
        functools.partial(patch_kernel, blocks_y),
        out_shape=sds((9, width_x, width_y), F32),
        in_specs=[smem, hbm, vmem],
        out_specs=hbm,
        scratch_shapes=[
            pltpu.VMEM((9, width_x, LANES), F32),
            pltpu.SemaphoreType.DMA((2,)),
        ],
        name="patch",
    )(wanted, new, returned)
    return (coarse_out, jnp.transpose(fine_out, (1, 0, 2)))


def solution(mesh):
    return jax.shard_map(
        local,
        mesh=mesh,
        in_specs=(P(None, "gx", "gy"), P(("gx", "gy"), None, None), P(("gx", "gy"))),
        out_specs=(P(None, "gx", "gy"), P(("gx", "gy"), None, None)),
        check_vma=False,
    )
```

```python
import functools

import jax
import jax.numpy as jnp
from jax import lax
from jax.experimental import pallas as pl
from jax.experimental.pallas import tpu as pltpu
from jax.sharding import PartitionSpec as P

FINE_EDGE = 64
COARSE_EDGE = 32
CAP = 2
LANES = 128
WINDOW = 42

along_x = [0, 1, 0, -1, 0, 1, -1, -1, 1]
along_y = [0, 0, 1, 0, -1, 1, 1, -1, -1]
opposite = [0, 3, 4, 1, 2, 7, 8, 5, 6]
UP = (1, 5, 8)
DOWN = (3, 6, 7)
LEFT = (2, 5, 6)
RIGHT = (4, 8, 7)
ORDER = (0, 1, -1)

F32 = jnp.float32
GRANT = pltpu.CompilerParams(vmem_limit_bytes=24 << 20)


def rates_of(relax_time, factor=1.0):
    return tuple((1.0 - factor) + factor * rate for rate in (1.4, 1.4, 1.2, 1.0 / relax_time))


COARSE = rates_of(0.65)
FINE = rates_of(0.8)
GHOST = rates_of(0.8, 0.8 / 1.3)
COALESCE = (1.0 - 1.3 / 0.8,) * 4


def relax(p, rates, which=tuple(range(9))):
    s_e, s_p, s_q, s_n = rates
    p0, p1, p2, p3, p4, p5, p6, p7, p8 = p
    s1, d1 = p1 + p3, p1 - p3
    s2, d2 = p2 + p4, p2 - p4
    s5, d5 = p5 + p7, p5 - p7
    s6, d6 = p6 + p8, p6 - p8
    axial, diagonal = s1 + s2, s5 + s6
    rho = p0 + axial + diagonal
    dq, sq = d5 - d6, d5 + d6
    jx, jy = d1 + dq, d2 + sq
    inv = 1.0 / rho
    xx, yy = jx * jx, jy * jy
    square = 3.0 * ((xx + yy) * inv)
    e = (axial - 2.0 * p0) + 4.0 * diagonal - square
    eps = 3.0 * (p0 - axial) + square
    a = (s_e / 36.0) * e
    b = (s_p / 36.0) * eps
    c = (s_q / 12.0) * (2.0 * dq - d1)
    d = (s_q / 12.0) * (2.0 * sq - d2)
    f = (s_n / 4.0) * ((s1 - s2) - (xx - yy) * inv)
    g = (s_n / 4.0) * ((s5 - s6) - (jx * jy) * inv)
    out = {}
    t = a + 2.0 * b
    w = 2.0 * a + b
    if 0 in which:
        out[0] = p0 + 4.0 * (a - b)
    if 1 in which:
        out[1] = p1 + ((t - f) + 2.0 * c)
    if 3 in which:
        out[3] = p3 + ((t - f) - 2.0 * c)
    if 2 in which:
        out[2] = p2 + ((t + f) + 2.0 * d)
    if 4 in which:
        out[4] = p4 + ((t + f) - 2.0 * d)
    if 5 in which:
        out[5] = p5 - ((w + g) + (c + d))
    if 7 in which:
        out[7] = p7 - ((w + g) - (c + d))
    if 6 in which:
        out[6] = p6 - ((w - g) - (c - d))
    if 8 in which:
        out[8] = p8 - ((w - g) + (c - d))
    return out


def lane_of(shape):
    return lax.broadcasted_iota(jnp.int32, shape, 1)


def row_of(shape):
    return lax.broadcasted_iota(jnp.int32, shape, 0)


def take_lanes(value, index):
    return jnp.take_along_axis(value, index, axis=1, mode="promise_in_bounds")


def ask_kernel(
    columns, blocks_x, blocks_y, count_x, block_hbm, coarse, ask, slot_ref, block_ref, id_ref, seen_ref, edge, rows, sems
):
    width = coarse.shape[1]
    places = count_x * CAP
    copies = [
        pltpu.make_async_copy(coarse.at[:, pl.ds(at, 8), :], edge.at[k], sems.at[k])
        for k, at in enumerate((0, width - 8))
    ]
    blocks = pltpu.make_async_copy(block_hbm, block_ref, sems.at[2])
    blocks.start()
    for copy in copies:
        copy.start()
    for place in range(places):
        id_ref[place] = -1
        slot_ref[place] = -1
        slot_ref[places + place] = 0
    for owner in range(count_x):
        seen_ref[owner] = 0
    blocks.wait()
    for slot in range(block_ref.shape[0]):
        block = block_ref[slot]
        column = lax.div(block, columns)
        row = block - column * columns
        owner = lax.div(column, blocks_x)
        rank = seen_ref[owner]
        seen_ref[owner] = rank + 1
        place = owner * CAP + rank
        id_ref[place] = (column - owner * blocks_x) * blocks_y + lax.rem(row, blocks_y)
        slot_ref[place] = slot
        slot_ref[places + place] = jnp.where(row == 0, 1, 0) + jnp.where(row == columns - 1, 2, 0)
    rows[...] = jnp.full(rows.shape, 0.1, F32)
    for copy in copies:
        copy.wait()
    for d in range(9):
        rows[0, 2 * d : 2 * d + 2, :] = edge[0, d, 0:2, :]
        rows[1, 2 * d : 2 * d + 2, :] = edge[1, d, 6:8, :]
    shape = rows.shape[1:]
    lane, row = lane_of(shape), row_of(shape)
    after = lax.rem(lax.axis_index("gx") + 1, count_x)
    for owner in range(count_x):
        number = jnp.zeros(shape, jnp.int32)
        for rank in range(CAP):
            number = jnp.where(lane == rank, id_ref[owner * CAP + rank], number)
        value = jnp.where(after == owner, rows[1], rows[0])
        ask[owner] = jnp.where(row == 18, number.astype(F32), value)


def columns_of(shape):
    lane = lane_of(shape)
    key = lax.rem(lane, 24)
    col = 32 * (key & 3) + (key >> 3) + jnp.where((key & 4) == 0, -2, 31)
    return lane, col & (LANES - 1)


def place_columns(z, d, start, count, value):
    group, part = divmod(d, 5)
    lane, col = columns_of((count, LANES))
    got = take_lanes(value, col)
    if part:
        inside = (lane >= 24 * part) & (lane < 24 * part + 24)
        got = jnp.where(inside, got, z[group, pl.ds(start, count), :])
    z[group, pl.ds(start, count), :] = got


def turn_columns(z, sets, to_high, to_low):
    to_high[...] = jnp.full(to_high.shape, 0.1, F32)
    to_low[...] = jnp.full(to_low.shape, 0.1, F32)
    for group in range(2):
        for t in range(z.shape[1] // LANES):
            lanes = pl.ds(t * LANES, LANES)
            turned = z[group, t * LANES : (t + 1) * LANES, :].T
            for part in range(5 - group):
                d = 5 * group + part
                for s in range(3):
                    sets[s, d, :, lanes] = turned[24 * part + 8 * s : 24 * part + 8 * s + 8]
                base = 24 * part
                to_high[2 * d : 2 * d + 1, lanes] = turned[base : base + 1]
                to_high[2 * d + 1 : 2 * d + 2, lanes] = turned[base + 8 : base + 9]
                to_low[2 * d : 2 * d + 1, lanes] = turned[base + 15 : base + 16]
                to_low[2 * d + 1 : 2 * d + 2, lanes] = turned[base + 23 : base + 24]


def pack_kernel(coarse, sets, to_high, to_low, buf, z, sems):
    width = coarse.shape[1]
    copies = [pltpu.make_async_copy(coarse.at[d], buf.at[d], sems.at[d]) for d in range(9)]
    for copy in copies:
        copy.start()
    rows = 512
    for d in range(9):
        copies[d].wait()

        def chunk(k, carry, d=d):
            start = pl.multiple_of(k * rows, rows)
            place_columns(z, d, start, rows, buf[d, pl.ds(start, rows), :])
            return carry

        lax.fori_loop(0, width // rows, chunk, 0)
    turn_columns(z, sets, to_high, to_low)


def neighbours(count_x):
    index = lax.axis_index("gx")
    return lax.rem(index + count_x - 1, count_x), lax.rem(index + 1, count_x)


def corner_kernel(count_x, asked, sets, to_high, to_low, ext, z):
    before, after = neighbours(count_x)
    ext[...] = jnp.full(ext.shape, 0.1, F32)
    z[...] = jnp.full(z.shape, 0.1, F32)
    for d in range(9):
        ext[0, d, 0:2, :] = asked[after, 2 * d : 2 * d + 2, :]
        ext[1, d, 6:8, :] = asked[before, 2 * d : 2 * d + 2, :]
    for d in range(9):
        place_columns(z, d, 0, 8, ext[0, d])
        place_columns(z, d, LANES - 8, 8, ext[1, d])
    turn_columns(z, sets, to_high, to_low)


def window(parts, j, off):
    lane = lane_of((8, LANES))
    before, value, after = parts
    shift = (WINDOW * j - off + 1) % LANES

    def move(part):
        return pltpu.roll(part, shift, 1) if shift else part

    value = move(value)
    if off == 0:
        value = jnp.where(lane == WINDOW * j, move(before), value)
    if off == LANES - COARSE_EDGE:
        value = jnp.where(lane == WINDOW * j + COARSE_EDGE + 1, move(after), value)
    return value


def join(parts):
    lane = lane_of((8, LANES))
    first, second, third = parts
    return jnp.where(lane < WINDOW, first, jnp.where(lane < 2 * WINDOW, second, third))


def ghost_kernel(
    count_x,
    count_y,
    coarse,
    asked,
    sets_main,
    low_main,
    high_main,
    sets_ext,
    low_ext,
    high_ext,
    message,
    inject_hbm,
    ids,
    numbers,
    first,
    last,
    turn,
    mt,
    old_t,
    post_t,
    new_t,
    g_t,
    pack_t,
    raw_r,
    post_r,
    new_r,
    g_r,
    far,
    pack_r,
    inject,
    sems,
):
    blocks_x = coarse.shape[1]
    width = blocks_x * COARSE_EDGE
    wide = width + LANES
    tiles = wide // LANES
    width_y = LANES
    blocks_y = width_y // COARSE_EDGE
    total_y = width_y * count_y
    base_y = lax.axis_index("gy") * width_y
    copy_first = pltpu.make_async_copy(coarse.at[:, :, pl.ds(0, 8), :], first, sems.at[0])
    copy_last = pltpu.make_async_copy(
        coarse.at[:, :, pl.ds(COARSE_EDGE - 8, 8), :], last, sems.at[1]
    )
    copy_first.start()
    copy_last.start()
    copy_ids = pltpu.make_async_copy(asked.at[:, pl.ds(16, 8), :], numbers, sems.at[2])
    copy_ids.start()
    index_before, index_after = neighbours(count_x)

    turn[...] = jnp.full(turn.shape, 0.1, F32)
    for d in range(9):
        at = (4 * d - 2) % LANES
        turn[4 * d : 4 * d + 2, 0:width] = high_main[2 * d : 2 * d + 2, :]
        turn[4 * d : 4 * d + 2, width:] = high_ext[2 * d : 2 * d + 2, :]
        turn[at : at + 2, 0:width] = low_main[2 * d : 2 * d + 2, :]
        turn[at : at + 2, width:] = low_ext[2 * d : 2 * d + 2, :]
    for t in range(tiles):
        mt[t * LANES : (t + 1) * LANES, :] = turn[:, t * LANES : (t + 1) * LANES].T
    tile = (8, LANES)
    row8 = row_of(tile)

    def collide_tile(sets, from_low, from_high, at, lanes):
        for s in range(3):
            p = []
            for d in range(9):
                value = sets[s, d, :, at]
                if s < 2:
                    value = jnp.where(row8 == 0, from_low[2 * d + s : 2 * d + s + 1, at], value)
                if s > 0:
                    value = jnp.where(row8 == 7, from_high[2 * d + s - 1 : 2 * d + s, at], value)
                if s == 1:
                    old_t[d, :, lanes] = value
                p.append(value)
            out = relax(p, COARSE)
            for d in range(9):
                post_t[s, d, :, lanes] = out[d]

    def collide_t(t, carry):
        lanes = pl.ds(pl.multiple_of(t * LANES, LANES), LANES)
        collide_tile(sets_main, low_main, high_main, lanes, lanes)
        return carry

    lax.fori_loop(0, tiles - 1, collide_t, 0)
    collide_tile(sets_ext, low_ext, high_ext, pl.ds(0, LANES), pl.ds(width, LANES))
    turn[...] = jnp.zeros(turn.shape, F32)
    row_t = row_of((8, wide))
    coord_t = base_y + 32 * (row_t & 3) + jnp.where(row_t < 4, -1, 32)
    for d in range(9):
        source = post_t[{1: 0, 0: 1, -1: 2}[along_y[d]], d]
        if along_x[d]:
            source = pltpu.roll(source, along_x[d] % wide, 1)
        back = coord_t - along_y[d]
        beyond = (back < 0) | (back >= total_y)
        new_t[d] = jnp.where(beyond, post_t[1, opposite[d]], source)
    for j in range(3):
        for side, (d, row) in enumerate(((LEFT[j], 0), (RIGHT[j], 7))):
            source = post_t[1, d]
            if along_x[d]:
                source = pltpu.roll(source, along_x[d] % wide, 1)
            turn[3 * side + j : 3 * side + j + 1, :] = source[row : row + 1, :]
    for t in range(width // LANES):
        inject[t * LANES : (t + 1) * LANES, :] = turn[:, t * LANES : (t + 1) * LANES].T
    copy_inject = pltpu.make_async_copy(inject, inject_hbm, sems.at[3])
    copy_inject.start()

    def ghosts_t(t, carry):
        lanes = pl.ds(pl.multiple_of(t * LANES, LANES), LANES)
        old = [old_t[d, :, lanes] for d in range(9)]
        mean = [0.5 * (old[d] + new_t[d, :, lanes]) for d in range(9)]
        for sub, p in enumerate((old, mean)):
            out = relax(p, GHOST, LEFT + RIGHT)
            for j in range(3):
                g_t[sub, j, :, lanes] = jnp.where(row8 < 4, out[LEFT[j]], out[RIGHT[j]])
        return carry

    lax.fori_loop(0, tiles, ghosts_t, 0)
    for sub in range(2):
        for bx in range(blocks_x):
            t, off = divmod(COARSE_EDGE * bx, LANES)
            near = [(t + step) % tiles for step in (-1, 0, 1)]
            got = []
            for j in range(3):
                parts = [g_t[sub, j, :, LANES * k : LANES * (k + 1)] for k in near]
                got.append(window(parts, j, off))
            pack_t[sub, bx] = join(got)

    plane = (blocks_x, LANES)
    rows_b = row_of(plane)

    def lower(value, row):
        return jnp.where(rows_b == 0, row, pltpu.roll(value, 1, 0))

    def upper(value, row):
        return jnp.where(rows_b == blocks_x - 1, row, pltpu.roll(value, blocks_x - 1, 0))

    def every(ref, start, step):
        return ref[pl.ds(start, blocks_x, stride=step), :]

    side_rows = [every(mt, c, COARSE_EDGE) for c in (0, 1, COARSE_EDGE - 2, COARSE_EDGE - 1)]
    m0, m1, m30, m31 = side_rows
    extra = (
        lower(m30, mt[wide - 2 : wide - 1, :]),
        lower(m31, mt[wide - 1 : wide, :]),
        m0,
        m31,
        upper(m0, mt[width : width + 1, :]),
        upper(m1, mt[width + 1 : width + 2, :]),
    )
    copy_first.wait()
    copy_last.wait()
    first2 = first.reshape(9 * blocks_x * 8, LANES)
    last2 = last.reshape(9 * blocks_x * 8, LANES)
    for k in range(6):
        far[k] = extra[k]

    def raw_rows(d, carry):
        at = d * (blocks_x * 8)
        a0, a1 = every(first2, at, 8), every(first2, at + 1, 8)
        b30, b31 = every(last2, at + 6, 8), every(last2, at + 7, 8)
        main = (
            lower(b30, asked[index_before, pl.ds(2 * d, 1), :]),
            lower(b31, asked[index_before, pl.ds(2 * d + 1, 1), :]),
            a0,
            b31,
            upper(a0, asked[index_after, pl.ds(2 * d, 1), :]),
            upper(a1, asked[index_after, pl.ds(2 * d + 1, 1), :]),
        )
        for k in range(6):
            raw_r[k, d, :, 0:LANES] = main[k]
            raw_r[k, d, :, LANES:] = pltpu.roll(far[k], lax.rem(LANES - 4 * d, LANES), 1)
        return carry

    lax.fori_loop(0, 9, raw_rows, 0)

    def collide_r(k, carry):
        rows = pl.ds(pl.multiple_of(k * 8, 8), 8)
        for s in range(6):
            for half in range(2):
                lanes = pl.ds(half * LANES, LANES)
                out = relax([raw_r[s, d, rows, lanes] for d in range(9)], COARSE)
                for d in range(9):
                    post_r[s, d, rows, lanes] = out[d]
        return carry

    lax.fori_loop(0, blocks_x // 8, collide_r, 0)
    double = (8, 2 * LANES)
    lane_r = lane_of(double)
    coord_r = base_y + jnp.where(lane_r < LANES + 2, lane_r, lane_r - 2 * LANES)

    def ghosts_r(k, carry):
        rows = pl.ds(pl.multiple_of(k * 8, 8), 8)
        for side in range(2):
            for d in range(9):
                source = post_r[3 * side + {1: 0, 0: 1, -1: 2}[along_x[d]], d, rows, :]
                if along_y[d]:
                    source = pltpu.roll(source, along_y[d] % (2 * LANES), 1)
                back = coord_r - along_y[d]
                beyond = (back < 0) | (back >= total_y)
                new_r[d] = jnp.where(beyond, post_r[3 * side + 1, opposite[d], rows, :], source)
            which = (UP, DOWN)[side]
            for half in range(2):
                lanes = pl.ds(half * LANES, LANES)
                old = [raw_r[3 * side + 1, d, rows, lanes] for d in range(9)]
                mean = [0.5 * (old[d] + new_r[d, :, lanes]) for d in range(9)]
                for sub, p in enumerate((old, mean)):
                    out = relax(p, GHOST, which)
                    for j in range(3):
                        g_r[side, j, sub, rows, lanes] = out[which[j]]
        return carry

    lax.fori_loop(0, blocks_x // 8, ghosts_r, 0)

    def windows_r(k, carry):
        rows = pl.ds(pl.multiple_of(k * 8, 8), 8)
        for side in range(2):
            for sub in range(2):
                for by in range(blocks_y):
                    got = []
                    for j in range(3):
                        one = g_r[side, j, sub, rows, 0:LANES]
                        two = g_r[side, j, sub, rows, LANES:]
                        got.append(window((two, one, two), j, COARSE_EDGE * by))
                    pack_r[side, sub, by, rows, :] = join(got)
        return carry

    lax.fori_loop(0, blocks_x // 8, windows_r, 0)

    copy_ids.wait()
    for q in range(message.shape[0]):
        ids[q] = numbers[q // CAP, 2, q % CAP].astype(jnp.int32)

    def pick(q, carry):
        block = jnp.maximum(ids[q], 0)
        bx = lax.div(block, blocks_y)
        by = block - bx * blocks_y
        for sub in range(2):
            for side in range(2):
                row = 4 * sub + side
                message[q, row : row + 1, :] = pack_r[side, sub, by, pl.ds(bx, 1), :]
                row = 4 * sub + 2 + side
                message[q, row : row + 1, :] = pack_t[sub, bx, pl.ds(4 * side + by, 1), :]
        return carry

    lax.fori_loop(0, message.shape[0], pick, 0)
    copy_inject.wait()


def start_kernel(slot, fine, post, sem):
    places = post.shape[1]
    copies = []
    for q in range(places):
        source = fine.at[:, pl.ds(jnp.maximum(slot[q], 0), 1), :]
        copy = pltpu.make_async_copy(source, post.at[:, pl.ds(q, 1), :], sem.at[q])
        copy.start()
        copies.append(copy)
    for copy in copies:
        copy.wait()

    def body(k, carry):
        lanes = pl.ds(pl.multiple_of(k * LANES, LANES), LANES)
        for h in range(places // 8):
            rows = pl.ds(8 * h, 8)
            out = relax([post[d, rows, lanes] for d in range(9)], FINE)
            for d in range(9):
                post[d, rows, lanes] = out[d]
        return carry

    lax.fori_loop(0, post.shape[2] // LANES, body, 0, unroll=2)


def fine_kernel(slot, post, ghosts, fine, back, result, post_two, line, mean, swapped, sem):
    places = post.shape[1]
    tiles = post.shape[2] // LANES
    tile = (8, LANES)
    lane, row = lane_of(tile), row_of(tile)
    low_half = lane < 64
    at_low = (lane & 63) == 0
    at_high = (lane & 63) == 63
    ghosts2 = ghosts.reshape(places * 8, LANES)
    over = [WINDOW * j + 1 + (((lane & 63) - c) >> 1) for j, c in enumerate(ORDER)]
    even = (lane & 1) == 0
    turn_back = jnp.where(even, lane, (lane - 63) & (LANES - 1))
    cell = (turn_back & 63) + (turn_back >> 6)
    along = [(WINDOW * j + 1 + ((cell - c) >> 1)) & (LANES - 1) for j, c in enumerate(ORDER)]
    squeeze = 64 * ((lane >> 5) & 1) + 2 * (lane & 31) + (lane >> 6)

    def copy(q):
        target = fine.at[:, pl.ds(jnp.maximum(slot[q], 0), 1), :]
        return pltpu.make_async_copy(result.at[:, pl.ds(q, 1), :], target, sem.at[q])

    def half(h, carry):
        rows = pl.ds(pl.multiple_of(8 * h, 8), 8)
        wall = jnp.zeros(tile, jnp.int32)
        for r in range(8):
            wall = jnp.where(row == r, slot[places + 8 * h + r], wall)
        wall_low = at_low & ((wall & 1) != 0)
        wall_high = at_high & ((wall & 2) != 0)

        def substep(sub, source, emit):
            border = [
                ghosts2[pl.ds(h * 64 + 4 * sub + side, 8, stride=8), :] for side in range(4)
            ]
            up = [take_lanes(border[0], over[j]) for j in range(3)]
            down = [take_lanes(border[1], over[j]) for j in range(3)]
            beside = [
                jnp.where(even, take_lanes(border[2], along[j]), take_lanes(border[3], along[j]))
                for j in range(3)
            ]

            def load(d, k):
                return source[d, rows, k * LANES : (k + 1) * LANES]

            def crossed(d, k):
                if k < 0:
                    return up[UP.index(d)]
                if k == tiles:
                    return down[DOWN.index(d)]
                return pltpu.roll(load(d, k), (64 + along_y[d]) % LANES, 1)

            before = {d: crossed(d, -1) for d in UP}
            now = {d: crossed(d, 0) for d in DOWN}
            for k in range(tiles):
                ghosts_k = [
                    pltpu.roll(value, (-2 * k) % LANES, 1) if k else value for value in beside
                ]
                out = []
                for d in range(9):
                    if along_x[d] > 0:
                        turned = crossed(d, k)
                        value = jnp.where(low_half, before[d], turned)
                        before[d] = turned
                    elif along_x[d] < 0:
                        turned = crossed(d, k + 1)
                        value = jnp.where(low_half, now[d], turned)
                        now[d] = turned
                    else:
                        value = load(d, k)
                        if along_y[d]:
                            value = pltpu.roll(value, along_y[d] % LANES, 1)
                    if along_y[d] > 0:
                        value = jnp.where(at_low, ghosts_k[LEFT.index(d)], value)
                        value = jnp.where(wall_low, load(opposite[d], k), value)
                    elif along_y[d] < 0:
                        value = jnp.where(at_high, ghosts_k[RIGHT.index(d)], value)
                        value = jnp.where(wall_high, load(opposite[d], k), value)
                    out.append(value)
                emit(k, out)

        def emit_first(k, p):
            out = relax(p, FINE)
            for d in range(9):
                post_two[d, :, k * LANES : (k + 1) * LANES] = out[d]

        def emit_second(k, p):
            for d in range(9):
                result[d, rows, k * LANES : (k + 1) * LANES] = p[d]

        post_rows = post
        substep(0, post_rows, emit_first)
        substep(1, _Rows(post_two), emit_second)
        for r in range(8):

            @pl.when(slot[8 * h + r] >= 0)
            def _(r=r):
                copy(8 * h + r).start()

        def tile_of(ref, d, k):
            return ref[d, rows, pl.ds(pl.multiple_of(k * LANES, LANES), LANES)]

        def pair_up(step, carry):
            for u in range(4):
                i = 4 * step + u
                for d in range(9):
                    pairs = []
                    for m in range(2):
                        one = tile_of(result, d, i + 16 * m)
                        two = tile_of(result, d, i + 16 * m + 8)
                        other = pltpu.roll(jnp.where(low_half, two, one), 64, 1)
                        pairs.append(jnp.where(low_half, one, two) + other)
                    mean[d, i] = jnp.where(even, pairs[0], pairs[1])
                    swapped[d, i] = jnp.where(even, pairs[1], pairs[0])
            return carry

        def merge(step, carry):
            for u in range(4):
                i = 4 * step + u
                total = []
                for d in range(9):
                    moved = swapped[d, i]
                    moved = jnp.where(even, pltpu.roll(moved, 127, 1), pltpu.roll(moved, 1, 1))
                    total.append(0.25 * (mean[d, i] + moved))
                out = relax(total, COALESCE)
                for d in range(9):
                    mean[d, i] = out[d]
            return carry

        def compress(step, carry):
            for u in range(4):
                i = 4 * step + u
                for d in range(9):
                    at = pl.ds(pl.multiple_of(i * 8, 8), 8)
                    line[d, at, :] = take_lanes(mean[d, i], squeeze)
            return carry

        lax.fori_loop(0, 2, pair_up, 0)
        lax.fori_loop(0, 2, merge, 0)
        lax.fori_loop(0, 2, compress, 0)
        for d in range(9):
            flat = line.at[d]
            for q in range(8):
                back[8 * h + q, d * 8 : d * 8 + 8, :] = flat[pl.ds(q, 8, stride=8), :]
        return carry

    lax.fori_loop(0, places // 8, half, 0)
    for q in range(places):

        @pl.when(slot[q] >= 0)
        def _(q=q):
            copy(q).wait()


class _Rows:
    def __init__(self, ref):
        self.ref = ref

    def __getitem__(self, key):
        d, _, lanes = key
        return self.ref[d, :, lanes]


def coarse_kernel(
    count_x, count_y, coarse, asked, inject_hbm, after, ids, base, strips, home, inject, new, post, load, save, cut
):
    width = coarse.shape[1]
    places = ids.shape[0]
    blocks_y = coarse.shape[2] // COARSE_EDGE
    tile = (8, LANES)
    lane = lane_of(tile)
    parts = 4
    size = width // parts
    copies = [
        pltpu.make_async_copy(
            coarse.at[:, pl.ds(k * size, size), :],
            post.at[:, pl.ds(8 + k * size, size), :],
            load.at[k],
        )
        for k in range(parts)
    ]
    for copy in copies:
        copy.start()
    copy_inject = pltpu.make_async_copy(inject_hbm, inject, load.at[parts])
    copy_inject.start()
    before, following = neighbours(count_x)
    out = relax([asked[before, 2 * d + 1 : 2 * d + 2, :] for d in range(9)], COARSE)
    for d in range(9):
        post[d, 7:8, :] = out[d]
    out = relax([asked[following, 2 * d : 2 * d + 1, :] for d in range(9)], COARSE)
    for d in range(9):
        post[d, width + 8 : width + 9, :] = out[d]

    def collide(k, carry):
        rows = pl.ds(pl.multiple_of(8 + 8 * k, 8), 8)
        out = relax([post[d, rows, :] for d in range(9)], COARSE)
        for d in range(9):
            post[d, rows, :] = out[d]
        return carry

    index_y = lax.axis_index("gy")
    wall_low = (lane == 0) & (index_y == 0)
    wall_high = (lane == LANES - 1) & (index_y == count_y - 1)

    def stream(k, carry):
        start = pl.multiple_of(8 * k, 8)
        edge = inject[pl.ds(start, 8), :]
        for d in range(9):
            value = post[d, pl.ds(start + (8 - along_x[d]), 8), :]
            if along_y[d]:
                value = pltpu.roll(value, along_y[d] % LANES, 1)
                same = post[opposite[d], pl.ds(start + 8, 8), :]
                if along_y[d] > 0:
                    j = LEFT.index(d)
                    value = jnp.where(lane == 0, pltpu.roll(edge, (-j) % LANES, 1), value)
                    value = jnp.where(wall_low, same, value)
                else:
                    j = RIGHT.index(d)
                    moved = pltpu.roll(edge, LANES - 4 - j, 1)
                    value = jnp.where(lane == LANES - 1, moved, value)
                    value = jnp.where(wall_high, same, value)
            new[d, pl.ds(start, 8), :] = value
        return carry

    copy_inject.wait()
    copies[0].wait()
    lax.fori_loop(0, size // 8, collide, 0, unroll=4)
    stores = []
    for k in range(parts):
        if k + 1 < parts:
            copies[k + 1].wait()
            lax.fori_loop((k + 1) * size // 8, (k + 2) * size // 8, collide, 0, unroll=4)
        lax.fori_loop(k * size // 8, (k + 1) * size // 8, stream, 0, unroll=4)
        rows = pl.ds(k * size, size)
        store = pltpu.make_async_copy(new.at[:, rows, :], base.at[:, rows, :], save.at[k])
        store.start()
        stores.append(store)

    def column(q):
        return lax.div(jnp.maximum(ids[q], 0), blocks_y)

    def strip(q):
        rows = pl.ds(pl.multiple_of(COARSE_EDGE * column(q), COARSE_EDGE), COARSE_EDGE)
        return pltpu.make_async_copy(
            new.at[:, rows, :], strips.at[:, pl.ds(COARSE_EDGE * q, COARSE_EDGE), :], cut.at[q]
        )

    for q in range(places):

        @pl.when(ids[q] >= 0)
        def _(q=q):
            strip(q).start()

    for q in range(places):
        first, last = jnp.int32(q), jnp.int32(1)
        for other in reversed(range(places)):
            if other != q:
                same = (ids[q] >= 0) & (ids[other] >= 0) & (column(q) == column(other))
                if other < q:
                    first = jnp.where(same, other, first)
                else:
                    last = jnp.where(same, 0, last)
        home[q] = first
        home[places + q] = last
    for store in stores:
        store.wait()
    for q in range(places):

        @pl.when(ids[q] >= 0)
        def _(q=q):
            strip(q).wait()


def patch_kernel(blocks_y, ids, home, base, strips_in, back, strips, out, save):
    lane = lane_of((8, LANES))
    places = ids.shape[0]

    def store(q):
        bx = lax.div(jnp.maximum(ids[q], 0), blocks_y)
        rows = pl.ds(pl.multiple_of(COARSE_EDGE * bx, COARSE_EDGE), COARSE_EDGE)
        own = pl.ds(pl.multiple_of(COARSE_EDGE * home[q], COARSE_EDGE), COARSE_EDGE)
        return pltpu.make_async_copy(strips.at[:, own, :], out.at[:, rows, :], save.at[q])

    def patch(q, carry):
        @pl.when(ids[q] >= 0)
        def _():
            by = lax.rem(ids[q], blocks_y)
            inside = (lane >> 5) == by
            start = pl.multiple_of(COARSE_EDGE * home[q], COARSE_EDGE)
            for group in (range(5), range(5, 9)):
                merged = []
                for d in group:
                    value = back[q, d * 8 : d * 8 + 8, :]
                    for j in range(4):
                        moved = pltpu.roll(value, lax.rem(by + 4 - j, 4) * 32, 1)
                        merged.append((d, pl.ds(start + 8 * j, 8), moved))
                merged = [
                    (d, rows, jnp.where(inside, moved, strips[d, rows, :]))
                    for d, rows, moved in merged
                ]
                for d, rows, value in merged:
                    strips[d, rows, :] = value

        @pl.when((ids[q] >= 0) & (home[places + q] == 1))
        def _():
            store(q).start()

        return carry

    lax.fori_loop(0, places, patch, 0)
    for q in range(places):

        @pl.when((ids[q] >= 0) & (home[places + q] == 1))
        def _(q=q):
            store(q).wait()


def in_hbm(value):
    return pltpu.with_memory_space_constraint(value, pltpu.HBM)


def in_vmem(value):
    return pltpu.with_memory_space_constraint(value, pltpu.VMEM)


def local(coarse_pop, fine_pop, fine_block):
    width_x, width_y = coarse_pop.shape[1:]
    blocks_x = width_x // COARSE_EDGE
    blocks_y = width_y // COARSE_EDGE
    count_x = lax.axis_size("gx")
    count_y = lax.axis_size("gy")
    columns = blocks_y * count_y
    places = count_x * CAP
    slots = fine_block.shape[0]
    cells = FINE_EDGE * FINE_EDGE
    wide = width_x + LANES
    smem = pl.BlockSpec(memory_space=pltpu.SMEM)
    vmem = pl.BlockSpec(memory_space=pltpu.VMEM)
    hbm = pl.BlockSpec(memory_space=pltpu.HBM)
    sds = jax.ShapeDtypeStruct

    def held(*shape):
        return pltpu.VMEM(shape, F32)

    ask, slot = pl.pallas_call(
        functools.partial(ask_kernel, columns, blocks_x, blocks_y, count_x),
        out_shape=(held(count_x, 24, LANES), sds((2 * places,), jnp.int32)),
        in_specs=[hbm, hbm],
        out_specs=(vmem, smem),
        scratch_shapes=[
            pltpu.SMEM((slots,), jnp.int32),
            pltpu.SMEM((places,), jnp.int32),
            pltpu.SMEM((count_x,), jnp.int32),
            held(2, 9, 8, LANES),
            held(2, 24, LANES),
            pltpu.SemaphoreType.DMA((3,)),
        ],
        name="ask",
        compiler_params=GRANT,
    )(in_hbm(fine_block), in_hbm(coarse_pop))
    asked = in_vmem(lax.all_to_all(ask, "gx", split_axis=0, concat_axis=0, tiled=True))
    forward_y = [(i, (i + 1) % count_y) for i in range(count_y)]
    backward_y = [(target, source) for source, target in forward_y]

    def columns_round(packed):
        sets, to_high, to_low = packed
        from_low = lax.ppermute(to_high, "gy", forward_y)
        from_high = lax.ppermute(to_low, "gy", backward_y)
        return [in_vmem(value) for value in (sets, from_low, from_high)]

    main = columns_round(
        pl.pallas_call(
            pack_kernel,
            out_shape=(held(3, 9, 8, width_x), held(24, width_x), held(24, width_x)),
            in_specs=[hbm],
            out_specs=(vmem, vmem, vmem),
            scratch_shapes=[
                held(9, width_x, LANES),
                held(2, width_x, LANES),
                pltpu.SemaphoreType.DMA((9,)),
            ],
            name="pack",
        compiler_params=GRANT,
        )(in_hbm(coarse_pop))
    )
    corner = columns_round(
        pl.pallas_call(
            functools.partial(corner_kernel, count_x),
            out_shape=(held(3, 9, 8, LANES), held(24, LANES), held(24, LANES)),
            in_specs=[vmem],
            out_specs=(vmem, vmem, vmem),
            scratch_shapes=[held(2, 9, 8, LANES), held(2, LANES, LANES)],
            name="corner",
        compiler_params=GRANT,
        )(asked)
    )
    fine_turned = jnp.transpose(fine_pop, (1, 0, 2))
    post = pl.pallas_call(
        start_kernel,
        out_shape=held(9, places, cells),
        in_specs=[smem, hbm],
        out_specs=vmem,
        scratch_shapes=[pltpu.SemaphoreType.DMA((places,))],
        name="start",
        compiler_params=GRANT,
    )(slot, in_hbm(fine_turned))
    message, inject, wanted = pl.pallas_call(
        functools.partial(ghost_kernel, count_x, count_y),
        out_shape=(
            held(places, 8, LANES),
            pltpu.HBM((width_x, LANES), F32),
            sds((places,), jnp.int32),
        ),
        in_specs=[hbm] + [vmem] * 7,
        out_specs=(vmem, hbm, smem),
        scratch_shapes=[
            pltpu.SMEM((count_x, 8, LANES), F32),
            held(9, blocks_x, 8, LANES),
            held(9, blocks_x, 8, LANES),
            held(LANES, wide),
            held(wide, LANES),
            held(9, 8, wide),
            held(3, 9, 8, wide),
            held(9, 8, wide),
            held(2, 3, 8, wide),
            held(2, blocks_x, 8, LANES),
            held(6, 9, blocks_x, 2 * LANES),
            held(6, 9, blocks_x, 2 * LANES),
            held(9, 8, 2 * LANES),
            held(2, 3, 2, blocks_x, 2 * LANES),
            held(6, blocks_x, LANES),
            held(2, 2, blocks_y, blocks_x, LANES),
            held(width_x, LANES),
            pltpu.SemaphoreType.DMA((4,)),
        ],
        name="ghost",
        compiler_params=GRANT,
    )(in_hbm(coarse_pop.reshape(9, blocks_x, COARSE_EDGE, width_y)), asked, *main, *corner)
    ghosts = in_vmem(lax.all_to_all(message, "gx", split_axis=0, concat_axis=0, tiled=True))
    fine_out, back = pl.pallas_call(
        fine_kernel,
        out_shape=(pltpu.HBM((9, slots, cells), F32), held(places, 72, LANES)),
        in_specs=[smem, vmem, vmem],
        out_specs=(hbm, vmem),
        scratch_shapes=[
            held(9, places, cells),
            held(9, 8, cells),
            held(9, 64, LANES),
            held(9, 8, 8, LANES),
            held(9, 8, 8, LANES),
            pltpu.SemaphoreType.DMA((places,)),
        ],
        name="fine",
        compiler_params=GRANT,
    )(slot, in_vmem(post), ghosts)
    returned = in_vmem(lax.all_to_all(back, "gx", split_axis=0, concat_axis=0, tiled=True))
    base, strips, home = pl.pallas_call(
        functools.partial(coarse_kernel, count_x, count_y),
        out_shape=(
            pltpu.HBM((9, width_x, width_y), F32),
            held(9, COARSE_EDGE * places, width_y),
            sds((2 * places,), jnp.int32),
        ),
        in_specs=[hbm, vmem, hbm, vmem, smem],
        out_specs=(hbm, vmem, smem),
        scratch_shapes=[
            held(width_x, LANES),
            held(9, width_x, LANES),
            held(9, width_x + 16, LANES),
            pltpu.SemaphoreType.DMA((5,)),
            pltpu.SemaphoreType.DMA((4,)),
            pltpu.SemaphoreType.DMA((places,)),
        ],
        name="coarse",
        compiler_params=GRANT,
    )(in_hbm(coarse_pop), asked, in_hbm(inject), in_vmem(back), wanted)
    _, coarse_out = pl.pallas_call(
        functools.partial(patch_kernel, blocks_y),
        out_shape=(
            held(9, COARSE_EDGE * places, width_y),
            pltpu.HBM((9, width_x, width_y), F32),
        ),
        in_specs=[smem, smem, hbm, vmem, vmem],
        out_specs=(vmem, hbm),
        scratch_shapes=[pltpu.SemaphoreType.DMA((places,))],
        input_output_aliases={2: 1, 3: 0},
        name="patch",
        compiler_params=GRANT,
    )(wanted, home, in_hbm(base), in_vmem(strips), returned)
    return (coarse_out, jnp.transpose(fine_out, (1, 0, 2)))


def solution(mesh):
    return jax.shard_map(
        local,
        mesh=mesh,
        in_specs=(P(None, "gx", "gy"), P(("gx", "gy"), None, None), P(("gx", "gy"))),
        out_specs=(P(None, "gx", "gy"), P(("gx", "gy"), None, None)),
        check_vma=False,
    )
```

```python
import functools

import jax
import jax.numpy as jnp
from jax import lax
from jax.experimental import pallas as pl
from jax.experimental.pallas import tpu as pltpu
from jax.sharding import PartitionSpec as P

FINE_EDGE = 64
COARSE_EDGE = 32
CAP = 2
LANES = 128
WINDOW = 42

along_x = [0, 1, 0, -1, 0, 1, -1, -1, 1]
along_y = [0, 0, 1, 0, -1, 1, 1, -1, -1]
opposite = [0, 3, 4, 1, 2, 7, 8, 5, 6]
UP = (1, 5, 8)
DOWN = (3, 6, 7)
LEFT = (2, 5, 6)
RIGHT = (4, 8, 7)
ORDER = (0, 1, -1)

F32 = jnp.float32
GRANT = pltpu.CompilerParams(vmem_limit_bytes=24 << 20)


def rates_of(relax_time, factor=1.0):
    return tuple((1.0 - factor) + factor * rate for rate in (1.4, 1.4, 1.2, 1.0 / relax_time))


COARSE = rates_of(0.65)
FINE = rates_of(0.8)
GHOST = rates_of(0.8, 0.8 / 1.3)
COALESCE = (1.0 - 1.3 / 0.8,) * 4


def relax(p, rates, which=tuple(range(9))):
    s_e, s_p, s_q, s_n = rates
    p0, p1, p2, p3, p4, p5, p6, p7, p8 = p
    s1, d1 = p1 + p3, p1 - p3
    s2, d2 = p2 + p4, p2 - p4
    s5, d5 = p5 + p7, p5 - p7
    s6, d6 = p6 + p8, p6 - p8
    axial, diagonal = s1 + s2, s5 + s6
    rho = p0 + axial + diagonal
    dq, sq = d5 - d6, d5 + d6
    jx, jy = d1 + dq, d2 + sq
    inv = 1.0 / rho
    xx, yy = jx * jx, jy * jy
    square = 3.0 * ((xx + yy) * inv)
    e = (axial - 2.0 * p0) + 4.0 * diagonal - square
    eps = 3.0 * (p0 - axial) + square
    a = (s_e / 36.0) * e
    b = (s_p / 36.0) * eps
    c = (s_q / 12.0) * (2.0 * dq - d1)
    d = (s_q / 12.0) * (2.0 * sq - d2)
    f = (s_n / 4.0) * ((s1 - s2) - (xx - yy) * inv)
    g = (s_n / 4.0) * ((s5 - s6) - (jx * jy) * inv)
    out = {}
    t = a + 2.0 * b
    w = 2.0 * a + b
    if 0 in which:
        out[0] = p0 + 4.0 * (a - b)
    if 1 in which:
        out[1] = p1 + ((t - f) + 2.0 * c)
    if 3 in which:
        out[3] = p3 + ((t - f) - 2.0 * c)
    if 2 in which:
        out[2] = p2 + ((t + f) + 2.0 * d)
    if 4 in which:
        out[4] = p4 + ((t + f) - 2.0 * d)
    if 5 in which:
        out[5] = p5 - ((w + g) + (c + d))
    if 7 in which:
        out[7] = p7 - ((w + g) - (c + d))
    if 6 in which:
        out[6] = p6 - ((w - g) - (c - d))
    if 8 in which:
        out[8] = p8 - ((w - g) + (c - d))
    return out


def lane_of(shape):
    return lax.broadcasted_iota(jnp.int32, shape, 1)


def row_of(shape):
    return lax.broadcasted_iota(jnp.int32, shape, 0)


def take_lanes(value, index):
    return jnp.take_along_axis(value, index, axis=1, mode="promise_in_bounds")


def ask_kernel(
    columns, blocks_x, blocks_y, count_x, block_hbm, coarse, ask, slot_ref, block_ref, id_ref, seen_ref, edge, rows, sems
):
    width = coarse.shape[1]
    places = count_x * CAP
    copies = [
        pltpu.make_async_copy(coarse.at[:, pl.ds(at, 8), :], edge.at[k], sems.at[k])
        for k, at in enumerate((0, width - 8))
    ]
    blocks = pltpu.make_async_copy(block_hbm, block_ref, sems.at[2])
    blocks.start()
    for copy in copies:
        copy.start()
    for place in range(places):
        id_ref[place] = -1
        slot_ref[place] = -1
        slot_ref[places + place] = 0
    for owner in range(count_x):
        seen_ref[owner] = 0
    blocks.wait()
    for slot in range(block_ref.shape[0]):
        block = block_ref[slot]
        column = lax.div(block, columns)
        row = block - column * columns
        owner = lax.div(column, blocks_x)
        rank = seen_ref[owner]
        seen_ref[owner] = rank + 1
        place = owner * CAP + rank
        id_ref[place] = (column - owner * blocks_x) * blocks_y + lax.rem(row, blocks_y)
        slot_ref[place] = slot
        slot_ref[places + place] = jnp.where(row == 0, 1, 0) + jnp.where(row == columns - 1, 2, 0)
    rows[...] = jnp.full(rows.shape, 0.1, F32)
    for copy in copies:
        copy.wait()
    for d in range(9):
        rows[0, 2 * d : 2 * d + 2, :] = edge[0, d, 0:2, :]
        rows[1, 2 * d : 2 * d + 2, :] = edge[1, d, 6:8, :]
    shape = rows.shape[1:]
    lane, row = lane_of(shape), row_of(shape)
    after = lax.rem(lax.axis_index("gx") + 1, count_x)
    for owner in range(count_x):
        number = jnp.zeros(shape, jnp.int32)
        for rank in range(CAP):
            number = jnp.where(lane == rank, id_ref[owner * CAP + rank], number)
        value = jnp.where(after == owner, rows[1], rows[0])
        ask[owner] = jnp.where(row == 18, number.astype(F32), value)


def columns_of(shape):
    lane = lane_of(shape)
    key = lax.rem(lane, 24)
    col = 32 * (key & 3) + (key >> 3) + jnp.where((key & 4) == 0, -2, 31)
    return lane, col & (LANES - 1)


def place_columns(z, d, start, count, value):
    group, part = divmod(d, 5)
    lane, col = columns_of((count, LANES))
    got = take_lanes(value, col)
    if part:
        inside = (lane >= 24 * part) & (lane < 24 * part + 24)
        got = jnp.where(inside, got, z[group, pl.ds(start, count), :])
    z[group, pl.ds(start, count), :] = got


def turn_columns(z, sets, to_high, to_low):
    to_high[...] = jnp.full(to_high.shape, 0.1, F32)
    to_low[...] = jnp.full(to_low.shape, 0.1, F32)
    for group in range(2):
        for t in range(z.shape[1] // LANES):
            lanes = pl.ds(t * LANES, LANES)
            turned = z[group, t * LANES : (t + 1) * LANES, :].T
            for part in range(5 - group):
                d = 5 * group + part
                for s in range(3):
                    sets[s, d, :, lanes] = turned[24 * part + 8 * s : 24 * part + 8 * s + 8]
                base = 24 * part
                to_high[2 * d : 2 * d + 1, lanes] = turned[base : base + 1]
                to_high[2 * d + 1 : 2 * d + 2, lanes] = turned[base + 8 : base + 9]
                to_low[2 * d : 2 * d + 1, lanes] = turned[base + 15 : base + 16]
                to_low[2 * d + 1 : 2 * d + 2, lanes] = turned[base + 23 : base + 24]


def pack_kernel(coarse, sets, to_high, to_low, buf, z, sems):
    width = coarse.shape[1]
    copies = [pltpu.make_async_copy(coarse.at[d], buf.at[d], sems.at[d]) for d in range(9)]
    for copy in copies:
        copy.start()
    rows = 512
    for d in range(9):
        copies[d].wait()

        def chunk(k, carry, d=d):
            start = pl.multiple_of(k * rows, rows)
            place_columns(z, d, start, rows, buf[d, pl.ds(start, rows), :])
            return carry

        lax.fori_loop(0, width // rows, chunk, 0)
    turn_columns(z, sets, to_high, to_low)


def neighbours(count_x):
    index = lax.axis_index("gx")
    return lax.rem(index + count_x - 1, count_x), lax.rem(index + 1, count_x)


def corner_kernel(count_x, asked, sets, to_high, to_low, ext, z):
    before, after = neighbours(count_x)
    ext[...] = jnp.full(ext.shape, 0.1, F32)
    z[...] = jnp.full(z.shape, 0.1, F32)
    for d in range(9):
        ext[0, d, 0:2, :] = asked[after, 2 * d : 2 * d + 2, :]
        ext[1, d, 6:8, :] = asked[before, 2 * d : 2 * d + 2, :]
    for d in range(9):
        place_columns(z, d, 0, 8, ext[0, d])
        place_columns(z, d, LANES - 8, 8, ext[1, d])
    turn_columns(z, sets, to_high, to_low)


def window(parts, j, off):
    lane = lane_of((8, LANES))
    before, value, after = parts
    shift = (WINDOW * j - off + 1) % LANES

    def move(part):
        return pltpu.roll(part, shift, 1) if shift else part

    value = move(value)
    if off == 0:
        value = jnp.where(lane == WINDOW * j, move(before), value)
    if off == LANES - COARSE_EDGE:
        value = jnp.where(lane == WINDOW * j + COARSE_EDGE + 1, move(after), value)
    return value


def join(parts):
    lane = lane_of((8, LANES))
    first, second, third = parts
    return jnp.where(lane < WINDOW, first, jnp.where(lane < 2 * WINDOW, second, third))


def ghost_kernel(
    count_x,
    count_y,
    coarse,
    asked,
    sets_main,
    low_main,
    high_main,
    sets_ext,
    low_ext,
    high_ext,
    message,
    inject_hbm,
    ids,
    numbers,
    first,
    last,
    turn,
    mt,
    old_t,
    post_t,
    new_t,
    g_t,
    pack_t,
    raw_r,
    post_r,
    new_r,
    g_r,
    far,
    pack_r,
    inject,
    sems,
):
    blocks_x = coarse.shape[1]
    width = blocks_x * COARSE_EDGE
    wide = width + LANES
    tiles = wide // LANES
    width_y = LANES
    blocks_y = width_y // COARSE_EDGE
    total_y = width_y * count_y
    base_y = lax.axis_index("gy") * width_y
    copy_first = pltpu.make_async_copy(coarse.at[:, :, pl.ds(0, 8), :], first, sems.at[0])
    copy_last = pltpu.make_async_copy(
        coarse.at[:, :, pl.ds(COARSE_EDGE - 8, 8), :], last, sems.at[1]
    )
    copy_first.start()
    copy_last.start()
    copy_ids = pltpu.make_async_copy(asked.at[:, pl.ds(16, 8), :], numbers, sems.at[2])
    copy_ids.start()
    index_before, index_after = neighbours(count_x)

    turn[...] = jnp.full(turn.shape, 0.1, F32)
    for d in range(9):
        at = (4 * d - 2) % LANES
        turn[4 * d : 4 * d + 2, 0:width] = high_main[2 * d : 2 * d + 2, :]
        turn[4 * d : 4 * d + 2, width:] = high_ext[2 * d : 2 * d + 2, :]
        turn[at : at + 2, 0:width] = low_main[2 * d : 2 * d + 2, :]
        turn[at : at + 2, width:] = low_ext[2 * d : 2 * d + 2, :]
    for t in range(tiles):
        mt[t * LANES : (t + 1) * LANES, :] = turn[:, t * LANES : (t + 1) * LANES].T
    tile = (8, LANES)
    row8 = row_of(tile)

    def collide_tile(sets, from_low, from_high, at, lanes):
        for s in range(3):
            p = []
            for d in range(9):
                value = sets[s, d, :, at]
                if s < 2:
                    value = jnp.where(row8 == 0, from_low[2 * d + s : 2 * d + s + 1, at], value)
                if s > 0:
                    value = jnp.where(row8 == 7, from_high[2 * d + s - 1 : 2 * d + s, at], value)
                if s == 1:
                    old_t[d, :, lanes] = value
                p.append(value)
            out = relax(p, COARSE)
            for d in range(9):
                post_t[s, d, :, lanes] = out[d]

    def collide_t(t, carry):
        lanes = pl.ds(pl.multiple_of(t * LANES, LANES), LANES)
        collide_tile(sets_main, low_main, high_main, lanes, lanes)
        return carry

    lax.fori_loop(0, tiles - 1, collide_t, 0)
    collide_tile(sets_ext, low_ext, high_ext, pl.ds(0, LANES), pl.ds(width, LANES))
    turn[...] = jnp.zeros(turn.shape, F32)
    row_t = row_of((8, wide))
    coord_t = base_y + 32 * (row_t & 3) + jnp.where(row_t < 4, -1, 32)
    for d in range(9):
        source = post_t[{1: 0, 0: 1, -1: 2}[along_y[d]], d]
        if along_x[d]:
            source = pltpu.roll(source, along_x[d] % wide, 1)
        back = coord_t - along_y[d]
        beyond = (back < 0) | (back >= total_y)
        new_t[d] = jnp.where(beyond, post_t[1, opposite[d]], source)
    for j in range(3):
        for side, (d, row) in enumerate(((LEFT[j], 0), (RIGHT[j], 7))):
            source = post_t[1, d]
            if along_x[d]:
                source = pltpu.roll(source, along_x[d] % wide, 1)
            turn[3 * side + j : 3 * side + j + 1, :] = source[row : row + 1, :]
    for t in range(width // LANES):
        inject[t * LANES : (t + 1) * LANES, :] = turn[:, t * LANES : (t + 1) * LANES].T
    copy_inject = pltpu.make_async_copy(inject, inject_hbm, sems.at[3])
    copy_inject.start()

    def ghosts_t(t, carry):
        lanes = pl.ds(pl.multiple_of(t * LANES, LANES), LANES)
        old = [old_t[d, :, lanes] for d in range(9)]
        mean = [0.5 * (old[d] + new_t[d, :, lanes]) for d in range(9)]
        for sub, p in enumerate((old, mean)):
            out = relax(p, GHOST, LEFT + RIGHT)
            for j in range(3):
                g_t[sub, j, :, lanes] = jnp.where(row8 < 4, out[LEFT[j]], out[RIGHT[j]])
        return carry

    lax.fori_loop(0, tiles, ghosts_t, 0)
    for sub in range(2):
        for bx in range(blocks_x):
            t, off = divmod(COARSE_EDGE * bx, LANES)
            near = [(t + step) % tiles for step in (-1, 0, 1)]
            got = []
            for j in range(3):
                parts = [g_t[sub, j, :, LANES * k : LANES * (k + 1)] for k in near]
                got.append(window(parts, j, off))
            pack_t[sub, bx] = join(got)

    plane = (blocks_x, LANES)
    rows_b = row_of(plane)

    def lower(value, row):
        return jnp.where(rows_b == 0, row, pltpu.roll(value, 1, 0))

    def upper(value, row):
        return jnp.where(rows_b == blocks_x - 1, row, pltpu.roll(value, blocks_x - 1, 0))

    def every(ref, start, step):
        return ref[pl.ds(start, blocks_x, stride=step), :]

    side_rows = [every(mt, c, COARSE_EDGE) for c in (0, 1, COARSE_EDGE - 2, COARSE_EDGE - 1)]
    m0, m1, m30, m31 = side_rows
    extra = (
        lower(m30, mt[wide - 2 : wide - 1, :]),
        lower(m31, mt[wide - 1 : wide, :]),
        m0,
        m31,
        upper(m0, mt[width : width + 1, :]),
        upper(m1, mt[width + 1 : width + 2, :]),
    )
    copy_first.wait()
    copy_last.wait()
    first2 = first.reshape(9 * blocks_x * 8, LANES)
    last2 = last.reshape(9 * blocks_x * 8, LANES)
    for k in range(6):
        far[k] = extra[k]

    def raw_rows(d, carry):
        at = d * (blocks_x * 8)
        a0, a1 = every(first2, at, 8), every(first2, at + 1, 8)
        b30, b31 = every(last2, at + 6, 8), every(last2, at + 7, 8)
        main = (
            lower(b30, asked[index_before, pl.ds(2 * d, 1), :]),
            lower(b31, asked[index_before, pl.ds(2 * d + 1, 1), :]),
            a0,
            b31,
            upper(a0, asked[index_after, pl.ds(2 * d, 1), :]),
            upper(a1, asked[index_after, pl.ds(2 * d + 1, 1), :]),
        )
        for k in range(6):
            raw_r[k, d, :, 0:LANES] = main[k]
            raw_r[k, d, :, LANES:] = pltpu.roll(far[k], lax.rem(LANES - 4 * d, LANES), 1)
        return carry

    lax.fori_loop(0, 9, raw_rows, 0)

    def collide_r(k, carry):
        rows = pl.ds(pl.multiple_of(k * 8, 8), 8)
        for s in range(6):
            for half in range(2):
                lanes = pl.ds(half * LANES, LANES)
                out = relax([raw_r[s, d, rows, lanes] for d in range(9)], COARSE)
                for d in range(9):
                    post_r[s, d, rows, lanes] = out[d]
        return carry

    lax.fori_loop(0, blocks_x // 8, collide_r, 0)
    double = (8, 2 * LANES)
    lane_r = lane_of(double)
    coord_r = base_y + jnp.where(lane_r < LANES + 2, lane_r, lane_r - 2 * LANES)

    def ghosts_r(k, carry):
        rows = pl.ds(pl.multiple_of(k * 8, 8), 8)
        for side in range(2):
            for d in range(9):
                source = post_r[3 * side + {1: 0, 0: 1, -1: 2}[along_x[d]], d, rows, :]
                if along_y[d]:
                    source = pltpu.roll(source, along_y[d] % (2 * LANES), 1)
                back = coord_r - along_y[d]
                beyond = (back < 0) | (back >= total_y)
                new_r[d] = jnp.where(beyond, post_r[3 * side + 1, opposite[d], rows, :], source)
            which = (UP, DOWN)[side]
            for half in range(2):
                lanes = pl.ds(half * LANES, LANES)
                old = [raw_r[3 * side + 1, d, rows, lanes] for d in range(9)]
                mean = [0.5 * (old[d] + new_r[d, :, lanes]) for d in range(9)]
                for sub, p in enumerate((old, mean)):
                    out = relax(p, GHOST, which)
                    for j in range(3):
                        g_r[side, j, sub, rows, lanes] = out[which[j]]
        return carry

    lax.fori_loop(0, blocks_x // 8, ghosts_r, 0)

    def windows_r(k, carry):
        rows = pl.ds(pl.multiple_of(k * 8, 8), 8)
        for side in range(2):
            for sub in range(2):
                for by in range(blocks_y):
                    got = []
                    for j in range(3):
                        one = g_r[side, j, sub, rows, 0:LANES]
                        two = g_r[side, j, sub, rows, LANES:]
                        got.append(window((two, one, two), j, COARSE_EDGE * by))
                    pack_r[side, sub, by, rows, :] = join(got)
        return carry

    lax.fori_loop(0, blocks_x // 8, windows_r, 0)

    copy_ids.wait()
    for q in range(message.shape[0]):
        ids[q] = numbers[q // CAP, 2, q % CAP].astype(jnp.int32)

    def pick(q, carry):
        block = jnp.maximum(ids[q], 0)
        bx = lax.div(block, blocks_y)
        by = block - bx * blocks_y
        for sub in range(2):
            for side in range(2):
                row = 4 * sub + side
                message[q, row : row + 1, :] = pack_r[side, sub, by, pl.ds(bx, 1), :]
                row = 4 * sub + 2 + side
                message[q, row : row + 1, :] = pack_t[sub, bx, pl.ds(4 * side + by, 1), :]
        return carry

    lax.fori_loop(0, message.shape[0], pick, 0)
    copy_inject.wait()


def start_kernel(slot, fine, post, sem):
    places = post.shape[1]
    copies = []
    for q in range(places):
        source = fine.at[:, pl.ds(jnp.maximum(slot[q], 0), 1), :]
        copy = pltpu.make_async_copy(source, post.at[:, pl.ds(q, 1), :], sem.at[q])
        copy.start()
        copies.append(copy)
    for copy in copies:
        copy.wait()

    def body(k, carry):
        lanes = pl.ds(pl.multiple_of(k * LANES, LANES), LANES)
        for h in range(places // 8):
            rows = pl.ds(8 * h, 8)
            out = relax([post[d, rows, lanes] for d in range(9)], FINE)
            for d in range(9):
                post[d, rows, lanes] = out[d]
        return carry

    lax.fori_loop(0, post.shape[2] // LANES, body, 0, unroll=2)


def fine_kernel(
    slot, post, ghosts, fine, back_hbm, result, back, post_two, line, mean, swapped, sem, back_sem
):
    places = post.shape[1]
    tiles = post.shape[2] // LANES
    tile = (8, LANES)
    lane, row = lane_of(tile), row_of(tile)
    low_half = lane < 64
    at_low = (lane & 63) == 0
    at_high = (lane & 63) == 63
    ghosts2 = ghosts.reshape(places * 8, LANES)
    over = [WINDOW * j + 1 + (((lane & 63) - c) >> 1) for j, c in enumerate(ORDER)]
    even = (lane & 1) == 0
    turn_back = jnp.where(even, lane, (lane - 63) & (LANES - 1))
    cell = (turn_back & 63) + (turn_back >> 6)
    along = [(WINDOW * j + 1 + ((cell - c) >> 1)) & (LANES - 1) for j, c in enumerate(ORDER)]
    squeeze = 64 * ((lane >> 5) & 1) + 2 * (lane & 31) + (lane >> 6)

    def copy(q):
        target = fine.at[:, pl.ds(jnp.maximum(slot[q], 0), 1), :]
        return pltpu.make_async_copy(result.at[:, pl.ds(q, 1), :], target, sem.at[q])

    def send(h):
        part = pl.ds(8 * h, 8)
        return pltpu.make_async_copy(back.at[part], back_hbm.at[part], back_sem.at[h])

    def half(h, carry):
        rows = pl.ds(pl.multiple_of(8 * h, 8), 8)
        wall = jnp.zeros(tile, jnp.int32)
        for r in range(8):
            wall = jnp.where(row == r, slot[places + 8 * h + r], wall)
        wall_low = at_low & ((wall & 1) != 0)
        wall_high = at_high & ((wall & 2) != 0)

        def substep(sub, source, emit):
            border = [
                ghosts2[pl.ds(h * 64 + 4 * sub + side, 8, stride=8), :] for side in range(4)
            ]
            up = [take_lanes(border[0], over[j]) for j in range(3)]
            down = [take_lanes(border[1], over[j]) for j in range(3)]
            beside = [
                jnp.where(even, take_lanes(border[2], along[j]), take_lanes(border[3], along[j]))
                for j in range(3)
            ]

            def load(d, k):
                return source[d, rows, k * LANES : (k + 1) * LANES]

            def crossed(d, k):
                if k < 0:
                    return up[UP.index(d)]
                if k == tiles:
                    return down[DOWN.index(d)]
                return pltpu.roll(load(d, k), (64 + along_y[d]) % LANES, 1)

            before = {d: crossed(d, -1) for d in UP}
            now = {d: crossed(d, 0) for d in DOWN}
            for k in range(tiles):
                ghosts_k = [
                    pltpu.roll(value, (-2 * k) % LANES, 1) if k else value for value in beside
                ]
                out = []
                for d in range(9):
                    if along_x[d] > 0:
                        turned = crossed(d, k)
                        value = jnp.where(low_half, before[d], turned)
                        before[d] = turned
                    elif along_x[d] < 0:
                        turned = crossed(d, k + 1)
                        value = jnp.where(low_half, now[d], turned)
                        now[d] = turned
                    else:
                        value = load(d, k)
                        if along_y[d]:
                            value = pltpu.roll(value, along_y[d] % LANES, 1)
                    if along_y[d] > 0:
                        value = jnp.where(at_low, ghosts_k[LEFT.index(d)], value)
                        value = jnp.where(wall_low, load(opposite[d], k), value)
                    elif along_y[d] < 0:
                        value = jnp.where(at_high, ghosts_k[RIGHT.index(d)], value)
                        value = jnp.where(wall_high, load(opposite[d], k), value)
                    out.append(value)
                emit(k, out)

        def emit_first(k, p):
            out = relax(p, FINE)
            for d in range(9):
                post_two[d, :, k * LANES : (k + 1) * LANES] = out[d]

        def emit_second(k, p):
            for d in range(9):
                result[d, rows, k * LANES : (k + 1) * LANES] = p[d]

        post_rows = post
        substep(0, post_rows, emit_first)
        substep(1, _Rows(post_two), emit_second)
        for r in range(8):

            @pl.when(slot[8 * h + r] >= 0)
            def _(r=r):
                copy(8 * h + r).start()

        def tile_of(ref, d, k):
            return ref[d, rows, pl.ds(pl.multiple_of(k * LANES, LANES), LANES)]

        def pair_up(step, carry):
            for u in range(4):
                i = 4 * step + u
                for d in range(9):
                    pairs = []
                    for m in range(2):
                        one = tile_of(result, d, i + 16 * m)
                        two = tile_of(result, d, i + 16 * m + 8)
                        other = pltpu.roll(jnp.where(low_half, two, one), 64, 1)
                        pairs.append(jnp.where(low_half, one, two) + other)
                    mean[d, i] = jnp.where(even, pairs[0], pairs[1])
                    swapped[d, i] = jnp.where(even, pairs[1], pairs[0])
            return carry

        def merge(step, carry):
            for u in range(4):
                i = 4 * step + u
                total = []
                for d in range(9):
                    moved = swapped[d, i]
                    moved = jnp.where(even, pltpu.roll(moved, 127, 1), pltpu.roll(moved, 1, 1))
                    total.append(0.25 * (mean[d, i] + moved))
                out = relax(total, COALESCE)
                for d in range(9):
                    mean[d, i] = out[d]
            return carry

        def compress(step, carry):
            for u in range(4):
                i = 4 * step + u
                for d in range(9):
                    at = pl.ds(pl.multiple_of(i * 8, 8), 8)
                    line[d, at, :] = take_lanes(mean[d, i], squeeze)
            return carry

        lax.fori_loop(0, 2, pair_up, 0)
        lax.fori_loop(0, 2, merge, 0)
        lax.fori_loop(0, 2, compress, 0)
        for d in range(9):
            flat = line.at[d]
            for q in range(8):
                back[8 * h + q, d * 8 : d * 8 + 8, :] = flat[pl.ds(q, 8, stride=8), :]
        send(h).start()
        return carry

    lax.fori_loop(0, places // 8, half, 0)
    for h in range(places // 8):
        send(h).wait()
    for q in range(places):

        @pl.when(slot[q] >= 0)
        def _(q=q):
            copy(q).wait()


class _Rows:
    def __init__(self, ref):
        self.ref = ref

    def __getitem__(self, key):
        d, _, lanes = key
        return self.ref[d, :, lanes]


def coarse_kernel(
    count_x, count_y, coarse, asked, inject_hbm, after, ids, base, strips, home, inject, new, post, load, save, cut
):
    width = coarse.shape[1]
    places = ids.shape[0]
    blocks_y = coarse.shape[2] // COARSE_EDGE
    tile = (8, LANES)
    lane = lane_of(tile)
    parts = 4
    size = width // parts
    copies = [
        pltpu.make_async_copy(
            coarse.at[:, pl.ds(k * size, size), :],
            post.at[:, pl.ds(8 + k * size, size), :],
            load.at[k],
        )
        for k in range(parts)
    ]
    for copy in copies:
        copy.start()
    copy_inject = pltpu.make_async_copy(inject_hbm, inject, load.at[parts])
    copy_inject.start()
    before, following = neighbours(count_x)
    out = relax([asked[before, 2 * d + 1 : 2 * d + 2, :] for d in range(9)], COARSE)
    for d in range(9):
        post[d, 7:8, :] = out[d]
    out = relax([asked[following, 2 * d : 2 * d + 1, :] for d in range(9)], COARSE)
    for d in range(9):
        post[d, width + 8 : width + 9, :] = out[d]

    def collide(k, carry):
        rows = pl.ds(pl.multiple_of(8 + 8 * k, 8), 8)
        out = relax([post[d, rows, :] for d in range(9)], COARSE)
        for d in range(9):
            post[d, rows, :] = out[d]
        return carry

    index_y = lax.axis_index("gy")
    wall_low = (lane == 0) & (index_y == 0)
    wall_high = (lane == LANES - 1) & (index_y == count_y - 1)

    def stream(k, carry):
        start = pl.multiple_of(8 * k, 8)
        edge = inject[pl.ds(start, 8), :]
        for d in range(9):
            value = post[d, pl.ds(start + (8 - along_x[d]), 8), :]
            if along_y[d]:
                value = pltpu.roll(value, along_y[d] % LANES, 1)
                same = post[opposite[d], pl.ds(start + 8, 8), :]
                if along_y[d] > 0:
                    j = LEFT.index(d)
                    value = jnp.where(lane == 0, pltpu.roll(edge, (-j) % LANES, 1), value)
                    value = jnp.where(wall_low, same, value)
                else:
                    j = RIGHT.index(d)
                    moved = pltpu.roll(edge, LANES - 4 - j, 1)
                    value = jnp.where(lane == LANES - 1, moved, value)
                    value = jnp.where(wall_high, same, value)
            new[d, pl.ds(start, 8), :] = value
        return carry

    copy_inject.wait()
    copies[0].wait()
    lax.fori_loop(0, size // 8, collide, 0, unroll=4)
    stores = []
    for k in range(parts):
        if k + 1 < parts:
            copies[k + 1].wait()
            lax.fori_loop((k + 1) * size // 8, (k + 2) * size // 8, collide, 0, unroll=4)
        lax.fori_loop(k * size // 8, (k + 1) * size // 8, stream, 0, unroll=4)
        rows = pl.ds(k * size, size)
        store = pltpu.make_async_copy(new.at[:, rows, :], base.at[:, rows, :], save.at[k])
        store.start()
        stores.append(store)

    def column(q):
        return lax.div(jnp.maximum(ids[q], 0), blocks_y)

    def strip(q):
        rows = pl.ds(pl.multiple_of(COARSE_EDGE * column(q), COARSE_EDGE), COARSE_EDGE)
        return pltpu.make_async_copy(
            new.at[:, rows, :], strips.at[:, pl.ds(COARSE_EDGE * q, COARSE_EDGE), :], cut.at[q]
        )

    for q in range(places):

        @pl.when(ids[q] >= 0)
        def _(q=q):
            strip(q).start()

    for q in range(places):
        first, last = jnp.int32(q), jnp.int32(1)
        for other in reversed(range(places)):
            if other != q:
                same = (ids[q] >= 0) & (ids[other] >= 0) & (column(q) == column(other))
                if other < q:
                    first = jnp.where(same, other, first)
                else:
                    last = jnp.where(same, 0, last)
        home[q] = first
        home[places + q] = last
    for store in stores:
        store.wait()
    for q in range(places):

        @pl.when(ids[q] >= 0)
        def _(q=q):
            strip(q).wait()


def patch_kernel(blocks_y, ids, home, base, strips_in, back, strips, out, save):
    lane = lane_of((8, LANES))
    places = ids.shape[0]

    def store(q):
        bx = lax.div(jnp.maximum(ids[q], 0), blocks_y)
        rows = pl.ds(pl.multiple_of(COARSE_EDGE * bx, COARSE_EDGE), COARSE_EDGE)
        own = pl.ds(pl.multiple_of(COARSE_EDGE * home[q], COARSE_EDGE), COARSE_EDGE)
        return pltpu.make_async_copy(strips.at[:, own, :], out.at[:, rows, :], save.at[q])

    def patch(q, carry):
        @pl.when(ids[q] >= 0)
        def _():
            by = lax.rem(ids[q], blocks_y)
            inside = (lane >> 5) == by
            start = pl.multiple_of(COARSE_EDGE * home[q], COARSE_EDGE)
            for group in (range(5), range(5, 9)):
                merged = []
                for d in group:
                    value = back[q, d * 8 : d * 8 + 8, :]
                    for j in range(4):
                        moved = pltpu.roll(value, lax.rem(by + 4 - j, 4) * 32, 1)
                        merged.append((d, pl.ds(start + 8 * j, 8), moved))
                merged = [
                    (d, rows, jnp.where(inside, moved, strips[d, rows, :]))
                    for d, rows, moved in merged
                ]
                for d, rows, value in merged:
                    strips[d, rows, :] = value

        @pl.when((ids[q] >= 0) & (home[places + q] == 1))
        def _():
            store(q).start()

        return carry

    lax.fori_loop(0, places, patch, 0)
    for q in range(places):

        @pl.when((ids[q] >= 0) & (home[places + q] == 1))
        def _(q=q):
            store(q).wait()


def in_hbm(value):
    return pltpu.with_memory_space_constraint(value, pltpu.HBM)


def in_smem(value):
    return pltpu.with_memory_space_constraint(value, pltpu.SMEM)


def in_vmem(value):
    return pltpu.with_memory_space_constraint(value, pltpu.VMEM)


def local(coarse_pop, fine_pop, fine_block):
    width_x, width_y = coarse_pop.shape[1:]
    blocks_x = width_x // COARSE_EDGE
    blocks_y = width_y // COARSE_EDGE
    count_x = lax.axis_size("gx")
    count_y = lax.axis_size("gy")
    columns = blocks_y * count_y
    places = count_x * CAP
    slots = fine_block.shape[0]
    cells = FINE_EDGE * FINE_EDGE
    wide = width_x + LANES
    smem = pl.BlockSpec(memory_space=pltpu.SMEM)
    vmem = pl.BlockSpec(memory_space=pltpu.VMEM)
    hbm = pl.BlockSpec(memory_space=pltpu.HBM)
    sds = jax.ShapeDtypeStruct

    def held(*shape):
        return pltpu.VMEM(shape, F32)

    def table(size):
        return pltpu.SMEM((size,), jnp.int32)

    ask, slot = pl.pallas_call(
        functools.partial(ask_kernel, columns, blocks_x, blocks_y, count_x),
        out_shape=(held(count_x, 24, LANES), table(2 * places)),
        in_specs=[hbm, hbm],
        out_specs=(vmem, smem),
        scratch_shapes=[
            pltpu.SMEM((slots,), jnp.int32),
            pltpu.SMEM((places,), jnp.int32),
            pltpu.SMEM((count_x,), jnp.int32),
            held(2, 9, 8, LANES),
            held(2, 24, LANES),
            pltpu.SemaphoreType.DMA((3,)),
        ],
        name="ask",
        compiler_params=GRANT,
    )(in_hbm(fine_block), in_hbm(coarse_pop))
    asked = in_vmem(lax.all_to_all(ask, "gx", split_axis=0, concat_axis=0, tiled=True))
    forward_y = [(i, (i + 1) % count_y) for i in range(count_y)]
    backward_y = [(target, source) for source, target in forward_y]

    def columns_round(packed):
        sets, to_high, to_low = packed
        from_low = lax.ppermute(to_high, "gy", forward_y)
        from_high = lax.ppermute(to_low, "gy", backward_y)
        return [in_vmem(value) for value in (sets, from_low, from_high)]

    main = columns_round(
        pl.pallas_call(
            pack_kernel,
            out_shape=(held(3, 9, 8, width_x), held(24, width_x), held(24, width_x)),
            in_specs=[hbm],
            out_specs=(vmem, vmem, vmem),
            scratch_shapes=[
                held(9, width_x, LANES),
                held(2, width_x, LANES),
                pltpu.SemaphoreType.DMA((9,)),
            ],
            name="pack",
        compiler_params=GRANT,
        )(in_hbm(coarse_pop))
    )
    corner = columns_round(
        pl.pallas_call(
            functools.partial(corner_kernel, count_x),
            out_shape=(held(3, 9, 8, LANES), held(24, LANES), held(24, LANES)),
            in_specs=[vmem],
            out_specs=(vmem, vmem, vmem),
            scratch_shapes=[held(2, 9, 8, LANES), held(2, LANES, LANES)],
            name="corner",
        compiler_params=GRANT,
        )(asked)
    )
    fine_turned = jnp.transpose(fine_pop, (1, 0, 2))
    post = pl.pallas_call(
        start_kernel,
        out_shape=held(9, places, cells),
        in_specs=[smem, hbm],
        out_specs=vmem,
        scratch_shapes=[pltpu.SemaphoreType.DMA((places,))],
        name="start",
        compiler_params=GRANT,
    )(in_smem(slot), in_hbm(fine_turned))
    message, inject, wanted = pl.pallas_call(
        functools.partial(ghost_kernel, count_x, count_y),
        out_shape=(
            held(places, 8, LANES),
            pltpu.HBM((width_x, LANES), F32),
            table(places),
        ),
        in_specs=[hbm] + [vmem] * 7,
        out_specs=(vmem, hbm, smem),
        scratch_shapes=[
            pltpu.SMEM((count_x, 8, LANES), F32),
            held(9, blocks_x, 8, LANES),
            held(9, blocks_x, 8, LANES),
            held(LANES, wide),
            held(wide, LANES),
            held(9, 8, wide),
            held(3, 9, 8, wide),
            held(9, 8, wide),
            held(2, 3, 8, wide),
            held(2, blocks_x, 8, LANES),
            held(6, 9, blocks_x, 2 * LANES),
            held(6, 9, blocks_x, 2 * LANES),
            held(9, 8, 2 * LANES),
            held(2, 3, 2, blocks_x, 2 * LANES),
            held(6, blocks_x, LANES),
            held(2, 2, blocks_y, blocks_x, LANES),
            held(width_x, LANES),
            pltpu.SemaphoreType.DMA((4,)),
        ],
        name="ghost",
        compiler_params=GRANT,
    )(in_hbm(coarse_pop.reshape(9, blocks_x, COARSE_EDGE, width_y)), asked, *main, *corner)
    ghosts = in_vmem(lax.all_to_all(message, "gx", split_axis=0, concat_axis=0, tiled=True))
    fine_out, back = pl.pallas_call(
        fine_kernel,
        out_shape=(pltpu.HBM((9, slots, cells), F32), pltpu.HBM((places, 72, LANES), F32)),
        in_specs=[smem, vmem, vmem],
        out_specs=(hbm, hbm),
        scratch_shapes=[
            held(9, places, cells),
            held(places, 72, LANES),
            held(9, 8, cells),
            held(9, 64, LANES),
            held(9, 8, 8, LANES),
            held(9, 8, 8, LANES),
            pltpu.SemaphoreType.DMA((places,)),
            pltpu.SemaphoreType.DMA((places // 8,)),
        ],
        name="fine",
        compiler_params=GRANT,
    )(in_smem(slot), in_vmem(post), ghosts)
    returned = in_vmem(lax.all_to_all(back, "gx", split_axis=0, concat_axis=0, tiled=True))
    base, strips, home = pl.pallas_call(
        functools.partial(coarse_kernel, count_x, count_y),
        out_shape=(
            pltpu.HBM((9, width_x, width_y), F32),
            held(9, COARSE_EDGE * places, width_y),
            table(2 * places),
        ),
        in_specs=[hbm, vmem, hbm, hbm, smem],
        out_specs=(hbm, vmem, smem),
        scratch_shapes=[
            held(width_x, LANES),
            held(9, width_x, LANES),
            held(9, width_x + 16, LANES),
            pltpu.SemaphoreType.DMA((5,)),
            pltpu.SemaphoreType.DMA((4,)),
            pltpu.SemaphoreType.DMA((places,)),
        ],
        name="coarse",
        compiler_params=GRANT,
    )(in_hbm(coarse_pop), asked, in_hbm(inject), in_hbm(back), in_smem(wanted))
    _, coarse_out = pl.pallas_call(
        functools.partial(patch_kernel, blocks_y),
        out_shape=(
            held(9, COARSE_EDGE * places, width_y),
            pltpu.HBM((9, width_x, width_y), F32),
        ),
        in_specs=[smem, smem, hbm, vmem, vmem],
        out_specs=(vmem, hbm),
        scratch_shapes=[pltpu.SemaphoreType.DMA((places,))],
        input_output_aliases={2: 1, 3: 0},
        name="patch",
        compiler_params=GRANT,
    )(in_smem(wanted), in_smem(home), in_hbm(base), in_vmem(strips), returned)
    return (coarse_out, jnp.transpose(fine_out, (1, 0, 2)))


def solution(mesh):
    return jax.shard_map(
        local,
        mesh=mesh,
        in_specs=(P(None, "gx", "gy"), P(("gx", "gy"), None, None), P(("gx", "gy"))),
        out_specs=(P(None, "gx", "gy"), P(("gx", "gy"), None, None)),
        check_vma=False,
    )
```

```python
import functools

import jax
import jax.numpy as jnp
from jax import lax
from jax.experimental import pallas as pl
from jax.experimental.pallas import tpu as pltpu
from jax.sharding import PartitionSpec as P

FINE_EDGE = 64
COARSE_EDGE = 32
CAP = 2
LANES = 128
WINDOW = 42

along_x = [0, 1, 0, -1, 0, 1, -1, -1, 1]
along_y = [0, 0, 1, 0, -1, 1, 1, -1, -1]
opposite = [0, 3, 4, 1, 2, 7, 8, 5, 6]
UP = (1, 5, 8)
DOWN = (3, 6, 7)
LEFT = (2, 5, 6)
RIGHT = (4, 8, 7)
ORDER = (0, 1, -1)

F32 = jnp.float32
GRANT = pltpu.CompilerParams(vmem_limit_bytes=24 << 20)


def rates_of(relax_time, factor=1.0):
    return tuple((1.0 - factor) + factor * rate for rate in (1.4, 1.4, 1.2, 1.0 / relax_time))


COARSE = rates_of(0.65)
FINE = rates_of(0.8)
GHOST = rates_of(0.8, 0.8 / 1.3)
COALESCE = (1.0 - 1.3 / 0.8,) * 4


def relax(p, rates, which=tuple(range(9))):
    s_e, s_p, s_q, s_n = rates
    p0, p1, p2, p3, p4, p5, p6, p7, p8 = p
    s1, d1 = p1 + p3, p1 - p3
    s2, d2 = p2 + p4, p2 - p4
    s5, d5 = p5 + p7, p5 - p7
    s6, d6 = p6 + p8, p6 - p8
    axial, diagonal = s1 + s2, s5 + s6
    rho = p0 + axial + diagonal
    dq, sq = d5 - d6, d5 + d6
    jx, jy = d1 + dq, d2 + sq
    inv = 1.0 / rho
    xx, yy = jx * jx, jy * jy
    square = 3.0 * ((xx + yy) * inv)
    e = (axial - 2.0 * p0) + 4.0 * diagonal - square
    eps = 3.0 * (p0 - axial) + square
    a = (s_e / 36.0) * e
    b = (s_p / 36.0) * eps
    c = (s_q / 12.0) * (2.0 * dq - d1)
    d = (s_q / 12.0) * (2.0 * sq - d2)
    f = (s_n / 4.0) * ((s1 - s2) - (xx - yy) * inv)
    g = (s_n / 4.0) * ((s5 - s6) - (jx * jy) * inv)
    out = {}
    t = a + 2.0 * b
    w = 2.0 * a + b
    if 0 in which:
        out[0] = p0 + 4.0 * (a - b)
    if 1 in which:
        out[1] = p1 + ((t - f) + 2.0 * c)
    if 3 in which:
        out[3] = p3 + ((t - f) - 2.0 * c)
    if 2 in which:
        out[2] = p2 + ((t + f) + 2.0 * d)
    if 4 in which:
        out[4] = p4 + ((t + f) - 2.0 * d)
    if 5 in which:
        out[5] = p5 - ((w + g) + (c + d))
    if 7 in which:
        out[7] = p7 - ((w + g) - (c + d))
    if 6 in which:
        out[6] = p6 - ((w - g) - (c - d))
    if 8 in which:
        out[8] = p8 - ((w - g) + (c - d))
    return out


def lane_of(shape):
    return lax.broadcasted_iota(jnp.int32, shape, 1)


def row_of(shape):
    return lax.broadcasted_iota(jnp.int32, shape, 0)


def take_lanes(value, index):
    return jnp.take_along_axis(value, index, axis=1, mode="promise_in_bounds")


def ask_kernel(
    columns, blocks_x, blocks_y, count_x, block_hbm, coarse, ask, slot_ref, block_ref, id_ref, seen_ref, edge, rows, sems
):
    width = coarse.shape[1]
    places = count_x * CAP
    copies = [
        pltpu.make_async_copy(coarse.at[:, pl.ds(at, 8), :], edge.at[k], sems.at[k])
        for k, at in enumerate((0, width - 8))
    ]
    blocks = pltpu.make_async_copy(block_hbm, block_ref, sems.at[2])
    blocks.start()
    for copy in copies:
        copy.start()
    for place in range(places):
        id_ref[place] = -1
        slot_ref[place] = -1
        for part in range(1, 4):
            slot_ref[part * places + place] = 0
    for owner in range(count_x):
        seen_ref[owner] = 0
    blocks.wait()
    for slot in range(block_ref.shape[0]):
        block = block_ref[slot]
        column = lax.div(block, columns)
        row = block - column * columns
        owner = lax.div(column, blocks_x)
        rank = seen_ref[owner]
        seen_ref[owner] = rank + 1
        place = owner * CAP + rank
        id_ref[place] = (column - owner * blocks_x) * blocks_y + lax.rem(row, blocks_y)
        slot_ref[place] = slot
        slot_ref[places + place] = jnp.where(row == 0, 1, 0) + jnp.where(row == columns - 1, 2, 0)
        slot_ref[2 * places + place] = lax.rem(row * COARSE_EDGE, LANES)
        slot_ref[3 * places + place] = lax.rem(column * COARSE_EDGE, LANES)
    rows[...] = jnp.full(rows.shape, 0.1, F32)
    for copy in copies:
        copy.wait()
    for d in range(9):
        rows[0, 2 * d : 2 * d + 2, :] = edge[0, d, 0:2, :]
        rows[1, 2 * d : 2 * d + 2, :] = edge[1, d, 6:8, :]
    shape = rows.shape[1:]
    lane, row = lane_of(shape), row_of(shape)
    after = lax.rem(lax.axis_index("gx") + 1, count_x)
    for owner in range(count_x):
        number = jnp.zeros(shape, jnp.int32)
        for rank in range(CAP):
            number = jnp.where(lane == rank, id_ref[owner * CAP + rank], number)
        value = jnp.where(after == owner, rows[1], rows[0])
        ask[owner] = jnp.where(row == 18, number.astype(F32), value)


def columns_of(shape):
    lane = lane_of(shape)
    key = lax.rem(lane, 24)
    col = 32 * (key & 3) + (key >> 3) + jnp.where((key & 4) == 0, -2, 31)
    return lane, col & (LANES - 1)


def place_columns(z, d, start, count, value):
    group, part = divmod(d, 5)
    lane, col = columns_of((count, LANES))
    got = take_lanes(value, col)
    if part:
        inside = (lane >= 24 * part) & (lane < 24 * part + 24)
        got = jnp.where(inside, got, z[group, pl.ds(start, count), :])
    z[group, pl.ds(start, count), :] = got


def turn_columns(z, sets, to_high, to_low):
    to_high[...] = jnp.full(to_high.shape, 0.1, F32)
    to_low[...] = jnp.full(to_low.shape, 0.1, F32)
    for group in range(2):
        for t in range(z.shape[1] // LANES):
            lanes = pl.ds(t * LANES, LANES)
            turned = z[group, t * LANES : (t + 1) * LANES, :].T
            for part in range(5 - group):
                d = 5 * group + part
                for s in range(3):
                    sets[s, d, :, lanes] = turned[24 * part + 8 * s : 24 * part + 8 * s + 8]
                base = 24 * part
                to_high[2 * d : 2 * d + 1, lanes] = turned[base : base + 1]
                to_high[2 * d + 1 : 2 * d + 2, lanes] = turned[base + 8 : base + 9]
                to_low[2 * d : 2 * d + 1, lanes] = turned[base + 15 : base + 16]
                to_low[2 * d + 1 : 2 * d + 2, lanes] = turned[base + 23 : base + 24]


def pack_kernel(coarse, sets, to_high, to_low, buf, z, sems):
    width = coarse.shape[1]
    copies = [pltpu.make_async_copy(coarse.at[d], buf.at[d], sems.at[d]) for d in range(9)]
    for copy in copies:
        copy.start()
    rows = 512
    for d in range(9):
        copies[d].wait()

        def chunk(k, carry, d=d):
            start = pl.multiple_of(k * rows, rows)
            place_columns(z, d, start, rows, buf[d, pl.ds(start, rows), :])
            return carry

        lax.fori_loop(0, width // rows, chunk, 0)
    turn_columns(z, sets, to_high, to_low)


def neighbours(count_x):
    index = lax.axis_index("gx")
    return lax.rem(index + count_x - 1, count_x), lax.rem(index + 1, count_x)


def corner_kernel(count_x, asked, sets, to_high, to_low, ext, z):
    before, after = neighbours(count_x)
    ext[...] = jnp.full(ext.shape, 0.1, F32)
    z[...] = jnp.full(z.shape, 0.1, F32)
    for d in range(9):
        ext[0, d, 0:2, :] = asked[after, 2 * d : 2 * d + 2, :]
        ext[1, d, 6:8, :] = asked[before, 2 * d : 2 * d + 2, :]
    for d in range(9):
        place_columns(z, d, 0, 8, ext[0, d])
        place_columns(z, d, LANES - 8, 8, ext[1, d])
    turn_columns(z, sets, to_high, to_low)


def turned(part, j):
    return pltpu.roll(part, WINDOW * j, 1) if j else part


def windows(parts, off):
    lane = lane_of((8, LANES))
    got = []
    for j, (before, value, after) in enumerate(parts):
        if off == 0:
            value = jnp.where(lane == (WINDOW * j - 1) % LANES, before, value)
        if off == LANES - COARSE_EDGE:
            value = jnp.where(lane == WINDOW * j, after, value)
        got.append(value)
    place = (lane - (off - 1)) & (LANES - 1)
    return jnp.where(place < WINDOW, got[0], jnp.where(place < 2 * WINDOW, got[1], got[2]))


def ghost_kernel(
    count_x,
    count_y,
    coarse,
    asked,
    sets_main,
    low_main,
    high_main,
    sets_ext,
    low_ext,
    high_ext,
    message,
    inject_hbm,
    ids,
    numbers,
    first,
    last,
    turn,
    mt,
    old_t,
    post_t,
    new_t,
    g_t,
    pack_t,
    raw_r,
    post_r,
    new_r,
    g_r,
    far,
    pack_r,
    inject,
    sems,
):
    blocks_x = coarse.shape[1]
    width = blocks_x * COARSE_EDGE
    wide = width + LANES
    tiles = wide // LANES
    width_y = LANES
    blocks_y = width_y // COARSE_EDGE
    total_y = width_y * count_y
    base_y = lax.axis_index("gy") * width_y
    copy_first = pltpu.make_async_copy(coarse.at[:, :, pl.ds(0, 8), :], first, sems.at[0])
    copy_last = pltpu.make_async_copy(
        coarse.at[:, :, pl.ds(COARSE_EDGE - 8, 8), :], last, sems.at[1]
    )
    copy_first.start()
    copy_last.start()
    copy_ids = pltpu.make_async_copy(asked.at[:, pl.ds(16, 8), :], numbers, sems.at[2])
    copy_ids.start()
    index_before, index_after = neighbours(count_x)

    turn[...] = jnp.full(turn.shape, 0.1, F32)
    for d in range(9):
        at = (4 * d - 2) % LANES
        turn[4 * d : 4 * d + 2, 0:width] = high_main[2 * d : 2 * d + 2, :]
        turn[4 * d : 4 * d + 2, width:] = high_ext[2 * d : 2 * d + 2, :]
        turn[at : at + 2, 0:width] = low_main[2 * d : 2 * d + 2, :]
        turn[at : at + 2, width:] = low_ext[2 * d : 2 * d + 2, :]
    for t in range(tiles):
        mt[t * LANES : (t + 1) * LANES, :] = turn[:, t * LANES : (t + 1) * LANES].T
    tile = (8, LANES)
    row8 = row_of(tile)

    def collide_tile(sets, from_low, from_high, at, lanes):
        for s in range(3):
            p = []
            for d in range(9):
                value = sets[s, d, :, at]
                if s < 2:
                    value = jnp.where(row8 == 0, from_low[2 * d + s : 2 * d + s + 1, at], value)
                if s > 0:
                    value = jnp.where(row8 == 7, from_high[2 * d + s - 1 : 2 * d + s, at], value)
                if s == 1:
                    old_t[d, :, lanes] = value
                p.append(value)
            out = relax(p, COARSE)
            for d in range(9):
                post_t[s, d, :, lanes] = out[d]

    def collide_t(t, carry):
        lanes = pl.ds(pl.multiple_of(t * LANES, LANES), LANES)
        collide_tile(sets_main, low_main, high_main, lanes, lanes)
        return carry

    lax.fori_loop(0, tiles - 1, collide_t, 0)
    collide_tile(sets_ext, low_ext, high_ext, pl.ds(0, LANES), pl.ds(width, LANES))
    turn[...] = jnp.zeros(turn.shape, F32)
    row_t = row_of((8, wide))
    coord_t = base_y + 32 * (row_t & 3) + jnp.where(row_t < 4, -1, 32)
    for d in range(9):
        source = post_t[{1: 0, 0: 1, -1: 2}[along_y[d]], d]
        if along_x[d]:
            source = pltpu.roll(source, along_x[d] % wide, 1)
        back = coord_t - along_y[d]
        beyond = (back < 0) | (back >= total_y)
        new_t[d] = jnp.where(beyond, post_t[1, opposite[d]], source)
    for j in range(3):
        for side, (d, row) in enumerate(((LEFT[j], 0), (RIGHT[j], 7))):
            source = post_t[1, d]
            if along_x[d]:
                source = pltpu.roll(source, along_x[d] % wide, 1)
            turn[3 * side + j : 3 * side + j + 1, :] = source[row : row + 1, :]
    for t in range(width // LANES):
        inject[t * LANES : (t + 1) * LANES, :] = turn[:, t * LANES : (t + 1) * LANES].T
    copy_inject = pltpu.make_async_copy(inject, inject_hbm, sems.at[3])
    copy_inject.start()

    def ghosts_t(t, carry):
        lanes = pl.ds(pl.multiple_of(t * LANES, LANES), LANES)
        old = [old_t[d, :, lanes] for d in range(9)]
        mean = [0.5 * (old[d] + new_t[d, :, lanes]) for d in range(9)]
        for sub, p in enumerate((old, mean)):
            out = relax(p, GHOST, LEFT + RIGHT)
            for j in range(3):
                g_t[sub, j, :, lanes] = jnp.where(row8 < 4, out[LEFT[j]], out[RIGHT[j]])
        return carry

    lax.fori_loop(0, tiles, ghosts_t, 0)
    for sub in range(2):
        moved = [
            [turned(g_t[sub, j, :, LANES * k : LANES * (k + 1)], j) for k in range(tiles)]
            for j in range(3)
        ]
        for bx in range(blocks_x):
            t, off = divmod(COARSE_EDGE * bx, LANES)
            parts = [(m[t - 1], m[t], m[t + 1]) for m in moved]
            pack_t[sub, bx] = windows(parts, off)

    plane = (blocks_x, LANES)
    rows_b = row_of(plane)

    def lower(value, row):
        return jnp.where(rows_b == 0, row, pltpu.roll(value, 1, 0))

    def upper(value, row):
        return jnp.where(rows_b == blocks_x - 1, row, pltpu.roll(value, blocks_x - 1, 0))

    def every(ref, start, step):
        return ref[pl.ds(start, blocks_x, stride=step), :]

    side_rows = [every(mt, c, COARSE_EDGE) for c in (0, 1, COARSE_EDGE - 2, COARSE_EDGE - 1)]
    m0, m1, m30, m31 = side_rows
    extra = (
        lower(m30, mt[wide - 2 : wide - 1, :]),
        lower(m31, mt[wide - 1 : wide, :]),
        m0,
        m31,
        upper(m0, mt[width : width + 1, :]),
        upper(m1, mt[width + 1 : width + 2, :]),
    )
    copy_first.wait()
    copy_last.wait()
    first2 = first.reshape(9 * blocks_x * 8, LANES)
    last2 = last.reshape(9 * blocks_x * 8, LANES)
    for k in range(6):
        far[k] = extra[k]

    def raw_rows(d, carry):
        at = d * (blocks_x * 8)
        a0, a1 = every(first2, at, 8), every(first2, at + 1, 8)
        b30, b31 = every(last2, at + 6, 8), every(last2, at + 7, 8)
        main = (
            lower(b30, asked[index_before, pl.ds(2 * d, 1), :]),
            lower(b31, asked[index_before, pl.ds(2 * d + 1, 1), :]),
            a0,
            b31,
            upper(a0, asked[index_after, pl.ds(2 * d, 1), :]),
            upper(a1, asked[index_after, pl.ds(2 * d + 1, 1), :]),
        )
        for k in range(6):
            raw_r[k, d, :, 0:LANES] = main[k]
            raw_r[k, d, :, LANES:] = pltpu.roll(far[k], lax.rem(LANES - 4 * d, LANES), 1)
        return carry

    lax.fori_loop(0, 9, raw_rows, 0)

    def collide_r(k, carry):
        rows = pl.ds(pl.multiple_of(k * 8, 8), 8)
        for s in range(6):
            for half in range(2):
                lanes = pl.ds(half * LANES, LANES)
                out = relax([raw_r[s, d, rows, lanes] for d in range(9)], COARSE)
                for d in range(9):
                    post_r[s, d, rows, lanes] = out[d]
        return carry

    lax.fori_loop(0, blocks_x // 8, collide_r, 0)
    double = (8, 2 * LANES)
    lane_r = lane_of(double)
    coord_r = base_y + jnp.where(lane_r < LANES + 2, lane_r, lane_r - 2 * LANES)

    def ghosts_r(k, carry):
        rows = pl.ds(pl.multiple_of(k * 8, 8), 8)
        for side in range(2):
            for d in range(9):
                source = post_r[3 * side + {1: 0, 0: 1, -1: 2}[along_x[d]], d, rows, :]
                if along_y[d]:
                    source = pltpu.roll(source, along_y[d] % (2 * LANES), 1)
                back = coord_r - along_y[d]
                beyond = (back < 0) | (back >= total_y)
                new_r[d] = jnp.where(beyond, post_r[3 * side + 1, opposite[d], rows, :], source)
            which = (UP, DOWN)[side]
            for half in range(2):
                lanes = pl.ds(half * LANES, LANES)
                old = [raw_r[3 * side + 1, d, rows, lanes] for d in range(9)]
                mean = [0.5 * (old[d] + new_r[d, :, lanes]) for d in range(9)]
                for sub, p in enumerate((old, mean)):
                    out = relax(p, GHOST, which)
                    for j in range(3):
                        g_r[side, j, sub, rows, lanes] = out[which[j]]
        return carry

    lax.fori_loop(0, blocks_x // 8, ghosts_r, 0)

    def windows_r(k, carry):
        rows = pl.ds(pl.multiple_of(k * 8, 8), 8)
        for side in range(2):
            for sub in range(2):
                parts = []
                for j in range(3):
                    one = turned(g_r[side, j, sub, rows, 0:LANES], j)
                    two = turned(g_r[side, j, sub, rows, LANES:], j)
                    parts.append((two, one, two))
                for by in range(blocks_y):
                    pack_r[side, sub, by, rows, :] = windows(parts, COARSE_EDGE * by)
        return carry

    lax.fori_loop(0, blocks_x // 8, windows_r, 0)

    copy_ids.wait()
    for q in range(message.shape[0]):
        ids[q] = numbers[q // CAP, 2, q % CAP].astype(jnp.int32)

    def pick(q, carry):
        block = jnp.maximum(ids[q], 0)
        bx = lax.div(block, blocks_y)
        by = block - bx * blocks_y
        for sub in range(2):
            for side in range(2):
                row = 4 * sub + side
                message[q, row : row + 1, :] = pack_r[side, sub, by, pl.ds(bx, 1), :]
                row = 4 * sub + 2 + side
                message[q, row : row + 1, :] = pack_t[sub, bx, pl.ds(4 * side + by, 1), :]
        return carry

    lax.fori_loop(0, message.shape[0], pick, 0, unroll=4)
    copy_inject.wait()


def start_kernel(slot, fine, post, sem):
    places = post.shape[1]
    copies = []
    for q in range(places):
        source = fine.at[:, pl.ds(jnp.maximum(slot[q], 0), 1), :]
        copy = pltpu.make_async_copy(source, post.at[:, pl.ds(q, 1), :], sem.at[q])
        copy.start()
        copies.append(copy)
    for copy in copies:
        copy.wait()

    def body(k, carry):
        lanes = pl.ds(pl.multiple_of(k * LANES, LANES), LANES)
        for h in range(places // 8):
            rows = pl.ds(8 * h, 8)
            out = relax([post[d, rows, lanes] for d in range(9)], FINE)
            for d in range(9):
                post[d, rows, lanes] = out[d]
        return carry

    lax.fori_loop(0, post.shape[2] // LANES, body, 0, unroll=2)


def fine_kernel(
    slot, post, ghosts, fine, back_hbm, result, back, post_two, line, mean, swapped, sem, back_sem
):
    places = post.shape[1]
    tiles = post.shape[2] // LANES
    tile = (8, LANES)
    lane, row = lane_of(tile), row_of(tile)
    low_half = lane < 64
    at_low = (lane & 63) == 0
    at_high = (lane & 63) == 63
    ghosts2 = ghosts.reshape(places * 8, LANES)
    over = [WINDOW * j + 1 + (((lane & 63) - c) >> 1) for j, c in enumerate(ORDER)]
    even = (lane & 1) == 0
    turn_back = jnp.where(even, lane, (lane - 63) & (LANES - 1))
    cell = (turn_back & 63) + (turn_back >> 6)
    along = [(WINDOW * j + 1 + ((cell - c) >> 1)) & (LANES - 1) for j, c in enumerate(ORDER)]

    def copy(q):
        target = fine.at[:, pl.ds(jnp.maximum(slot[q], 0), 1), :]
        return pltpu.make_async_copy(result.at[:, pl.ds(q, 1), :], target, sem.at[q])

    def send(h):
        part = pl.ds(8 * h, 8)
        return pltpu.make_async_copy(back.at[part], back_hbm.at[part], back_sem.at[h])

    def half(h, carry):
        rows = pl.ds(pl.multiple_of(8 * h, 8), 8)
        wall = jnp.zeros(tile, jnp.int32)
        off_y, off_x = wall, wall
        for r in range(8):
            here = row == r
            wall = jnp.where(here, slot[places + 8 * h + r], wall)
            off_y = jnp.where(here, slot[2 * places + 8 * h + r], off_y)
            off_x = jnp.where(here, slot[3 * places + 8 * h + r], off_x)
        over_own = [(index + off_y - 1) & (LANES - 1) for index in over]
        along_own = [(index + off_x - 1) & (LANES - 1) for index in along]
        quarter = ((lane >> 5) - (off_y >> 5)) & 3
        squeeze = 64 * (quarter & 1) + 2 * (lane & 31) + (quarter >> 1)
        wall_low = at_low & ((wall & 1) != 0)
        wall_high = at_high & ((wall & 2) != 0)

        def substep(sub, source, emit):
            border = [
                ghosts2[pl.ds(h * 64 + 4 * sub + side, 8, stride=8), :] for side in range(4)
            ]
            up = [take_lanes(border[0], over_own[j]) for j in range(3)]
            down = [take_lanes(border[1], over_own[j]) for j in range(3)]
            beside = [
                jnp.where(
                    even, take_lanes(border[2], along_own[j]), take_lanes(border[3], along_own[j])
                )
                for j in range(3)
            ]

            def load(d, k):
                return source[d, rows, k * LANES : (k + 1) * LANES]

            def crossed(d, k):
                if k < 0:
                    return up[UP.index(d)]
                if k == tiles:
                    return down[DOWN.index(d)]
                return pltpu.roll(load(d, k), (64 + along_y[d]) % LANES, 1)

            before = {d: crossed(d, -1) for d in UP}
            now = {d: crossed(d, 0) for d in DOWN}
            for k in range(tiles):
                ghosts_k = [
                    pltpu.roll(value, (-2 * k) % LANES, 1) if k else value for value in beside
                ]
                out = []
                for d in range(9):
                    if along_x[d] > 0:
                        turned = crossed(d, k)
                        value = jnp.where(low_half, before[d], turned)
                        before[d] = turned
                    elif along_x[d] < 0:
                        turned = crossed(d, k + 1)
                        value = jnp.where(low_half, now[d], turned)
                        now[d] = turned
                    else:
                        value = load(d, k)
                        if along_y[d]:
                            value = pltpu.roll(value, along_y[d] % LANES, 1)
                    if along_y[d] > 0:
                        value = jnp.where(at_low, ghosts_k[LEFT.index(d)], value)
                        value = jnp.where(wall_low, load(opposite[d], k), value)
                    elif along_y[d] < 0:
                        value = jnp.where(at_high, ghosts_k[RIGHT.index(d)], value)
                        value = jnp.where(wall_high, load(opposite[d], k), value)
                    out.append(value)
                emit(k, out)

        def emit_first(k, p):
            out = relax(p, FINE)
            for d in range(9):
                post_two[d, :, k * LANES : (k + 1) * LANES] = out[d]

        def emit_second(k, p):
            for d in range(9):
                result[d, rows, k * LANES : (k + 1) * LANES] = p[d]

        post_rows = post
        substep(0, post_rows, emit_first)
        substep(1, _Rows(post_two), emit_second)
        for r in range(8):

            @pl.when(slot[8 * h + r] >= 0)
            def _(r=r):
                copy(8 * h + r).start()

        def tile_of(ref, d, k):
            return ref[d, rows, pl.ds(pl.multiple_of(k * LANES, LANES), LANES)]

        def pair_up(step, carry):
            for u in range(4):
                i = 4 * step + u
                for d in range(9):
                    pairs = []
                    for m in range(2):
                        one = tile_of(result, d, i + 16 * m)
                        two = tile_of(result, d, i + 16 * m + 8)
                        other = pltpu.roll(jnp.where(low_half, two, one), 64, 1)
                        pairs.append(jnp.where(low_half, one, two) + other)
                    mean[d, i] = jnp.where(even, pairs[0], pairs[1])
                    swapped[d, i] = jnp.where(even, pairs[1], pairs[0])
            return carry

        def merge(step, carry):
            for u in range(4):
                i = 4 * step + u
                total = []
                for d in range(9):
                    moved = swapped[d, i]
                    moved = jnp.where(even, pltpu.roll(moved, 127, 1), pltpu.roll(moved, 1, 1))
                    total.append(0.25 * (mean[d, i] + moved))
                out = relax(total, COALESCE)
                for d in range(9):
                    mean[d, i] = out[d]
            return carry

        def compress(step, carry):
            for u in range(4):
                i = 4 * step + u
                for d in range(9):
                    at = pl.ds(pl.multiple_of(i * 8, 8), 8)
                    line[d, at, :] = take_lanes(mean[d, i], squeeze)
            return carry

        lax.fori_loop(0, 2, pair_up, 0)
        lax.fori_loop(0, 2, merge, 0)
        lax.fori_loop(0, 2, compress, 0)
        for d in range(9):
            flat = line.at[d]
            for q in range(8):
                back[8 * h + q, d * 8 : d * 8 + 8, :] = flat[pl.ds(q, 8, stride=8), :]
        send(h).start()
        return carry

    lax.fori_loop(0, places // 8, half, 0)
    for h in range(places // 8):
        send(h).wait()
    for q in range(places):

        @pl.when(slot[q] >= 0)
        def _(q=q):
            copy(q).wait()


class _Rows:
    def __init__(self, ref):
        self.ref = ref

    def __getitem__(self, key):
        d, _, lanes = key
        return self.ref[d, :, lanes]


def coarse_kernel(
    count_x, count_y, coarse, asked, inject_hbm, after, ids, base, strips, home, inject, new, post, load, save, cut
):
    width = coarse.shape[1]
    places = ids.shape[0]
    blocks_y = coarse.shape[2] // COARSE_EDGE
    tile = (8, LANES)
    lane = lane_of(tile)
    parts = 4
    size = width // parts
    copies = [
        pltpu.make_async_copy(
            coarse.at[:, pl.ds(k * size, size), :],
            post.at[:, pl.ds(8 + k * size, size), :],
            load.at[k],
        )
        for k in range(parts)
    ]
    for copy in copies:
        copy.start()
    copy_inject = pltpu.make_async_copy(inject_hbm, inject, load.at[parts])
    copy_inject.start()
    before, following = neighbours(count_x)
    out = relax([asked[before, 2 * d + 1 : 2 * d + 2, :] for d in range(9)], COARSE)
    for d in range(9):
        post[d, 7:8, :] = out[d]
    out = relax([asked[following, 2 * d : 2 * d + 1, :] for d in range(9)], COARSE)
    for d in range(9):
        post[d, width + 8 : width + 9, :] = out[d]

    def collide(k, carry):
        rows = pl.ds(pl.multiple_of(8 + 8 * k, 8), 8)
        out = relax([post[d, rows, :] for d in range(9)], COARSE)
        for d in range(9):
            post[d, rows, :] = out[d]
        return carry

    index_y = lax.axis_index("gy")
    wall_low = (lane == 0) & (index_y == 0)
    wall_high = (lane == LANES - 1) & (index_y == count_y - 1)

    def stream(k, carry):
        start = pl.multiple_of(8 * k, 8)
        edge = inject[pl.ds(start, 8), :]
        for d in range(9):
            value = post[d, pl.ds(start + (8 - along_x[d]), 8), :]
            if along_y[d]:
                value = pltpu.roll(value, along_y[d] % LANES, 1)
                same = post[opposite[d], pl.ds(start + 8, 8), :]
                if along_y[d] > 0:
                    j = LEFT.index(d)
                    value = jnp.where(lane == 0, pltpu.roll(edge, (-j) % LANES, 1), value)
                    value = jnp.where(wall_low, same, value)
                else:
                    j = RIGHT.index(d)
                    moved = pltpu.roll(edge, LANES - 4 - j, 1)
                    value = jnp.where(lane == LANES - 1, moved, value)
                    value = jnp.where(wall_high, same, value)
            new[d, pl.ds(start, 8), :] = value
        return carry

    copy_inject.wait()
    copies[0].wait()
    lax.fori_loop(0, size // 8, collide, 0, unroll=4)
    stores = []
    for k in range(parts):
        if k + 1 < parts:
            copies[k + 1].wait()
            lax.fori_loop((k + 1) * size // 8, (k + 2) * size // 8, collide, 0, unroll=4)
        lax.fori_loop(k * size // 8, (k + 1) * size // 8, stream, 0, unroll=4)
        rows = pl.ds(k * size, size)
        store = pltpu.make_async_copy(new.at[:, rows, :], base.at[:, rows, :], save.at[k])
        store.start()
        stores.append(store)

    def column(q):
        return lax.div(jnp.maximum(ids[q], 0), blocks_y)

    def strip(q):
        rows = pl.ds(pl.multiple_of(COARSE_EDGE * column(q), COARSE_EDGE), COARSE_EDGE)
        return pltpu.make_async_copy(
            new.at[:, rows, :], strips.at[:, pl.ds(COARSE_EDGE * q, COARSE_EDGE), :], cut.at[q]
        )

    for q in range(places):

        @pl.when(ids[q] >= 0)
        def _(q=q):
            strip(q).start()

    for q in range(places):
        first, last = jnp.int32(q), jnp.int32(1)
        for other in reversed(range(places)):
            if other != q:
                same = (ids[q] >= 0) & (ids[other] >= 0) & (column(q) == column(other))
                if other < q:
                    first = jnp.where(same, other, first)
                else:
                    last = jnp.where(same, 0, last)
        home[q] = first
        home[places + q] = last
    for store in stores:
        store.wait()
    for q in range(places):

        @pl.when(ids[q] >= 0)
        def _(q=q):
            strip(q).wait()


def patch_kernel(blocks_y, ids, home, base, strips_in, back, strips, out, save):
    lane = lane_of((8, LANES))
    places = ids.shape[0]

    def store(q):
        bx = lax.div(jnp.maximum(ids[q], 0), blocks_y)
        rows = pl.ds(pl.multiple_of(COARSE_EDGE * bx, COARSE_EDGE), COARSE_EDGE)
        own = pl.ds(pl.multiple_of(COARSE_EDGE * home[q], COARSE_EDGE), COARSE_EDGE)
        return pltpu.make_async_copy(strips.at[:, own, :], out.at[:, rows, :], save.at[q])

    def patch(q, carry):
        @pl.when(ids[q] >= 0)
        def _():
            by = lax.rem(ids[q], blocks_y)
            inside = (lane >> 5) == by
            start = pl.multiple_of(COARSE_EDGE * home[q], COARSE_EDGE)
            for group in (range(5), range(5, 9)):
                merged = []
                for d in group:
                    value = back[q, d * 8 : d * 8 + 8, :]
                    for j in range(4):
                        moved = pltpu.roll(value, LANES - 32 * j, 1) if j else value
                        merged.append((d, pl.ds(start + 8 * j, 8), moved))
                merged = [
                    (d, rows, jnp.where(inside, moved, strips[d, rows, :]))
                    for d, rows, moved in merged
                ]
                for d, rows, value in merged:
                    strips[d, rows, :] = value

        @pl.when((ids[q] >= 0) & (home[places + q] == 1))
        def _():
            store(q).start()

        return carry

    lax.fori_loop(0, places, patch, 0)
    for q in range(places):

        @pl.when((ids[q] >= 0) & (home[places + q] == 1))
        def _(q=q):
            store(q).wait()


def in_hbm(value):
    return pltpu.with_memory_space_constraint(value, pltpu.HBM)


def in_smem(value):
    return pltpu.with_memory_space_constraint(value, pltpu.SMEM)


def in_vmem(value):
    return pltpu.with_memory_space_constraint(value, pltpu.VMEM)


def local(coarse_pop, fine_pop, fine_block):
    width_x, width_y = coarse_pop.shape[1:]
    blocks_x = width_x // COARSE_EDGE
    blocks_y = width_y // COARSE_EDGE
    count_x = lax.axis_size("gx")
    count_y = lax.axis_size("gy")
    columns = blocks_y * count_y
    places = count_x * CAP
    slots = fine_block.shape[0]
    cells = FINE_EDGE * FINE_EDGE
    wide = width_x + LANES
    smem = pl.BlockSpec(memory_space=pltpu.SMEM)
    vmem = pl.BlockSpec(memory_space=pltpu.VMEM)
    hbm = pl.BlockSpec(memory_space=pltpu.HBM)
    sds = jax.ShapeDtypeStruct

    def held(*shape):
        return pltpu.VMEM(shape, F32)

    def table(size):
        return pltpu.SMEM((size,), jnp.int32)

    ask, slot = pl.pallas_call(
        functools.partial(ask_kernel, columns, blocks_x, blocks_y, count_x),
        out_shape=(held(count_x, 24, LANES), table(4 * places)),
        in_specs=[hbm, hbm],
        out_specs=(vmem, smem),
        scratch_shapes=[
            pltpu.SMEM((slots,), jnp.int32),
            pltpu.SMEM((places,), jnp.int32),
            pltpu.SMEM((count_x,), jnp.int32),
            held(2, 9, 8, LANES),
            held(2, 24, LANES),
            pltpu.SemaphoreType.DMA((3,)),
        ],
        name="ask",
        compiler_params=GRANT,
    )(in_hbm(fine_block), in_hbm(coarse_pop))
    asked = in_vmem(lax.all_to_all(ask, "gx", split_axis=0, concat_axis=0, tiled=True))
    forward_y = [(i, (i + 1) % count_y) for i in range(count_y)]
    backward_y = [(target, source) for source, target in forward_y]

    def columns_round(packed):
        sets, to_high, to_low = packed
        from_low = lax.ppermute(to_high, "gy", forward_y)
        from_high = lax.ppermute(to_low, "gy", backward_y)
        return [in_vmem(value) for value in (sets, from_low, from_high)]

    main = columns_round(
        pl.pallas_call(
            pack_kernel,
            out_shape=(held(3, 9, 8, width_x), held(24, width_x), held(24, width_x)),
            in_specs=[hbm],
            out_specs=(vmem, vmem, vmem),
            scratch_shapes=[
                held(9, width_x, LANES),
                held(2, width_x, LANES),
                pltpu.SemaphoreType.DMA((9,)),
            ],
            name="pack",
        compiler_params=GRANT,
        )(in_hbm(coarse_pop))
    )
    corner = columns_round(
        pl.pallas_call(
            functools.partial(corner_kernel, count_x),
            out_shape=(held(3, 9, 8, LANES), held(24, LANES), held(24, LANES)),
            in_specs=[vmem],
            out_specs=(vmem, vmem, vmem),
            scratch_shapes=[held(2, 9, 8, LANES), held(2, LANES, LANES)],
            name="corner",
        compiler_params=GRANT,
        )(asked)
    )
    fine_turned = jnp.transpose(fine_pop, (1, 0, 2))
    post = pl.pallas_call(
        start_kernel,
        out_shape=held(9, places, cells),
        in_specs=[smem, hbm],
        out_specs=vmem,
        scratch_shapes=[pltpu.SemaphoreType.DMA((places,))],
        name="start",
        compiler_params=GRANT,
    )(in_smem(slot), in_hbm(fine_turned))
    message, inject, wanted = pl.pallas_call(
        functools.partial(ghost_kernel, count_x, count_y),
        out_shape=(
            held(places, 8, LANES),
            pltpu.HBM((width_x, LANES), F32),
            table(places),
        ),
        in_specs=[hbm] + [vmem] * 7,
        out_specs=(vmem, hbm, smem),
        scratch_shapes=[
            pltpu.SMEM((count_x, 8, LANES), F32),
            held(9, blocks_x, 8, LANES),
            held(9, blocks_x, 8, LANES),
            held(LANES, wide),
            held(wide, LANES),
            held(9, 8, wide),
            held(3, 9, 8, wide),
            held(9, 8, wide),
            held(2, 3, 8, wide),
            held(2, blocks_x, 8, LANES),
            held(6, 9, blocks_x, 2 * LANES),
            held(6, 9, blocks_x, 2 * LANES),
            held(9, 8, 2 * LANES),
            held(2, 3, 2, blocks_x, 2 * LANES),
            held(6, blocks_x, LANES),
            held(2, 2, blocks_y, blocks_x, LANES),
            held(width_x, LANES),
            pltpu.SemaphoreType.DMA((4,)),
        ],
        name="ghost",
        compiler_params=GRANT,
    )(in_hbm(coarse_pop.reshape(9, blocks_x, COARSE_EDGE, width_y)), asked, *main, *corner)
    ghosts = in_vmem(lax.all_to_all(message, "gx", split_axis=0, concat_axis=0, tiled=True))
    fine_out, back = pl.pallas_call(
        fine_kernel,
        out_shape=(pltpu.HBM((9, slots, cells), F32), pltpu.HBM((places, 72, LANES), F32)),
        in_specs=[smem, vmem, vmem],
        out_specs=(hbm, hbm),
        scratch_shapes=[
            held(9, places, cells),
            held(places, 72, LANES),
            held(9, 8, cells),
            held(9, 64, LANES),
            held(9, 8, 8, LANES),
            held(9, 8, 8, LANES),
            pltpu.SemaphoreType.DMA((places,)),
            pltpu.SemaphoreType.DMA((places // 8,)),
        ],
        name="fine",
        compiler_params=GRANT,
    )(in_smem(slot), in_vmem(post), ghosts)
    returned = in_vmem(lax.all_to_all(back, "gx", split_axis=0, concat_axis=0, tiled=True))
    base, strips, home = pl.pallas_call(
        functools.partial(coarse_kernel, count_x, count_y),
        out_shape=(
            pltpu.HBM((9, width_x, width_y), F32),
            held(9, COARSE_EDGE * places, width_y),
            table(2 * places),
        ),
        in_specs=[hbm, vmem, hbm, hbm, smem],
        out_specs=(hbm, vmem, smem),
        scratch_shapes=[
            held(width_x, LANES),
            held(9, width_x, LANES),
            held(9, width_x + 16, LANES),
            pltpu.SemaphoreType.DMA((5,)),
            pltpu.SemaphoreType.DMA((4,)),
            pltpu.SemaphoreType.DMA((places,)),
        ],
        name="coarse",
        compiler_params=GRANT,
    )(in_hbm(coarse_pop), asked, in_hbm(inject), in_hbm(back), in_smem(wanted))
    _, coarse_out = pl.pallas_call(
        functools.partial(patch_kernel, blocks_y),
        out_shape=(
            held(9, COARSE_EDGE * places, width_y),
            pltpu.HBM((9, width_x, width_y), F32),
        ),
        in_specs=[smem, smem, hbm, vmem, vmem],
        out_specs=(vmem, hbm),
        scratch_shapes=[pltpu.SemaphoreType.DMA((places,))],
        input_output_aliases={2: 1, 3: 0},
        name="patch",
        compiler_params=GRANT,
    )(in_smem(wanted), in_smem(home), in_hbm(base), in_vmem(strips), returned)
    return (coarse_out, jnp.transpose(fine_out, (1, 0, 2)))


def solution(mesh):
    return jax.shard_map(
        local,
        mesh=mesh,
        in_specs=(P(None, "gx", "gy"), P(("gx", "gy"), None, None), P(("gx", "gy"))),
        out_specs=(P(None, "gx", "gy"), P(("gx", "gy"), None, None)),
        check_vma=False,
    )
```

```python
import functools

import jax
import jax.numpy as jnp
from jax import lax
from jax.experimental import pallas as pl
from jax.experimental.pallas import tpu as pltpu
from jax.sharding import PartitionSpec as P

FINE_EDGE = 64
COARSE_EDGE = 32
CAP = 2
LANES = 128
WINDOW = 42

along_x = [0, 1, 0, -1, 0, 1, -1, -1, 1]
along_y = [0, 0, 1, 0, -1, 1, 1, -1, -1]
opposite = [0, 3, 4, 1, 2, 7, 8, 5, 6]
UP = (1, 5, 8)
DOWN = (3, 6, 7)
LEFT = (2, 5, 6)
RIGHT = (4, 8, 7)
ORDER = (0, 1, -1)

F32 = jnp.float32
GRANT = pltpu.CompilerParams(vmem_limit_bytes=24 << 20)


def rates_of(relax_time, factor=1.0):
    return tuple((1.0 - factor) + factor * rate for rate in (1.4, 1.4, 1.2, 1.0 / relax_time))


COARSE = rates_of(0.65)
FINE = rates_of(0.8)
GHOST = rates_of(0.8, 0.8 / 1.3)
COALESCE = (1.0 - 1.3 / 0.8,) * 4


def relax(p, rates, which=tuple(range(9))):
    s_e, s_p, s_q, s_n = rates
    p0, p1, p2, p3, p4, p5, p6, p7, p8 = p
    s1, d1 = p1 + p3, p1 - p3
    s2, d2 = p2 + p4, p2 - p4
    s5, d5 = p5 + p7, p5 - p7
    s6, d6 = p6 + p8, p6 - p8
    axial, diagonal = s1 + s2, s5 + s6
    rho = p0 + axial + diagonal
    dq, sq = d5 - d6, d5 + d6
    jx, jy = d1 + dq, d2 + sq
    inv = 1.0 / rho
    xx, yy = jx * jx, jy * jy
    square = 3.0 * ((xx + yy) * inv)
    e = (axial - 2.0 * p0) + 4.0 * diagonal - square
    eps = 3.0 * (p0 - axial) + square
    a = (s_e / 36.0) * e
    b = (s_p / 36.0) * eps
    c = (s_q / 12.0) * (2.0 * dq - d1)
    d = (s_q / 12.0) * (2.0 * sq - d2)
    f = (s_n / 4.0) * ((s1 - s2) - (xx - yy) * inv)
    g = (s_n / 4.0) * ((s5 - s6) - (jx * jy) * inv)
    out = {}
    t = a + 2.0 * b
    w = 2.0 * a + b
    if 0 in which:
        out[0] = p0 + 4.0 * (a - b)
    if 1 in which:
        out[1] = p1 + ((t - f) + 2.0 * c)
    if 3 in which:
        out[3] = p3 + ((t - f) - 2.0 * c)
    if 2 in which:
        out[2] = p2 + ((t + f) + 2.0 * d)
    if 4 in which:
        out[4] = p4 + ((t + f) - 2.0 * d)
    if 5 in which:
        out[5] = p5 - ((w + g) + (c + d))
    if 7 in which:
        out[7] = p7 - ((w + g) - (c + d))
    if 6 in which:
        out[6] = p6 - ((w - g) - (c - d))
    if 8 in which:
        out[8] = p8 - ((w - g) + (c - d))
    return out


def lane_of(shape):
    return lax.broadcasted_iota(jnp.int32, shape, 1)


def row_of(shape):
    return lax.broadcasted_iota(jnp.int32, shape, 0)


def take_lanes(value, index):
    return jnp.take_along_axis(value, index, axis=1, mode="promise_in_bounds")


def ask_kernel(
    columns, blocks_x, blocks_y, count_x, block_hbm, coarse, ask, slot_ref, block_ref, id_ref, seen_ref, edge, rows, sems
):
    width = coarse.shape[1]
    places = count_x * CAP
    copies = [
        pltpu.make_async_copy(coarse.at[:, pl.ds(at, 8), :], edge.at[k], sems.at[k])
        for k, at in enumerate((0, width - 8))
    ]
    blocks = pltpu.make_async_copy(block_hbm, block_ref, sems.at[2])
    blocks.start()
    for copy in copies:
        copy.start()
    for place in range(places):
        id_ref[place] = -1
        slot_ref[place] = -1
        for part in range(1, 4):
            slot_ref[part * places + place] = 0
    for owner in range(count_x):
        seen_ref[owner] = 0
    blocks.wait()
    for slot in range(block_ref.shape[0]):
        block = block_ref[slot]
        column = lax.div(block, columns)
        row = block - column * columns
        owner = lax.div(column, blocks_x)
        rank = seen_ref[owner]
        seen_ref[owner] = rank + 1
        place = owner * CAP + rank
        id_ref[place] = (column - owner * blocks_x) * blocks_y + lax.rem(row, blocks_y)
        slot_ref[place] = slot
        slot_ref[places + place] = jnp.where(row == 0, 1, 0) + jnp.where(row == columns - 1, 2, 0)
        slot_ref[2 * places + place] = lax.rem(row * COARSE_EDGE, LANES)
        slot_ref[3 * places + place] = lax.rem(column * COARSE_EDGE, LANES)
    rows[...] = jnp.full(rows.shape, 0.1, F32)
    for copy in copies:
        copy.wait()
    for d in range(9):
        rows[0, 2 * d : 2 * d + 2, :] = edge[0, d, 0:2, :]
        rows[1, 2 * d : 2 * d + 2, :] = edge[1, d, 6:8, :]
    shape = rows.shape[1:]
    lane, row = lane_of(shape), row_of(shape)
    after = lax.rem(lax.axis_index("gx") + 1, count_x)
    for owner in range(count_x):
        number = jnp.zeros(shape, jnp.int32)
        for rank in range(CAP):
            number = jnp.where(lane == rank, id_ref[owner * CAP + rank], number)
        value = jnp.where(after == owner, rows[1], rows[0])
        ask[owner] = jnp.where(row == 18, number.astype(F32), value)


def columns_of(shape):
    lane = lane_of(shape)
    key = lax.rem(lane, 24)
    col = 32 * (key & 3) + (key >> 3) + jnp.where((key & 4) == 0, -2, 31)
    return lane, col & (LANES - 1)


def place_columns(z, d, start, count, value):
    group, part = divmod(d, 5)
    lane, col = columns_of((count, LANES))
    got = take_lanes(value, col)
    if part:
        inside = (lane >= 24 * part) & (lane < 24 * part + 24)
        got = jnp.where(inside, got, z[group, pl.ds(start, count), :])
    z[group, pl.ds(start, count), :] = got


def turn_columns(z, sets, to_high, to_low):
    to_high[...] = jnp.full(to_high.shape, 0.1, F32)
    to_low[...] = jnp.full(to_low.shape, 0.1, F32)
    for group in range(2):
        for t in range(z.shape[1] // LANES):
            lanes = pl.ds(t * LANES, LANES)
            turned = z[group, t * LANES : (t + 1) * LANES, :].T
            for part in range(5 - group):
                d = 5 * group + part
                for s in range(3):
                    sets[s, d, :, lanes] = turned[24 * part + 8 * s : 24 * part + 8 * s + 8]
                base = 24 * part
                to_high[2 * d : 2 * d + 1, lanes] = turned[base : base + 1]
                to_high[2 * d + 1 : 2 * d + 2, lanes] = turned[base + 8 : base + 9]
                to_low[2 * d : 2 * d + 1, lanes] = turned[base + 15 : base + 16]
                to_low[2 * d + 1 : 2 * d + 2, lanes] = turned[base + 23 : base + 24]


def pack_kernel(coarse, sets, to_high, to_low, buf, z, sems):
    width = coarse.shape[1]
    copies = [pltpu.make_async_copy(coarse.at[d], buf.at[d], sems.at[d]) for d in range(9)]
    for copy in copies:
        copy.start()
    rows = 512
    for d in range(9):
        copies[d].wait()

        def chunk(k, carry, d=d):
            start = pl.multiple_of(k * rows, rows)
            place_columns(z, d, start, rows, buf[d, pl.ds(start, rows), :])
            return carry

        lax.fori_loop(0, width // rows, chunk, 0)
    turn_columns(z, sets, to_high, to_low)


def neighbours(count_x):
    index = lax.axis_index("gx")
    return lax.rem(index + count_x - 1, count_x), lax.rem(index + 1, count_x)


def corner_kernel(count_x, asked, sets, to_high, to_low, ext, z):
    before, after = neighbours(count_x)
    ext[...] = jnp.full(ext.shape, 0.1, F32)
    z[...] = jnp.full(z.shape, 0.1, F32)
    for d in range(9):
        ext[0, d, 0:2, :] = asked[after, 2 * d : 2 * d + 2, :]
        ext[1, d, 6:8, :] = asked[before, 2 * d : 2 * d + 2, :]
    for d in range(9):
        place_columns(z, d, 0, 8, ext[0, d])
        place_columns(z, d, LANES - 8, 8, ext[1, d])
    turn_columns(z, sets, to_high, to_low)


def turned(part, j):
    return pltpu.roll(part, WINDOW * j, 1) if j else part


def windows(parts, off):
    lane = lane_of((8, LANES))
    got = []
    for j, (before, value, after) in enumerate(parts):
        if off == 0:
            value = jnp.where(lane == (WINDOW * j - 1) % LANES, before, value)
        if off == LANES - COARSE_EDGE:
            value = jnp.where(lane == WINDOW * j, after, value)
        got.append(value)
    place = (lane - (off - 1)) & (LANES - 1)
    return jnp.where(place < WINDOW, got[0], jnp.where(place < 2 * WINDOW, got[1], got[2]))


def ghost_kernel(
    count_x,
    count_y,
    coarse,
    asked,
    sets_main,
    low_main,
    high_main,
    sets_ext,
    low_ext,
    high_ext,
    message,
    inject_hbm,
    ids,
    numbers,
    first,
    last,
    turn,
    mt,
    old_t,
    post_t,
    new_t,
    g_t,
    pack_t,
    raw_r,
    post_r,
    new_r,
    g_r,
    far,
    pack_r,
    inject,
    sems,
):
    blocks_x = coarse.shape[1]
    width = blocks_x * COARSE_EDGE
    wide = width + LANES
    tiles = wide // LANES
    width_y = LANES
    blocks_y = width_y // COARSE_EDGE
    total_y = width_y * count_y
    base_y = lax.axis_index("gy") * width_y
    copy_first = pltpu.make_async_copy(coarse.at[:, :, pl.ds(0, 8), :], first, sems.at[0])
    copy_last = pltpu.make_async_copy(
        coarse.at[:, :, pl.ds(COARSE_EDGE - 8, 8), :], last, sems.at[1]
    )
    copy_first.start()
    copy_last.start()
    copy_ids = pltpu.make_async_copy(asked.at[:, pl.ds(16, 8), :], numbers, sems.at[2])
    copy_ids.start()
    index_before, index_after = neighbours(count_x)

    turn[...] = jnp.full(turn.shape, 0.1, F32)
    for d in range(9):
        at = (4 * d - 2) % LANES
        turn[4 * d : 4 * d + 2, 0:width] = high_main[2 * d : 2 * d + 2, :]
        turn[4 * d : 4 * d + 2, width:] = high_ext[2 * d : 2 * d + 2, :]
        turn[at : at + 2, 0:width] = low_main[2 * d : 2 * d + 2, :]
        turn[at : at + 2, width:] = low_ext[2 * d : 2 * d + 2, :]
    for t in range(tiles):
        mt[t * LANES : (t + 1) * LANES, :] = turn[:, t * LANES : (t + 1) * LANES].T
    tile = (8, LANES)
    row8 = row_of(tile)

    def collide_tile(sets, from_low, from_high, at, lanes):
        for s in range(3):
            p = []
            for d in range(9):
                value = sets[s, d, :, at]
                if s < 2:
                    value = jnp.where(row8 == 0, from_low[2 * d + s : 2 * d + s + 1, at], value)
                if s > 0:
                    value = jnp.where(row8 == 7, from_high[2 * d + s - 1 : 2 * d + s, at], value)
                if s == 1:
                    old_t[d, :, lanes] = value
                p.append(value)
            out = relax(p, COARSE)
            for d in range(9):
                post_t[s, d, :, lanes] = out[d]

    def collide_t(t, carry):
        lanes = pl.ds(pl.multiple_of(t * LANES, LANES), LANES)
        collide_tile(sets_main, low_main, high_main, lanes, lanes)
        return carry

    lax.fori_loop(0, tiles - 1, collide_t, 0, unroll=2)
    collide_tile(sets_ext, low_ext, high_ext, pl.ds(0, LANES), pl.ds(width, LANES))
    turn[...] = jnp.zeros(turn.shape, F32)
    row_t = row_of((8, wide))
    coord_t = base_y + 32 * (row_t & 3) + jnp.where(row_t < 4, -1, 32)
    for d in range(9):
        source = post_t[{1: 0, 0: 1, -1: 2}[along_y[d]], d]
        if along_x[d]:
            source = pltpu.roll(source, along_x[d] % wide, 1)
        back = coord_t - along_y[d]
        beyond = (back < 0) | (back >= total_y)
        new_t[d] = jnp.where(beyond, post_t[1, opposite[d]], source)
    for j in range(3):
        for side, (d, row) in enumerate(((LEFT[j], 0), (RIGHT[j], 7))):
            source = post_t[1, d]
            if along_x[d]:
                source = pltpu.roll(source, along_x[d] % wide, 1)
            turn[3 * side + j : 3 * side + j + 1, :] = source[row : row + 1, :]
    for t in range(width // LANES):
        inject[t * LANES : (t + 1) * LANES, :] = turn[:, t * LANES : (t + 1) * LANES].T
    copy_inject = pltpu.make_async_copy(inject, inject_hbm, sems.at[3])
    copy_inject.start()

    def ghosts_t(t, carry):
        lanes = pl.ds(pl.multiple_of(t * LANES, LANES), LANES)
        old = [old_t[d, :, lanes] for d in range(9)]
        mean = [0.5 * (old[d] + new_t[d, :, lanes]) for d in range(9)]
        for sub, p in enumerate((old, mean)):
            out = relax(p, GHOST, LEFT + RIGHT)
            for j in range(3):
                g_t[sub, j, :, lanes] = jnp.where(row8 < 4, out[LEFT[j]], out[RIGHT[j]])
        return carry

    lax.fori_loop(0, tiles, ghosts_t, 0, unroll=3)
    for sub in range(2):
        moved = [
            [turned(g_t[sub, j, :, LANES * k : LANES * (k + 1)], j) for k in range(tiles)]
            for j in range(3)
        ]
        for bx in range(blocks_x):
            t, off = divmod(COARSE_EDGE * bx, LANES)
            parts = [(m[t - 1], m[t], m[t + 1]) for m in moved]
            pack_t[sub, bx] = windows(parts, off)

    plane = (blocks_x, LANES)
    rows_b = row_of(plane)

    def lower(value, row):
        return jnp.where(rows_b == 0, row, pltpu.roll(value, 1, 0))

    def upper(value, row):
        return jnp.where(rows_b == blocks_x - 1, row, pltpu.roll(value, blocks_x - 1, 0))

    def every(ref, start, step):
        return ref[pl.ds(start, blocks_x, stride=step), :]

    side_rows = [every(mt, c, COARSE_EDGE) for c in (0, 1, COARSE_EDGE - 2, COARSE_EDGE - 1)]
    m0, m1, m30, m31 = side_rows
    extra = (
        lower(m30, mt[wide - 2 : wide - 1, :]),
        lower(m31, mt[wide - 1 : wide, :]),
        m0,
        m31,
        upper(m0, mt[width : width + 1, :]),
        upper(m1, mt[width + 1 : width + 2, :]),
    )
    copy_first.wait()
    copy_last.wait()
    first2 = first.reshape(9 * blocks_x * 8, LANES)
    last2 = last.reshape(9 * blocks_x * 8, LANES)
    for k in range(6):
        far[k] = extra[k]

    def raw_rows(d, carry):
        at = d * (blocks_x * 8)
        a0, a1 = every(first2, at, 8), every(first2, at + 1, 8)
        b30, b31 = every(last2, at + 6, 8), every(last2, at + 7, 8)
        main = (
            lower(b30, asked[index_before, pl.ds(2 * d, 1), :]),
            lower(b31, asked[index_before, pl.ds(2 * d + 1, 1), :]),
            a0,
            b31,
            upper(a0, asked[index_after, pl.ds(2 * d, 1), :]),
            upper(a1, asked[index_after, pl.ds(2 * d + 1, 1), :]),
        )
        for k in range(6):
            raw_r[k, d, :, 0:LANES] = main[k]
            raw_r[k, d, :, LANES:] = pltpu.roll(far[k], lax.rem(LANES - 4 * d, LANES), 1)
        return carry

    lax.fori_loop(0, 9, raw_rows, 0, unroll=3)

    def collide_r(k, carry):
        rows = pl.ds(pl.multiple_of(k * 8, 8), 8)
        for s in range(6):
            for half in range(2):
                lanes = pl.ds(half * LANES, LANES)
                out = relax([raw_r[s, d, rows, lanes] for d in range(9)], COARSE)
                for d in range(9):
                    post_r[s, d, rows, lanes] = out[d]
        return carry

    lax.fori_loop(0, blocks_x // 8, collide_r, 0)
    double = (8, 2 * LANES)
    lane_r = lane_of(double)
    coord_r = base_y + jnp.where(lane_r < LANES + 2, lane_r, lane_r - 2 * LANES)

    def ghosts_r(k, carry):
        rows = pl.ds(pl.multiple_of(k * 8, 8), 8)
        for side in range(2):
            for d in range(9):
                source = post_r[3 * side + {1: 0, 0: 1, -1: 2}[along_x[d]], d, rows, :]
                if along_y[d]:
                    source = pltpu.roll(source, along_y[d] % (2 * LANES), 1)
                back = coord_r - along_y[d]
                beyond = (back < 0) | (back >= total_y)
                new_r[d] = jnp.where(beyond, post_r[3 * side + 1, opposite[d], rows, :], source)
            which = (UP, DOWN)[side]
            for half in range(2):
                lanes = pl.ds(half * LANES, LANES)
                old = [raw_r[3 * side + 1, d, rows, lanes] for d in range(9)]
                mean = [0.5 * (old[d] + new_r[d, :, lanes]) for d in range(9)]
                for sub, p in enumerate((old, mean)):
                    out = relax(p, GHOST, which)
                    for j in range(3):
                        g_r[side, j, sub, rows, lanes] = out[which[j]]
        return carry

    lax.fori_loop(0, blocks_x // 8, ghosts_r, 0)

    def windows_r(k, carry):
        rows = pl.ds(pl.multiple_of(k * 8, 8), 8)
        for side in range(2):
            for sub in range(2):
                parts = []
                for j in range(3):
                    one = turned(g_r[side, j, sub, rows, 0:LANES], j)
                    two = turned(g_r[side, j, sub, rows, LANES:], j)
                    parts.append((two, one, two))
                for by in range(blocks_y):
                    pack_r[side, sub, by, rows, :] = windows(parts, COARSE_EDGE * by)
        return carry

    lax.fori_loop(0, blocks_x // 8, windows_r, 0)

    copy_ids.wait()
    for q in range(message.shape[0]):
        ids[q] = numbers[q // CAP, 2, q % CAP].astype(jnp.int32)

    def pick(q, carry):
        block = jnp.maximum(ids[q], 0)
        bx = lax.div(block, blocks_y)
        by = block - bx * blocks_y
        for sub in range(2):
            for side in range(2):
                row = 4 * sub + side
                message[q, row : row + 1, :] = pack_r[side, sub, by, pl.ds(bx, 1), :]
                row = 4 * sub + 2 + side
                message[q, row : row + 1, :] = pack_t[sub, bx, pl.ds(4 * side + by, 1), :]
        return carry

    lax.fori_loop(0, message.shape[0], pick, 0, unroll=4)
    copy_inject.wait()


def start_kernel(slot, fine, post, sem):
    places = post.shape[1]
    copies = []
    for q in range(places):
        source = fine.at[:, pl.ds(jnp.maximum(slot[q], 0), 1), :]
        copy = pltpu.make_async_copy(source, post.at[:, pl.ds(q, 1), :], sem.at[q])
        copy.start()
        copies.append(copy)
    for copy in copies:
        copy.wait()

    def body(k, carry):
        lanes = pl.ds(pl.multiple_of(k * LANES, LANES), LANES)
        for h in range(places // 8):
            rows = pl.ds(8 * h, 8)
            out = relax([post[d, rows, lanes] for d in range(9)], FINE)
            for d in range(9):
                post[d, rows, lanes] = out[d]
        return carry

    lax.fori_loop(0, post.shape[2] // LANES, body, 0, unroll=2)


def fine_kernel(
    slot, post, ghosts, fine, back_hbm, result, back, post_two, line, mean, swapped, sem, back_sem
):
    places = post.shape[1]
    tiles = post.shape[2] // LANES
    tile = (8, LANES)
    lane, row = lane_of(tile), row_of(tile)
    low_half = lane < 64
    at_low = (lane & 63) == 0
    at_high = (lane & 63) == 63
    ghosts2 = ghosts.reshape(places * 8, LANES)
    over = [WINDOW * j + 1 + (((lane & 63) - c) >> 1) for j, c in enumerate(ORDER)]
    even = (lane & 1) == 0
    turn_back = jnp.where(even, lane, (lane - 63) & (LANES - 1))
    cell = (turn_back & 63) + (turn_back >> 6)
    along = [(WINDOW * j + 1 + ((cell - c) >> 1)) & (LANES - 1) for j, c in enumerate(ORDER)]

    def copy(q):
        target = fine.at[:, pl.ds(jnp.maximum(slot[q], 0), 1), :]
        return pltpu.make_async_copy(result.at[:, pl.ds(q, 1), :], target, sem.at[q])

    def send(h):
        part = pl.ds(8 * h, 8)
        return pltpu.make_async_copy(back.at[part], back_hbm.at[part], back_sem.at[h])

    def half(h, carry):
        rows = pl.ds(pl.multiple_of(8 * h, 8), 8)
        wall = jnp.zeros(tile, jnp.int32)
        off_y, off_x = wall, wall
        for r in range(8):
            here = row == r
            wall = jnp.where(here, slot[places + 8 * h + r], wall)
            off_y = jnp.where(here, slot[2 * places + 8 * h + r], off_y)
            off_x = jnp.where(here, slot[3 * places + 8 * h + r], off_x)
        over_own = [(index + off_y - 1) & (LANES - 1) for index in over]
        along_own = [(index + off_x - 1) & (LANES - 1) for index in along]
        quarter = ((lane >> 5) - (off_y >> 5)) & 3
        squeeze = 64 * (quarter & 1) + 2 * (lane & 31) + (quarter >> 1)
        wall_low = at_low & ((wall & 1) != 0)
        wall_high = at_high & ((wall & 2) != 0)

        def substep(sub, source, emit):
            border = [
                ghosts2[pl.ds(h * 64 + 4 * sub + side, 8, stride=8), :] for side in range(4)
            ]
            up = [take_lanes(border[0], over_own[j]) for j in range(3)]
            down = [take_lanes(border[1], over_own[j]) for j in range(3)]
            beside = [
                jnp.where(
                    even, take_lanes(border[2], along_own[j]), take_lanes(border[3], along_own[j])
                )
                for j in range(3)
            ]

            def load(d, k):
                return source[d, rows, k * LANES : (k + 1) * LANES]

            def crossed(d, k):
                if k < 0:
                    return up[UP.index(d)]
                if k == tiles:
                    return down[DOWN.index(d)]
                return pltpu.roll(load(d, k), (64 + along_y[d]) % LANES, 1)

            before = {d: crossed(d, -1) for d in UP}
            now = {d: crossed(d, 0) for d in DOWN}
            for k in range(tiles):
                ghosts_k = [
                    pltpu.roll(value, (-2 * k) % LANES, 1) if k else value for value in beside
                ]
                out = []
                for d in range(9):
                    if along_x[d] > 0:
                        turned = crossed(d, k)
                        value = jnp.where(low_half, before[d], turned)
                        before[d] = turned
                    elif along_x[d] < 0:
                        turned = crossed(d, k + 1)
                        value = jnp.where(low_half, now[d], turned)
                        now[d] = turned
                    else:
                        value = load(d, k)
                        if along_y[d]:
                            value = pltpu.roll(value, along_y[d] % LANES, 1)
                    if along_y[d] > 0:
                        value = jnp.where(at_low, ghosts_k[LEFT.index(d)], value)
                        value = jnp.where(wall_low, load(opposite[d], k), value)
                    elif along_y[d] < 0:
                        value = jnp.where(at_high, ghosts_k[RIGHT.index(d)], value)
                        value = jnp.where(wall_high, load(opposite[d], k), value)
                    out.append(value)
                emit(k, out)

        def emit_first(k, p):
            out = relax(p, FINE)
            for d in range(9):
                post_two[d, :, k * LANES : (k + 1) * LANES] = out[d]

        def emit_second(k, p):
            for d in range(9):
                result[d, rows, k * LANES : (k + 1) * LANES] = p[d]

        post_rows = post
        substep(0, post_rows, emit_first)
        substep(1, _Rows(post_two), emit_second)
        for r in range(8):

            @pl.when(slot[8 * h + r] >= 0)
            def _(r=r):
                copy(8 * h + r).start()

        def tile_of(ref, d, k):
            return ref[d, rows, pl.ds(pl.multiple_of(k * LANES, LANES), LANES)]

        def pair_up(step, carry):
            for u in range(4):
                i = 4 * step + u
                for d in range(9):
                    pairs = []
                    for m in range(2):
                        one = tile_of(result, d, i + 16 * m)
                        two = tile_of(result, d, i + 16 * m + 8)
                        other = pltpu.roll(jnp.where(low_half, two, one), 64, 1)
                        pairs.append(jnp.where(low_half, one, two) + other)
                    mean[d, i] = jnp.where(even, pairs[0], pairs[1])
                    swapped[d, i] = jnp.where(even, pairs[1], pairs[0])
            return carry

        def merge(step, carry):
            for u in range(4):
                i = 4 * step + u
                total = []
                for d in range(9):
                    moved = swapped[d, i]
                    moved = jnp.where(even, pltpu.roll(moved, 127, 1), pltpu.roll(moved, 1, 1))
                    total.append(0.25 * (mean[d, i] + moved))
                out = relax(total, COALESCE)
                for d in range(9):
                    mean[d, i] = out[d]
            return carry

        def compress(step, carry):
            for u in range(4):
                i = 4 * step + u
                for d in range(9):
                    at = pl.ds(pl.multiple_of(i * 8, 8), 8)
                    line[d, at, :] = take_lanes(mean[d, i], squeeze)
            return carry

        lax.fori_loop(0, 2, pair_up, 0)
        lax.fori_loop(0, 2, merge, 0)
        lax.fori_loop(0, 2, compress, 0)
        for d in range(9):
            flat = line.at[d]
            for q in range(8):
                back[8 * h + q, d * 8 : d * 8 + 8, :] = flat[pl.ds(q, 8, stride=8), :]
        send(h).start()
        return carry

    lax.fori_loop(0, places // 8, half, 0)
    for h in range(places // 8):
        send(h).wait()
    for q in range(places):

        @pl.when(slot[q] >= 0)
        def _(q=q):
            copy(q).wait()


class _Rows:
    def __init__(self, ref):
        self.ref = ref

    def __getitem__(self, key):
        d, _, lanes = key
        return self.ref[d, :, lanes]


def coarse_kernel(
    count_x, count_y, coarse, asked, inject_hbm, after, ids, base, strips, home, inject, new, post, load, save, cut
):
    width = coarse.shape[1]
    places = ids.shape[0]
    blocks_y = coarse.shape[2] // COARSE_EDGE
    tile = (8, LANES)
    lane = lane_of(tile)
    parts = 4
    size = width // parts
    copies = [
        pltpu.make_async_copy(
            coarse.at[:, pl.ds(k * size, size), :],
            post.at[:, pl.ds(8 + k * size, size), :],
            load.at[k],
        )
        for k in range(parts)
    ]
    for copy in copies:
        copy.start()
    copy_inject = pltpu.make_async_copy(inject_hbm, inject, load.at[parts])
    copy_inject.start()
    before, following = neighbours(count_x)
    out = relax([asked[before, 2 * d + 1 : 2 * d + 2, :] for d in range(9)], COARSE)
    for d in range(9):
        post[d, 7:8, :] = out[d]
    out = relax([asked[following, 2 * d : 2 * d + 1, :] for d in range(9)], COARSE)
    for d in range(9):
        post[d, width + 8 : width + 9, :] = out[d]

    def collide(k, carry):
        rows = pl.ds(pl.multiple_of(8 + 8 * k, 8), 8)
        out = relax([post[d, rows, :] for d in range(9)], COARSE)
        for d in range(9):
            post[d, rows, :] = out[d]
        return carry

    index_y = lax.axis_index("gy")
    wall_low = (lane == 0) & (index_y == 0)
    wall_high = (lane == LANES - 1) & (index_y == count_y - 1)

    def stream(k, carry):
        start = pl.multiple_of(8 * k, 8)
        edge = inject[pl.ds(start, 8), :]
        for d in range(9):
            value = post[d, pl.ds(start + (8 - along_x[d]), 8), :]
            if along_y[d]:
                value = pltpu.roll(value, along_y[d] % LANES, 1)
                same = post[opposite[d], pl.ds(start + 8, 8), :]
                if along_y[d] > 0:
                    j = LEFT.index(d)
                    value = jnp.where(lane == 0, pltpu.roll(edge, (-j) % LANES, 1), value)
                    value = jnp.where(wall_low, same, value)
                else:
                    j = RIGHT.index(d)
                    moved = pltpu.roll(edge, LANES - 4 - j, 1)
                    value = jnp.where(lane == LANES - 1, moved, value)
                    value = jnp.where(wall_high, same, value)
            new[d, pl.ds(start, 8), :] = value
        return carry

    copy_inject.wait()
    copies[0].wait()
    lax.fori_loop(0, size // 8, collide, 0, unroll=4)
    stores = []
    for k in range(parts):
        if k + 1 < parts:
            copies[k + 1].wait()
            lax.fori_loop((k + 1) * size // 8, (k + 2) * size // 8, collide, 0, unroll=4)
        lax.fori_loop(k * size // 8, (k + 1) * size // 8, stream, 0, unroll=4)
        rows = pl.ds(k * size, size)
        store = pltpu.make_async_copy(new.at[:, rows, :], base.at[:, rows, :], save.at[k])
        store.start()
        stores.append(store)

    def column(q):
        return lax.div(jnp.maximum(ids[q], 0), blocks_y)

    def strip(q):
        rows = pl.ds(pl.multiple_of(COARSE_EDGE * column(q), COARSE_EDGE), COARSE_EDGE)
        return pltpu.make_async_copy(
            new.at[:, rows, :], strips.at[:, pl.ds(COARSE_EDGE * q, COARSE_EDGE), :], cut.at[q]
        )

    for q in range(places):

        @pl.when(ids[q] >= 0)
        def _(q=q):
            strip(q).start()

    for q in range(places):
        first, last = jnp.int32(q), jnp.int32(1)
        for other in reversed(range(places)):
            if other != q:
                same = (ids[q] >= 0) & (ids[other] >= 0) & (column(q) == column(other))
                if other < q:
                    first = jnp.where(same, other, first)
                else:
                    last = jnp.where(same, 0, last)
        home[q] = first
        home[places + q] = last
    for store in stores:
        store.wait()
    for q in range(places):

        @pl.when(ids[q] >= 0)
        def _(q=q):
            strip(q).wait()


def patch_kernel(blocks_y, ids, home, base, strips_in, back, strips, out, save):
    lane = lane_of((8, LANES))
    places = ids.shape[0]

    def store(q):
        bx = lax.div(jnp.maximum(ids[q], 0), blocks_y)
        rows = pl.ds(pl.multiple_of(COARSE_EDGE * bx, COARSE_EDGE), COARSE_EDGE)
        own = pl.ds(pl.multiple_of(COARSE_EDGE * home[q], COARSE_EDGE), COARSE_EDGE)
        return pltpu.make_async_copy(strips.at[:, own, :], out.at[:, rows, :], save.at[q])

    def patch(q, carry):
        @pl.when(ids[q] >= 0)
        def _():
            by = lax.rem(ids[q], blocks_y)
            inside = (lane >> 5) == by
            start = pl.multiple_of(COARSE_EDGE * home[q], COARSE_EDGE)
            for group in (range(5), range(5, 9)):
                merged = []
                for d in group:
                    value = back[q, d * 8 : d * 8 + 8, :]
                    for j in range(4):
                        moved = pltpu.roll(value, LANES - 32 * j, 1) if j else value
                        merged.append((d, pl.ds(start + 8 * j, 8), moved))
                merged = [
                    (d, rows, jnp.where(inside, moved, strips[d, rows, :]))
                    for d, rows, moved in merged
                ]
                for d, rows, value in merged:
                    strips[d, rows, :] = value

        @pl.when((ids[q] >= 0) & (home[places + q] == 1))
        def _():
            store(q).start()

        return carry

    lax.fori_loop(0, places, patch, 0)
    for q in range(places):

        @pl.when((ids[q] >= 0) & (home[places + q] == 1))
        def _(q=q):
            store(q).wait()


def in_hbm(value):
    return pltpu.with_memory_space_constraint(value, pltpu.HBM)


def in_smem(value):
    return pltpu.with_memory_space_constraint(value, pltpu.SMEM)


def in_vmem(value):
    return pltpu.with_memory_space_constraint(value, pltpu.VMEM)


def local(coarse_pop, fine_pop, fine_block):
    width_x, width_y = coarse_pop.shape[1:]
    blocks_x = width_x // COARSE_EDGE
    blocks_y = width_y // COARSE_EDGE
    count_x = lax.axis_size("gx")
    count_y = lax.axis_size("gy")
    columns = blocks_y * count_y
    places = count_x * CAP
    slots = fine_block.shape[0]
    cells = FINE_EDGE * FINE_EDGE
    wide = width_x + LANES
    smem = pl.BlockSpec(memory_space=pltpu.SMEM)
    vmem = pl.BlockSpec(memory_space=pltpu.VMEM)
    hbm = pl.BlockSpec(memory_space=pltpu.HBM)
    sds = jax.ShapeDtypeStruct

    def held(*shape):
        return pltpu.VMEM(shape, F32)

    def table(size):
        return pltpu.SMEM((size,), jnp.int32)

    ask, slot = pl.pallas_call(
        functools.partial(ask_kernel, columns, blocks_x, blocks_y, count_x),
        out_shape=(held(count_x, 24, LANES), table(4 * places)),
        in_specs=[hbm, hbm],
        out_specs=(vmem, smem),
        scratch_shapes=[
            pltpu.SMEM((slots,), jnp.int32),
            pltpu.SMEM((places,), jnp.int32),
            pltpu.SMEM((count_x,), jnp.int32),
            held(2, 9, 8, LANES),
            held(2, 24, LANES),
            pltpu.SemaphoreType.DMA((3,)),
        ],
        name="ask",
        compiler_params=GRANT,
    )(in_hbm(fine_block), in_hbm(coarse_pop))
    asked = in_vmem(lax.all_to_all(ask, "gx", split_axis=0, concat_axis=0, tiled=True))
    forward_y = [(i, (i + 1) % count_y) for i in range(count_y)]
    backward_y = [(target, source) for source, target in forward_y]

    def columns_round(packed):
        sets, to_high, to_low = packed
        from_low = lax.ppermute(to_high, "gy", forward_y)
        from_high = lax.ppermute(to_low, "gy", backward_y)
        return [in_vmem(value) for value in (sets, from_low, from_high)]

    main = columns_round(
        pl.pallas_call(
            pack_kernel,
            out_shape=(held(3, 9, 8, width_x), held(24, width_x), held(24, width_x)),
            in_specs=[hbm],
            out_specs=(vmem, vmem, vmem),
            scratch_shapes=[
                held(9, width_x, LANES),
                held(2, width_x, LANES),
                pltpu.SemaphoreType.DMA((9,)),
            ],
            name="pack",
        compiler_params=GRANT,
        )(in_hbm(coarse_pop))
    )
    corner = columns_round(
        pl.pallas_call(
            functools.partial(corner_kernel, count_x),
            out_shape=(held(3, 9, 8, LANES), held(24, LANES), held(24, LANES)),
            in_specs=[vmem],
            out_specs=(vmem, vmem, vmem),
            scratch_shapes=[held(2, 9, 8, LANES), held(2, LANES, LANES)],
            name="corner",
        compiler_params=GRANT,
        )(asked)
    )
    fine_turned = jnp.transpose(fine_pop, (1, 0, 2))
    post = pl.pallas_call(
        start_kernel,
        out_shape=held(9, places, cells),
        in_specs=[smem, hbm],
        out_specs=vmem,
        scratch_shapes=[pltpu.SemaphoreType.DMA((places,))],
        name="start",
        compiler_params=GRANT,
    )(in_smem(slot), in_hbm(fine_turned))
    message, inject, wanted = pl.pallas_call(
        functools.partial(ghost_kernel, count_x, count_y),
        out_shape=(
            held(places, 8, LANES),
            pltpu.HBM((width_x, LANES), F32),
            table(places),
        ),
        in_specs=[hbm] + [vmem] * 7,
        out_specs=(vmem, hbm, smem),
        scratch_shapes=[
            pltpu.SMEM((count_x, 8, LANES), F32),
            held(9, blocks_x, 8, LANES),
            held(9, blocks_x, 8, LANES),
            held(LANES, wide),
            held(wide, LANES),
            held(9, 8, wide),
            held(3, 9, 8, wide),
            held(9, 8, wide),
            held(2, 3, 8, wide),
            held(2, blocks_x, 8, LANES),
            held(6, 9, blocks_x, 2 * LANES),
            held(6, 9, blocks_x, 2 * LANES),
            held(9, 8, 2 * LANES),
            held(2, 3, 2, blocks_x, 2 * LANES),
            held(6, blocks_x, LANES),
            held(2, 2, blocks_y, blocks_x, LANES),
            held(width_x, LANES),
            pltpu.SemaphoreType.DMA((4,)),
        ],
        name="ghost",
        compiler_params=GRANT,
    )(in_hbm(coarse_pop.reshape(9, blocks_x, COARSE_EDGE, width_y)), asked, *main, *corner)
    ghosts = in_vmem(lax.all_to_all(message, "gx", split_axis=0, concat_axis=0, tiled=True))
    fine_out, back = pl.pallas_call(
        fine_kernel,
        out_shape=(pltpu.HBM((9, slots, cells), F32), pltpu.HBM((places, 72, LANES), F32)),
        in_specs=[smem, vmem, vmem],
        out_specs=(hbm, hbm),
        scratch_shapes=[
            held(9, places, cells),
            held(places, 72, LANES),
            held(9, 8, cells),
            held(9, 64, LANES),
            held(9, 8, 8, LANES),
            held(9, 8, 8, LANES),
            pltpu.SemaphoreType.DMA((places,)),
            pltpu.SemaphoreType.DMA((places // 8,)),
        ],
        name="fine",
        compiler_params=GRANT,
    )(in_smem(slot), in_vmem(post), ghosts)
    returned = in_vmem(lax.all_to_all(back, "gx", split_axis=0, concat_axis=0, tiled=True))
    base, strips, home = pl.pallas_call(
        functools.partial(coarse_kernel, count_x, count_y),
        out_shape=(
            pltpu.HBM((9, width_x, width_y), F32),
            held(9, COARSE_EDGE * places, width_y),
            table(2 * places),
        ),
        in_specs=[hbm, vmem, hbm, hbm, smem],
        out_specs=(hbm, vmem, smem),
        scratch_shapes=[
            held(width_x, LANES),
            held(9, width_x, LANES),
            held(9, width_x + 16, LANES),
            pltpu.SemaphoreType.DMA((5,)),
            pltpu.SemaphoreType.DMA((4,)),
            pltpu.SemaphoreType.DMA((places,)),
        ],
        name="coarse",
        compiler_params=GRANT,
    )(in_hbm(coarse_pop), asked, in_hbm(inject), in_hbm(back), in_smem(wanted))
    _, coarse_out = pl.pallas_call(
        functools.partial(patch_kernel, blocks_y),
        out_shape=(
            held(9, COARSE_EDGE * places, width_y),
            pltpu.HBM((9, width_x, width_y), F32),
        ),
        in_specs=[smem, smem, hbm, vmem, vmem],
        out_specs=(vmem, hbm),
        scratch_shapes=[pltpu.SemaphoreType.DMA((places,))],
        input_output_aliases={2: 1, 3: 0},
        name="patch",
        compiler_params=GRANT,
    )(in_smem(wanted), in_smem(home), in_hbm(base), in_vmem(strips), returned)
    return (coarse_out, jnp.transpose(fine_out, (1, 0, 2)))


def solution(mesh):
    return jax.shard_map(
        local,
        mesh=mesh,
        in_specs=(P(None, "gx", "gy"), P(("gx", "gy"), None, None), P(("gx", "gy"))),
        out_specs=(P(None, "gx", "gy"), P(("gx", "gy"), None, None)),
        check_vma=False,
    )
```
